32 devices in a mesh: res: 8 (over z, x), edge: 4 (over y, core).
Axes of the slice: x: 2, y: 2, z: 4, core: 2. Of those that a mesh axis runs over, the one named last changes fastest.
Arguments:
- node_in: bfloat16 [1280, 512], P(('res', 'edge')), may hold values from -6 to 6
- edge_in: bfloat16 [1280, 60, 192], P('res', 'edge'), may hold values from -6 to 6
- neighbors: int32 [1280, 60], P('res', 'edge'), may hold values from 0 to 1279, as said below
- chain_ids: int32 [1280], replicated, may hold values from 0 to 9, never falling along the last dimension, each value on 1 to 256 neighbouring positions
- residue_mask: int32 [1280], replicated, may hold values 0 or 1
- w_msg_in: bfloat16 [1216, 512], replicated, may hold values from -0.15625 to 0.15625
- chain_vec: float32 [512], replicated, may hold values from -3 to 3
- w_msg_out: bfloat16 [512, 512], replicated, may hold values from -0.25 to 0.25
- gain_one: float32 [512], replicated, may hold values from 0.25 to 1.75
- w_ffn_in: bfloat16 [512, 2048], replicated, may hold values from -0.25 to 0.25
- w_ffn_out: bfloat16 [2048, 512], replicated, may hold values from -0.125 to 0.125
- gain_two: float32 [512], replicated, may hold values from 0.25 to 1.75
- w_edge_in: bfloat16 [1216, 192], replicated, may hold values from -0.15625 to 0.15625
- w_edge_out: bfloat16 [192, 192], replicated, may hold values from -0.4375 to 0.4375
- gain_three: float32 [192], replicated, may hold values from 0.25 to 1.75
- node_cot: bfloat16 [1280, 512], P(('res', 'edge')), may hold values from -6 to 6
- edge_cot: bfloat16 [1280, 60, 192], P('res', 'edge'), may hold values from -6 to 6
Outputs:
- node_out: bfloat16 [1280, 512], P(('res', 'edge'))
- edge_out: bfloat16 [1280, 60, 192], P('res', 'edge')
- node_grad: float32 [1280, 512], P(('res', 'edge'))
- edge_grad: float32 [1280, 60, 192], P('res', 'edge')
- grad_msg_in: float32 [1216, 512], replicated
- grad_chain_vec: float32 [512], replicated
- grad_msg_out: float32 [512, 512], replicated
- grad_gain_one: float32 [512], replicated
- grad_ffn_in: float32 [512, 2048], replicated
- grad_ffn_out: float32 [2048, 512], replicated
- grad_gain_two: float32 [512], replicated
- grad_edge_in: float32 [1216, 192], replicated
- grad_edge_out: float32 [192, 192], replicated
- grad_gain_three: float32 [192], replicated
The draws below stay inside these ranges and needn't reach their ends.
Inputs may be any that keep to these rules, and one draw needn't show every extreme that they name: `neighbors`: entry 0 of every residue's list of 60 neighbours is the residue itself. Take the edges of one device (the 160 residues of one index of res, one of the 4 equal shares of each list) and the node blocks of 40 rows in order; sources in the blocks of residue groups other than the device's own and the two beside it come to at most 56 from any one node block, and exactly 56 from some block, for every device.
All inputs are finite; a program needn't handle non-finite values.
Results may differ from the reference program's by a relative error of at most 0.023.
Values may be sent and summed in bfloat16 or wider, within the bound.
No kernel may reach another device: no remote copies, remote signals or barrier semaphores. Data moves between devices by JAX's collectives and lax.ppermute only.
A program may use at most 192 MiB of HBM per device.

```python
import math
import jax
import jax.numpy as jnp
import numpy as np
from jax import lax

DN = 512
DE = 192
FF = 2048
K = 60
R_DEV = 160
NODES = 1280
N_RES = 8
N_EDGE = 4
DEVICES = 32


def draw_neighbors(key, part):
    key_local, key_row, key_perm, key_shift = jax.random.split(key, 4)
    share_cols = K // N_EDGE
    far_slots = R_DEV * (share_cols // 2)
    far_owners = (N_RES - 3) * N_EDGE
    block_rows = R_DEV // N_EDGE
    window = min(16, R_DEV)
    row_index = jnp.arange(NODES, dtype=jnp.int32)[:, None]
    column = jnp.arange(K, dtype=jnp.int32)[None, :]
    group = row_index // R_DEV
    within = row_index % R_DEV
    share = column // share_cols
    inner = column % share_cols
    device = group * N_EDGE + share
    slot_index = jnp.minimum(within * (share_cols // 2) + inner // 2, far_slots - 1)
    orders = jax.vmap(lambda dev: jax.random.permutation(jax.random.fold_in(key_perm, dev), far_slots))(jnp.arange(DEVICES, dtype=jnp.int32)).astype(jnp.int32)
    shifts = jax.random.randint(key_shift, (DEVICES,), 0, far_owners, dtype=jnp.int32)
    rank = orders[device, slot_index]
    offset = (rank + shifts[device]) % far_owners
    owner = ((group + 2) * N_EDGE + offset) % DEVICES
    far_row = owner * block_rows + jax.random.randint(key_row, (NODES, K), 0, block_rows, dtype=jnp.int32)
    steps = jax.random.randint(key_local, (NODES, K), -window, window + 1, dtype=jnp.int32)
    nearby = jnp.clip(row_index + steps, 0, NODES - 1)
    chosen = jnp.where(inner % 2 == 1, far_row, nearby)
    return jnp.where(column == 0, row_index, chosen).astype(jnp.int32)


def place_ends(result, stream_key, least, high):
    longest = result.shape.index(max(result.shape))
    spots = []
    for shift in (0, 1):
        where = [jax.random.randint(jax.random.fold_in(stream_key, axis), (), 0, length) for axis, length in enumerate(result.shape)]
        where[longest] = (where[longest] + shift) % result.shape[longest]
        spots.append(tuple(where))
    return result.at[spots[0]].set(least).at[spots[1]].set(high)


def shard_levels(key, shape, cuts, least, top_value):
    loudness, own = 1.0, jax.random.fold_in(key, 6)
    for dim, parts in cuts:
        heights = jnp.exp(jax.random.uniform(jax.random.fold_in(own, dim), (parts,), jnp.float32, least / len(cuts), top_value / len(cuts)))
        loudness = loudness * jnp.repeat(heights, shape[dim] // parts).reshape([-1 if axis == dim else 1 for axis in range(len(shape))])
    return loudness


def split_up(amount, total, bound, slope):
    portions = [(1 << 20) // math.isqrt(grade ** slope) + 1 for grade in range(2, amount + 1)]
    spare, given = total - bound - (amount - 1), [1] * (amount - 1)
    while spare > 0:
        movable = [i for i in range(amount - 1) if given[i] < bound]
        mass, left = sum([portions[i] for i in movable]), spare
        for i in movable:
            addition = min(bound - given[i], max(1, left * portions[i] // mass), spare)
            given[i] = given[i] + addition
            spare = spare - addition
    return np.array([bound] + given)


def ragged(own_key, amount, total, reach, skew):
    if amount == 2:
        one = jax.random.randint(own_key, (), max(1, total - reach), min(reach, total - 1) + 1)
        return jnp.stack([one, total - one])
    lengths = jnp.asarray(split_up(amount, total, reach, skew), jnp.int32)
    twos = (amount - 1) // 2
    giver, taker = lengths[1:1 + 2 * twos:2], lengths[2:2 + 2 * twos:2]
    slack = jnp.minimum(giver - 1, reach - taker)
    shifted = jax.random.randint(jax.random.fold_in(own_key, 1), (twos,), 0, 1 << 20) % (slack + 1)
    lengths = lengths.at[1:1 + 2 * twos:2].set(giver - shifted).at[2:2 + 2 * twos:2].set(taker + shifted)
    return lengths[jax.random.permutation(jax.random.fold_in(own_key, 2), amount)]


def normal_values(rng, shape, scale, most, cuts=(), kind=jnp.bfloat16):
    array = jax.random.normal(rng, shape, jnp.float32) * scale
    if len(cuts) > 0:
        array = shard_levels(rng, shape, cuts, -0.22, 0.18) * array
    return jnp.clip(array, min=-most, max=most).astype(kind)


def setup_inputs(seed: int = 0) -> dict:
    seeds = jax.random.split(jax.random.key(seed), 18)
    return {
        "node_in": normal_values(seeds[0], (NODES, DN), 1.0, 6.0, ((0, 32),)),
        "edge_in": normal_values(seeds[1], (NODES, K, DE), 1.0, 6.0, ((0, 8), (1, 4))),
        "neighbors": draw_neighbors(jax.random.fold_in(seeds[17], 71), 0),
        "chain_ids": jnp.searchsorted(jnp.cumsum(ragged(seeds[3], max(NODES // 128, 2), NODES, min(256, NODES // 2 + NODES // 4), 1)), jnp.arange(NODES), side="right").astype(jnp.int32),
        "residue_mask": place_ends((jax.random.randint(seeds[4], (NODES,), 0, 8) < 7).astype(jnp.int32), jax.random.fold_in(seeds[4], 1), 0, 1),
        "w_msg_in": normal_values(seeds[5], (2 * DN + DE, DN), (2 * DN + DE) ** -0.5, 0.15625),
        "chain_vec": normal_values(seeds[6], (DN,), 0.5, 3.0, (), jnp.float32),
        "w_msg_out": normal_values(seeds[7], (DN, DN), DN ** -0.5, 0.25),
        "gain_one": jnp.clip(1.0 + 0.15 * jax.random.normal(seeds[8], (DN,), jnp.float32), 0.25, 1.75),
        "w_ffn_in": normal_values(seeds[9], (DN, FF), DN ** -0.5, 0.25),
        "w_ffn_out": normal_values(seeds[10], (FF, DN), FF ** -0.5, 0.125),
        "gain_two": jnp.clip(1.0 + 0.15 * jax.random.normal(seeds[11], (DN,), jnp.float32), 0.25, 1.75),
        "w_edge_in": normal_values(seeds[12], (2 * DN + DE, DE), (2 * DN + DE) ** -0.5, 0.15625),
        "w_edge_out": normal_values(seeds[13], (DE, DE), DE ** -0.5, 0.4375),
        "gain_three": jnp.clip(1.0 + 0.15 * jax.random.normal(seeds[14], (DE,), jnp.float32), 0.25, 1.75),
        "node_cot": normal_values(seeds[15], (NODES, DN), 1.0, 6.0, ((0, 32),)),
        "edge_cot": normal_values(seeds[16], (NODES, K, DE), 1.0, 6.0, ((0, 8), (1, 4))),
    }


@jax.custom_vjp
def low(v):
    return lax.optimization_barrier(v.astype(jnp.bfloat16)).astype(jnp.float32)

@jax.custom_vjp
def low_back(v):
    return v

def low_keep(v):
    return (low(v), None)

def low_pass(kept, grad):
    return (grad,)

def back_keep(v):
    return (v, None)

def back_low(kept, grad):
    return (low(grad),)
low.defvjp(low_keep, low_pass)
low_back.defvjp(back_keep, back_low)
EPS = 1e-05

def norm_gain(values, gain_vec):
    centre = values - lax.optimization_barrier(jnp.mean(values, axis=-1, keepdims=True))
    spread = lax.optimization_barrier(jnp.mean(centre * centre, axis=-1, keepdims=True))
    return centre * lax.rsqrt(spread + EPS) * gain_vec

def gelu_exact(values):
    return jax.nn.gelu(values, approximate=False)

def product(left_mat, right_mat):
    return jnp.einsum('...c,cd->...d', left_mat, right_mat, precision=lax.Precision.HIGHEST)

def message_block(pieces, node_f, w_msg_in, chain_vec, w_msg_out):
    own_block, edge_block, nbr_block, cross_block, mask_block = pieces
    source = jnp.take(node_f, nbr_block, axis=0)
    own_rows = jnp.broadcast_to(own_block[:, None, :], source.shape)
    joined = jnp.concatenate([own_rows, source, edge_block], axis=-1)
    pre_act = low_back(product(joined, w_msg_in) + cross_block[..., None] * chain_vec)
    hidden = low(gelu_exact(pre_act))
    message = product(hidden, w_msg_out)
    return low_back(lax.optimization_barrier(jnp.sum(mask_block[..., None] * message, axis=1)))

def edge_block_fn(pieces, updated, w_edge_in, w_edge_out, gain_three):
    own_block, edge_block, nbr_block, mask_block = pieces
    source = jnp.take(updated, nbr_block, axis=0)
    own_rows = jnp.broadcast_to(own_block[:, None, :], source.shape)
    joined = jnp.concatenate([own_rows, source, edge_block], axis=-1)
    pre_act = low_back(product(joined, w_edge_in))
    hidden = low(gelu_exact(pre_act))
    edge_delta = low_back(product(hidden, w_edge_out))
    return norm_gain(edge_block + mask_block[..., None] * edge_delta, gain_three)

def layer(node_f, edge_f, w_msg_in, chain_vec, w_msg_out, gain_one, w_ffn_in, w_ffn_out, gain_two, w_edge_in, w_edge_out, gain_three, neighbors, cross_chain, pair_mask):
    block_rows = R_DEV
    block_count = NODES // block_rows

    def by_blocks(array_in):
        return array_in.reshape((block_count, block_rows) + array_in.shape[1:])
    summed = lax.map(jax.checkpoint(lambda pieces: message_block(pieces, node_f, w_msg_in, chain_vec, w_msg_out)), (by_blocks(node_f), by_blocks(edge_f), by_blocks(neighbors), by_blocks(cross_chain), by_blocks(pair_mask)))
    summed = summed.reshape(NODES, DN)
    first_in = node_f + summed / math.sqrt(K)
    norm_one = norm_gain(first_in, gain_one)
    ffn_pre = low_back(product(low(norm_one), w_ffn_in))
    ffn_hidden = low(gelu_exact(ffn_pre))
    ffn_out = low_back(product(ffn_hidden, w_ffn_out))
    updated = low(norm_gain(norm_one + ffn_out, gain_two))
    edge_new = lax.map(jax.checkpoint(lambda pieces: edge_block_fn(pieces, updated, w_edge_in, w_edge_out, gain_three)), (by_blocks(updated), by_blocks(edge_f), by_blocks(neighbors), by_blocks(pair_mask)))
    return (updated, edge_new.reshape(NODES, K, DE))

def reference(node_in, edge_in, neighbors, chain_ids, residue_mask, w_msg_in, chain_vec, w_msg_out, gain_one, w_ffn_in, w_ffn_out, gain_two, w_edge_in, w_edge_out, gain_three, node_cot, edge_cot):
    mask_float = residue_mask.astype(jnp.float32)
    pair_mask = mask_float[:, None] * jnp.take(mask_float, neighbors, axis=0)
    cross_chain = (chain_ids[:, None] != jnp.take(chain_ids, neighbors, axis=0)).astype(jnp.float32)
    floats = tuple((member.astype(jnp.float32) for member in (node_in, edge_in, w_msg_in, chain_vec, w_msg_out, gain_one, w_ffn_in, w_ffn_out, gain_two, w_edge_in, w_edge_out, gain_three)))

    def forward(*params):
        return layer(*params, neighbors, cross_chain, pair_mask)
    outputs, backward = jax.vjp(forward, *floats)
    gradients = backward((node_cot.astype(jnp.float32), edge_cot.astype(jnp.float32)))
    node_out, edge_new = outputs
    return (node_out.astype(jnp.bfloat16), edge_new.astype(jnp.bfloat16), gradients[0], gradients[1], gradients[2], gradients[3], gradients[4], gradients[5], gradients[6], gradients[7], gradients[8], gradients[9], gradients[10], gradients[11])
```

```python
import functools
import math

import jax
import jax.numpy as jnp
from jax import lax
from jax.experimental import pallas as pl
from jax.experimental.pallas import tpu as pltpu
from jax.sharding import Mesh, PartitionSpec as P

EPS = 1e-05
CHIPS = ("z", "x", "y")
BF = jnp.bfloat16
F32 = jnp.float32
LANES = 256
HALF = 128
CHUNK = 128
RSQRT2 = math.sqrt(0.5)
INV_SQRT_2PI = 1.0 / math.sqrt(2.0 * math.pi)


def mm(a, b):
    return jnp.dot(a, b, preferred_element_type=F32)


def mm_nt(a, b):
    return lax.dot_general(a, b, (((1,), (1,)), ((), ())), preferred_element_type=F32)


def mm_tn(a, b):
    return lax.dot_general(a, b, (((0,), (0,)), ((), ())), preferred_element_type=F32)


def gelu_pair(v):
    cdf = 0.5 * (1.0 + lax.erf(v * RSQRT2))
    pdf = INV_SQRT_2PI * jnp.exp(-0.5 * v * v)
    return v * cdf, cdf + v * pdf


def norm_parts(z):
    centre = z - jnp.mean(z, axis=-1, keepdims=True)
    r = lax.rsqrt(jnp.mean(centre * centre, axis=-1, keepdims=True) + EPS)
    return centre * r, r


def norm_back(n, r, gain, cot):
    b = cot * gain
    dz = r * (b - jnp.mean(b, -1, keepdims=True) - n * jnp.mean(b * n, -1, keepdims=True))
    return dz, jnp.sum(cot * n, axis=0, keepdims=True)


def pad_rows(x, rows):
    return jnp.concatenate([x, jnp.zeros((rows - x.shape[0], x.shape[1]), x.dtype)], axis=0)


def one_hot_rows(tail, cols, total):
    hi = tail[:, cols["hi"] - HALF : cols["hi"] - HALF + 1].astype(F32)
    lo = tail[:, cols["lo"] - HALF : cols["lo"] - HALF + 1].astype(F32)
    index = (hi * 128.0 + lo).astype(jnp.int32)
    lane = lax.broadcasted_iota(jnp.int32, (tail.shape[0], total), 1)
    return jnp.where(lane == index, 1.0, 0.0).astype(BF)


def one_hot_cols(index_row, first, count):
    row = lax.broadcasted_iota(jnp.int32, (count, index_row.shape[1]), 0) + first
    return jnp.where(row == index_row, 1.0, 0.0).astype(BF)


def message_forward(
    cols, norm_scale,
    edge_ref, nodes_ref, own_ref, wmi_ref, chain_ref, wmo_ref, gain1_ref, wfi_any, wfo_any, gain2_ref, wei_ref,
    slope_ref, index_ref, total_ref, first_ref, second_ref, low_ref, fslope_ref, fhidden_ref, out_ref, src_ref, eown_ref,
    table, weights, acc, wfi, wfo, sems,
):
    step = pl.program_id(0)
    width = own_ref.shape[1]
    rows_own = own_ref.shape[0]
    nodes = nodes_ref.shape[0]
    edge_width = cols["width"]
    piece = edge_ref.shape[1]
    copy_in = pltpu.make_async_copy(wfi_any, wfi, sems.at[0])
    copy_out = pltpu.make_async_copy(wfo_any, wfo, sems.at[1])

    @pl.when(step == 0)
    def _():
        copy_in.start()
        copy_out.start()
        block = nodes // 5

        @pl.loop(0, 5)
        def _(i):
            start = pl.multiple_of(i * block, block)
            table[pl.ds(start, block), :] = mm(nodes_ref[pl.ds(start, block), :], wmi_ref[width : 2 * width, :]).astype(BF)

        own_part = mm(own_ref[...], wmi_ref[:width, :])
        vec = chain_ref[...]
        vec_hi = vec.astype(BF).astype(F32)
        vec_rows = jnp.concatenate([vec_hi, vec - vec_hi, jnp.zeros((6, width), F32)], axis=0)
        lower = pad_rows(jnp.concatenate([own_part, vec_rows], axis=0), LANES - edge_width)
        weights[:edge_width, :] = wmi_ref[2 * width :, :]
        weights[edge_width:, :] = lower.astype(BF)
        acc[...] = jnp.zeros_like(acc)

    for c in range(piece // CHUNK):
        a = edge_ref[0, c * CHUNK : (c + 1) * CHUNK, :]
        tail = a[:, HALF:]
        turned = jnp.transpose(tail.astype(F32))
        at = cols["hi"] - HALF
        index_ref[0, :, c * CHUNK : (c + 1) * CHUNK] = (turned[at : at + 1] * 128.0 + turned[at + 1 : at + 2]).astype(jnp.int32)
        pre = mm(a, weights[...]) + mm(one_hot_rows(tail, cols, nodes), table[...])
        hidden, slope = gelu_pair(pre)
        slope_ref[0, c * CHUNK : (c + 1) * CHUNK, :] = slope.astype(BF)
        acc[...] += mm_tn(tail, hidden.astype(BF))

    @pl.when(step == pl.num_programs(0) - 1)
    def _():
        at = cols["own"] - HALF
        total = acc[at : at + rows_own, :].astype(BF)
        total_ref[...] = total
        first_in = own_ref[...].astype(F32) + mm(total, wmo_ref[...]) * (1.0 / norm_scale)
        first_ref[...] = first_in
        norm_one = norm_parts(first_in)[0] * gain1_ref[...]
        low = norm_one.astype(BF)
        low_ref[...] = low
        copy_in.wait()
        hidden, slope = gelu_pair(mm(low, wfi[...]))
        hidden = hidden.astype(BF)
        fslope_ref[...] = slope
        fhidden_ref[...] = hidden
        copy_out.wait()
        second_in = norm_one + mm(hidden, wfo[...])
        second_ref[...] = second_in
        node_out = (norm_parts(second_in)[0] * gain2_ref[...]).astype(BF)
        out_ref[...] = node_out
        eown_ref[...] = mm(node_out, wei_ref[:width, :]).astype(BF)
        src_ref[...] = mm(node_out, wei_ref[width : 2 * width, :]).astype(BF)


def edge_network(
    cols,
    edge_ref, cot_ref, index_ref, table_ref, eown_ref, wei_ref, weo_ref, gain_ref,
    out_ref, dsum_ref, scatter_ref, gin_ref, gout_ref, ggain_ref,
    table, weights, outw, dpre_s, acc,
):
    step = pl.program_id(0)
    edge_width = cols["width"]
    nodes = table_ref.shape[0]
    piece = edge_ref.shape[1]
    width = (wei_ref.shape[0] - edge_width) // 2
    extra = LANES - edge_width

    @pl.when(step == 0)
    def _():
        table[...] = jnp.concatenate([table_ref[...].astype(F32), jnp.zeros((nodes, extra), F32)], axis=1).astype(BF)
        lower = pad_rows(eown_ref[...].astype(F32), extra)
        full = jnp.concatenate([wei_ref[2 * width :, :].astype(F32), lower], axis=0)
        weights[...] = jnp.concatenate([full, jnp.zeros((LANES, extra), F32)], axis=1).astype(BF)
        full = jnp.concatenate([weo_ref[...].astype(F32), jnp.zeros((edge_width, extra), F32)], axis=1)
        outw[...] = pad_rows(full, LANES).astype(BF)
        acc[...] = jnp.zeros_like(acc)
        gin_ref[...] = jnp.zeros_like(gin_ref)
        gout_ref[...] = jnp.zeros_like(gout_ref)
        ggain_ref[...] = jnp.zeros_like(ggain_ref)

    lane = lax.broadcasted_iota(jnp.int32, (CHUNK, LANES), 1)
    real = lane < edge_width
    gain = jnp.concatenate([gain_ref[...], jnp.zeros((1, extra), F32)], axis=1)
    inv = 1.0 / edge_width
    for c in range(piece // CHUNK):
        span = slice(c * CHUNK, (c + 1) * CHUNK)
        a = edge_ref[0, span, :]
        tail = a[:, HALF:]
        mask = tail[:, cols["mask"] - HALF : cols["mask"] - HALF + 1].astype(F32)
        pre = mm(a, weights[...]) + mm(one_hot_rows(tail, cols, nodes), table[...])
        hidden, slope = gelu_pair(pre)
        hidden = (hidden * mask).astype(BF)
        z = jnp.where(real, a.astype(F32), 0.0) + mm(hidden, outw[...])
        centre = jnp.where(real, z - jnp.sum(z, -1, keepdims=True) * inv, 0.0)
        r = lax.rsqrt(jnp.sum(centre * centre, -1, keepdims=True) * inv + EPS)
        n = centre * r
        out_ref[0, span, :] = (n * gain)[:, :edge_width].astype(BF)
        cot = cot_ref[0, span, :].astype(F32)
        cn = cot * n
        ggain_ref[...] += jnp.sum(cn.reshape(CHUNK // 8, 8, LANES), axis=0)
        b = cot * gain
        mean_b = jnp.sum(b, -1, keepdims=True) * inv
        mean_bn = jnp.sum(cn * gain, -1, keepdims=True) * inv
        dz = jnp.where(real, r * (b - mean_b - n * mean_bn), 0.0)
        d_delta = (dz * mask).astype(BF)
        gout_ref[...] += mm_tn(hidden, d_delta)
        d_pre = (slope * mm_nt(d_delta, outw[...])).astype(BF)
        dpre_s[span, :] = d_pre
        gin_ref[...] += mm_tn(a, d_pre)
        dsum_ref[0, span, :] = (dz + mm_nt(d_pre, weights[...]))[:, :edge_width].astype(BF)
    index_row = index_ref[0]
    block = nodes // 5

    @pl.loop(0, 5)
    def _(i):
        start = pl.multiple_of(i * block, block)
        acc[pl.ds(start, block), :] += mm(one_hot_cols(index_row, start, block), dpre_s[...])

    @pl.when(step == pl.num_programs(0) - 1)
    def _():
        scatter_ref[...] = acc[...].astype(BF)[:, :edge_width]


def node_backward(
    cols, norm_scale,
    parts_ref, gin_ref, node_cot_ref, out_ref, first_ref, second_ref, low_ref, fslope_ref, fhidden_ref, total_ref,
    wei_ref, wfi_ref, wfo_ref, wmo_ref, gain1_ref, gain2_ref,
    dffn_ref, d_ref, dfirst_ref, ggain_ref, gmo_ref, gei_ref,
):
    width = out_ref.shape[1]
    rows_own = out_ref.shape[0]
    edge_width = cols["width"]
    from_sources = parts_ref[0].astype(F32)
    for i in range(1, parts_ref.shape[0]):
        from_sources += parts_ref[i].astype(F32)
    from_sources = from_sources.astype(BF)
    from_own = gin_ref[cols["own"] : cols["own"] + rows_own, :edge_width].astype(BF)
    d_updated = (
        node_cot_ref[...].astype(F32)
        + mm_nt(from_own, wei_ref[:width, :])
        + mm_nt(from_sources, wei_ref[width : 2 * width, :])
    )
    node_out = out_ref[...]
    gei_ref[:, :edge_width] = mm_tn(node_out, from_own).astype(BF)
    gei_ref[:, LANES : LANES + edge_width] = mm_tn(node_out, from_sources).astype(BF)
    zeros = jnp.zeros((width, LANES - edge_width), BF)
    gei_ref[:, edge_width:LANES] = zeros
    gei_ref[:, LANES + edge_width :] = zeros
    n, r = norm_parts(second_ref[...])
    d_second, ggain2 = norm_back(n, r, gain2_ref[...], d_updated)
    dffn = d_second.astype(BF)
    dffn_ref[...] = dffn
    d_ffn_pre = (fslope_ref[...] * mm_nt(dffn, wfo_ref[...])).astype(BF)
    d_norm_one = d_second + mm_nt(d_ffn_pre, wfi_ref[...])
    n, r = norm_parts(first_ref[...])
    d_first, ggain1 = norm_back(n, r, gain1_ref[...], d_norm_one)
    dfirst_ref[...] = d_first
    d_summed = (d_first * (1.0 / norm_scale)).astype(BF)
    gmo_ref[...] = mm_tn(total_ref[...], d_summed).astype(BF)
    d_ref[...] = mm_nt(d_summed, wmo_ref[...]).astype(BF)
    ggain_ref[...] = jnp.concatenate([ggain1, ggain2, jnp.zeros((6, width), F32)], axis=0)


def message_backward(
    cols,
    edge_ref, slope_ref, d_ref, index_ref, dsum_ref, wmi_ref, nodes_ref, own_ref, dfirst_ref,
    scatter_ref, eg_ref, pay_ref, ngrad_ref,
    weights, dpre_s, acc, gin,
):
    step = pl.program_id(0)
    edge_width = cols["width"]
    nodes, width = nodes_ref.shape
    rows_own = own_ref.shape[0]
    piece = edge_ref.shape[1]
    at = cols["own"] - HALF

    @pl.when(step == 0)
    def _():
        own = pad_rows(d_ref[...].astype(F32), HALF - at)
        weights[...] = jnp.concatenate([jnp.zeros((at, width), F32), own], axis=0).astype(BF)
        acc[...] = jnp.zeros_like(acc)
        gin[...] = jnp.zeros_like(gin)

    for c in range(piece // CHUNK):
        span = slice(c * CHUNK, (c + 1) * CHUNK)
        a = edge_ref[0, span, :]
        d_pre = (slope_ref[0, span, :].astype(F32) * mm(a[:, HALF:], weights[...])).astype(BF)
        dpre_s[span, :] = d_pre
        gin[...] += mm_tn(a, d_pre)
        back = mm_nt(d_pre, wmi_ref[2 * width :, :])
        eg_ref[0, span, :] = (dsum_ref[0, span, :].astype(F32) + back).astype(BF)
    index_row = index_ref[0]
    block = nodes // 5

    @pl.loop(0, 5)
    def _(i):
        start = pl.multiple_of(i * block, block)
        acc[pl.ds(start, block), :] += mm(one_hot_cols(index_row, start, block), dpre_s[...])

    @pl.when(step == pl.num_programs(0) - 1)
    def _():
        scattered = acc[...].astype(BF)
        scatter_ref[...] = scattered
        from_own = gin[cols["own"] : cols["own"] + rows_own, :].astype(BF)
        ngrad_ref[...] = dfirst_ref[...] + mm_nt(from_own, wmi_ref[:width, :])
        pay_ref[:width, :] = mm_tn(own_ref[...], from_own).astype(BF)
        pay_ref[width : 2 * width, :] = mm_tn(nodes_ref[...], scattered).astype(BF)
        pay_ref[2 * width : 2 * width + edge_width, :] = gin[:edge_width, :].astype(BF)
        chain = gin[cols["cross"] : cols["cross"] + 8, :]
        pay_ref[2 * width + edge_width :, :] = pad_rows(chain[:1, :], pay_ref.shape[0] - 2 * width - edge_width).astype(BF)


def finish_nodes(parts_ref, ngrad_ref, wmi_ref, out_ref):
    width = ngrad_ref.shape[1]
    total = parts_ref[0].astype(F32)
    for i in range(1, parts_ref.shape[0]):
        total += parts_ref[i].astype(F32)
    out_ref[...] = ngrad_ref[...] + mm_nt(total.astype(BF), wmi_ref[width : 2 * width, :])


def ffn_grads(low_ref, dffn_ref, wfi_ref, wfo_ref, gfi_ref, gfo_ref):
    low = low_ref[...]
    dffn = dffn_ref[...]
    hidden, slope = gelu_pair(mm(low, wfi_ref[...]))
    gfo_ref[...] = mm_tn(hidden.astype(BF), dffn)
    d_pre = (slope * mm_nt(dffn, wfo_ref[...])).astype(BF)
    gfi_ref[...] = mm_tn(low, d_pre)


def whole(shape):
    return pl.BlockSpec(shape, lambda *_: (0,) * len(shape))


def per_piece(shape):
    return pl.BlockSpec((1,) + tuple(shape[1:]), lambda i: (i,) + (0,) * (len(shape) - 1))


def params(limit=56):
    return pltpu.CompilerParams(vmem_limit_bytes=limit << 20, dimension_semantics=("arbitrary",))


def sds(shape, dtype):
    return jax.ShapeDtypeStruct(shape, dtype)


def swap(x, axis):
    return lax.ppermute(x, axis, [(0, 1), (1, 0)])


def gather_nodes(x):
    count = lax.axis_size(CHIPS)
    spread = jnp.broadcast_to(x[None], (count,) + x.shape)
    got = lax.all_to_all(spread, CHIPS, 0, 0).reshape(count * x.shape[0], x.shape[1])
    return jnp.concatenate([got, swap(got, "c")], axis=0)


def scatter_nodes(x):
    half = x.shape[0] // 2
    got = swap(x[half:], "c")
    both = (x[:half].astype(F32) + got.astype(F32)).astype(x.dtype)
    return lax.all_to_all(both.reshape(lax.axis_size(CHIPS), -1, x.shape[1]), CHIPS, 0, 0)


def sum_all(x):
    half = x.shape[0] // 2
    core = lax.axis_index("c")
    keep = lax.dynamic_slice_in_dim(x, core * half, half, 0)
    got = swap(lax.dynamic_slice_in_dim(x, (1 - core) * half, half, 0), "c")
    both = (keep.astype(F32) + got.astype(F32)).astype(x.dtype)
    count = lax.axis_size(CHIPS)
    parts = lax.all_to_all(both.reshape(count, -1, x.shape[1]), CHIPS, 0, 0)
    mine = parts.astype(F32).sum(0).astype(x.dtype)
    spread = jnp.broadcast_to(mine[None], (count,) + mine.shape)
    first = lax.all_to_all(spread, CHIPS, 0, 0).reshape(half, x.shape[1])
    second = swap(first, "c")
    return jnp.where(core == 0, jnp.concatenate([first, second]), jnp.concatenate([second, first]))


def per_device(
    node_in, edge_in, neighbors, chain_ids, residue_mask, w_msg_in, chain_vec, w_msg_out, gain_one,
    w_ffn_in, w_ffn_out, gain_two, w_edge_in, w_edge_out, gain_three, node_cot, edge_cot,
):
    dest_rows, width_k, edge_width = edge_in.shape
    rows_own, width = node_in.shape
    hidden_width = w_ffn_in.shape[1]
    nodes = chain_ids.shape[0]
    shares = lax.axis_size("y") * 2
    count_k = width_k + (-width_k) % 16
    piece = rows_own * count_k
    norm_scale = math.sqrt(width_k * shares)
    own_col = edge_width
    cols = {
        "width": edge_width, "own": own_col, "cross": own_col + rows_own,
        "mask": own_col + rows_own + 2, "hi": own_col + rows_own + 3, "lo": own_col + rows_own + 4,
    }
    me_core = lax.axis_index("c")
    share = lax.axis_index("y") * 2 + me_core
    group = lax.axis_index("z") * 2 + lax.axis_index("x")
    first_row = group * dest_rows

    dest_chain = lax.dynamic_slice_in_dim(chain_ids, first_row, dest_rows)
    dest_mask = lax.dynamic_slice_in_dim(residue_mask, first_row, dest_rows)
    lower = jnp.sum((chain_ids[None, :] < dest_chain[:, None]).astype(jnp.int32), axis=1)
    upper = jnp.sum((chain_ids[None, :] <= dest_chain[:, None]).astype(jnp.int32), axis=1)
    source = jnp.pad(neighbors, ((0, 0), (0, count_k - width_k)))
    bits = jnp.sum(residue_mask.reshape(nodes // 16, 16) << jnp.arange(16, dtype=jnp.int32)[None, :], axis=1)
    pick = (source >> 4)[:, :, None] == jnp.arange(nodes // 16, dtype=jnp.int32)[None, None, :]
    word = jnp.sum(jnp.where(pick, bits[None, None, :], 0), axis=2)
    present = (word >> (source & 15)) & 1
    inside = (jnp.arange(count_k) < width_k)[None, :]
    pair_mask = jnp.where(inside, dest_mask[:, None] * present, 0).astype(F32)
    cross = jnp.where((source < lower[:, None]) | (source >= upper[:, None]), pair_mask, 0.0)
    block = source // rows_own
    dest_core = ((jnp.arange(dest_rows) // rows_own) % 2)[:, None]
    place = ((block % 2) ^ dest_core) * (nodes // 2) + (block // 2) * rows_own + source % rows_own
    eye = (jnp.arange(dest_rows)[:, None] % rows_own == jnp.arange(rows_own)[None, :]).astype(F32)
    wide = jnp.concatenate(
        [
            jnp.pad(edge_in, ((0, 0), (0, count_k - width_k), (0, 0))),
            (pair_mask[:, :, None] * eye[:, None, :]).astype(BF),
            jnp.stack([cross, cross, pair_mask, (place >> 7).astype(F32), (place & 127).astype(F32)], axis=2).astype(BF),
            jnp.zeros((dest_rows, count_k, LANES - edge_width - rows_own - 5), BF),
        ],
        axis=2,
    )
    wide_cot = jnp.pad(edge_cot, ((0, 0), (0, count_k - width_k), (0, LANES - edge_width)))

    def to_owners(x):
        pieces = x.reshape((shares, rows_own) + x.shape[1:])
        got = [lax.dynamic_index_in_dim(pieces, share, 0, keepdims=False)]
        for q in range(1, shares):
            mine = lax.dynamic_index_in_dim(pieces, (share + q) % shares, 0, keepdims=False)
            got.append(lax.ppermute(mine, ("y", "c"), [(s, (s + q) % shares) for s in range(shares)]))
        return jnp.stack(got).reshape(shares, piece, x.shape[2])

    def to_shares(x):
        pieces = x.reshape(shares, rows_own, count_k, x.shape[2])
        got = [pieces[0]]
        for q in range(1, shares):
            got.append(lax.ppermute(pieces[q], ("y", "c"), [(s, (s - q) % shares) for s in range(shares)]))
        both = jnp.concatenate(got + got[:-1], axis=0)
        start = ((shares - share) % shares) * rows_own
        return lax.dynamic_slice_in_dim(both, start, dest_rows, 0)[:, :width_k, :]

    edges = to_owners(wide)
    cots = to_owners(wide_cot)
    nodes_all = gather_nodes(node_in)

    row = lambda v: v.reshape(1, -1)
    f_slope, index_rows, total, first_in, second_in, low, ffn_slope, ffn_hidden, node_out, e_src, e_own = pl.pallas_call(
        functools.partial(message_forward, cols, norm_scale),
        grid=(shares,),
        in_specs=[
            per_piece((shares, piece, LANES)), whole((nodes, width)), whole((rows_own, width)),
            whole(w_msg_in.shape), whole((1, width)), whole(w_msg_out.shape), whole((1, width)),
            pl.BlockSpec(memory_space=pl.ANY), pl.BlockSpec(memory_space=pl.ANY), whole((1, width)), whole(w_edge_in.shape),
        ],
        out_specs=[
            per_piece((shares, piece, width)), per_piece((shares, 1, piece)), whole((rows_own, width)), whole((rows_own, width)),
            whole((rows_own, width)), whole((rows_own, width)), whole((rows_own, hidden_width)), whole((rows_own, hidden_width)),
            whole((rows_own, width)), whole((rows_own, edge_width)), whole((rows_own, edge_width)),
        ],
        out_shape=[
            sds((shares, piece, width), BF), sds((shares, 1, piece), jnp.int32), sds((rows_own, width), BF), sds((rows_own, width), F32),
            sds((rows_own, width), F32), sds((rows_own, width), BF), sds((rows_own, hidden_width), F32), sds((rows_own, hidden_width), BF),
            sds((rows_own, width), BF), sds((rows_own, edge_width), BF), sds((rows_own, edge_width), BF),
        ],
        scratch_shapes=[
            pltpu.VMEM((nodes, width), BF), pltpu.VMEM((LANES, width), BF), pltpu.VMEM((HALF, width), F32),
            pltpu.VMEM(w_ffn_in.shape, BF), pltpu.VMEM(w_ffn_out.shape, BF), pltpu.SemaphoreType.DMA((2,)),
        ],
        compiler_params=params(),
        name="message_forward",
    )(edges, nodes_all, node_in, w_msg_in, row(chain_vec), w_msg_out, row(gain_one), w_ffn_in, w_ffn_out, row(gain_two), w_edge_in)

    e_table = gather_nodes(e_src)
    low_all = gather_nodes(low)

    edge_new, d_sum, e_scatter, g_in, g_out, g_gain3 = pl.pallas_call(
        functools.partial(edge_network, cols),
        grid=(shares,),
        in_specs=[
            per_piece((shares, piece, LANES)), per_piece((shares, piece, LANES)), per_piece((shares, 1, piece)),
            whole((nodes, edge_width)), whole((rows_own, edge_width)), whole(w_edge_in.shape), whole(w_edge_out.shape), whole((1, edge_width)),
        ],
        out_specs=[
            per_piece((shares, piece, edge_width)), per_piece((shares, piece, edge_width)), whole((nodes, edge_width)),
            whole((LANES, LANES)), whole((LANES, LANES)), whole((8, LANES)),
        ],
        out_shape=[
            sds((shares, piece, edge_width), BF), sds((shares, piece, edge_width), BF), sds((nodes, edge_width), BF),
            sds((LANES, LANES), F32), sds((LANES, LANES), F32), sds((8, LANES), F32),
        ],
        scratch_shapes=[
            pltpu.VMEM((nodes, LANES), BF), pltpu.VMEM((LANES, LANES), BF), pltpu.VMEM((LANES, LANES), BF),
            pltpu.VMEM((piece, LANES), BF), pltpu.VMEM((nodes, LANES), F32),
        ],
        compiler_params=params(),
        name="edge_network",
    )(edges, cots, index_rows, e_table, e_own, w_edge_in, w_edge_out, row(gain_three))

    e_parts = scatter_nodes(e_scatter)
    edge_out = to_shares(edge_new)

    d_ffn, d_hidden, d_first, g_gains, g_msg_out, g_edge_nodes = pl.pallas_call(
        functools.partial(node_backward, cols, norm_scale),
        out_shape=[
            sds((rows_own, width), BF), sds((rows_own, width), BF), sds((rows_own, width), F32), sds((8, width), F32),
            sds((width, width), BF), sds((width, 2 * LANES), BF),
        ],
        compiler_params=pltpu.CompilerParams(vmem_limit_bytes=56 << 20),
        name="node_backward",
    )(
        e_parts, g_in, node_cot, node_out, first_in, second_in, low, ffn_slope, ffn_hidden, total,
        w_edge_in, w_ffn_in, w_ffn_out, w_msg_out, row(gain_one), row(gain_two),
    )
    d_ffn_all = gather_nodes(d_ffn)

    pay_rows = 2 * width + edge_width + 64
    m_scatter, e_grad, pay, n_grad = pl.pallas_call(
        functools.partial(message_backward, cols),
        grid=(shares,),
        in_specs=[
            per_piece((shares, piece, LANES)), per_piece((shares, piece, width)), whole((rows_own, width)), per_piece((shares, 1, piece)),
            per_piece((shares, piece, edge_width)), whole(w_msg_in.shape), whole((nodes, width)), whole((rows_own, width)), whole((rows_own, width)),
        ],
        out_specs=[
            whole((nodes, width)), per_piece((shares, piece, edge_width)), whole((pay_rows, width)), whole((rows_own, width)),
        ],
        out_shape=[
            sds((nodes, width), BF), sds((shares, piece, edge_width), BF), sds((pay_rows, width), BF), sds((rows_own, width), F32),
        ],
        scratch_shapes=[
            pltpu.VMEM((HALF, width), BF), pltpu.VMEM((piece, width), BF), pltpu.VMEM((nodes, width), F32), pltpu.VMEM((LANES, width), F32),
        ],
        compiler_params=params(),
        name="message_backward",
    )(edges, f_slope, d_hidden, index_rows, d_sum, w_msg_in, nodes_all, node_in, d_first)

    edge_grad = to_shares(e_grad).astype(F32)
    m_parts = scatter_nodes(m_scatter)
    node_grad = pl.pallas_call(
        finish_nodes,
        out_shape=sds((rows_own, width), F32),
        compiler_params=pltpu.CompilerParams(vmem_limit_bytes=40 << 20),
        name="finish_nodes",
    )(m_parts, n_grad, w_msg_in)

    small = jnp.concatenate([g_in[:edge_width], g_out[:edge_width]], axis=1).astype(BF)
    g3 = jnp.pad(g_gain3.sum(0, keepdims=True), ((0, 0), (0, width - LANES)))
    vecs = jnp.concatenate([g_gains[:2], g3, jnp.zeros((61, width), F32)], axis=0).astype(BF)
    payload = jnp.concatenate([pay, g_msg_out, g_edge_nodes, small, vecs], axis=0)
    unit = 8 * lax.axis_size(CHIPS) * 2
    rows_pay = payload.shape[0]
    payload = jnp.pad(payload, ((0, (-rows_pay) % unit), (0, 0)))
    summed = sum_all(payload)

    g_ffn_in, g_ffn_out = pl.pallas_call(
        ffn_grads,
        grid=(hidden_width // 256,),
        in_specs=[
            whole((nodes, width)), whole((nodes, width)),
            pl.BlockSpec((width, 256), lambda i: (0, i)), pl.BlockSpec((256, width), lambda i: (i, 0)),
        ],
        out_specs=[pl.BlockSpec((width, 256), lambda i: (0, i)), pl.BlockSpec((256, width), lambda i: (i, 0))],
        out_shape=[sds(w_ffn_in.shape, F32), sds(w_ffn_out.shape, F32)],
        compiler_params=params(),
        name="ffn_grads",
    )(low_all, d_ffn_all, w_ffn_in, w_ffn_out)

    summed = summed.astype(F32)
    grad_msg_in = summed[: 2 * width + edge_width]
    grad_chain = summed[2 * width + edge_width]
    at = pay_rows
    grad_msg_out = summed[at : at + width]
    at += width
    g_nodes = summed[at : at + width]
    at += width
    small = summed[at : at + edge_width]
    at += edge_width
    grad_edge_in = jnp.concatenate(
        [g_nodes[:, :edge_width], g_nodes[:, LANES : LANES + edge_width], small[:, :edge_width]], axis=0
    )
    grad_edge_out = small[:, LANES : LANES + edge_width]
    return (
        node_out, edge_out, node_grad, edge_grad, grad_msg_in, grad_chain, grad_msg_out, summed[at],
        g_ffn_in, g_ffn_out, summed[at + 1], grad_edge_in, grad_edge_out, summed[at + 2, :edge_width],
    )


def solution(mesh):
    groups, shares = mesh.shape["res"], mesh.shape["edge"]
    fine = Mesh(mesh.devices.reshape(groups // 2, 2, shares // 2, 2), ("z", "x", "y", "c"))
    rows = P(("z", "x", "y", "c"), None)
    edges = P(("z", "x"), ("y", "c"), None)
    in_specs = (rows, edges, P(("z", "x"), ("y", "c"))) + (P(),) * 12 + (rows, edges)
    out_specs = (rows, edges, rows, edges) + (P(),) * 10
    return jax.shard_map(per_device, mesh=fine, in_specs=in_specs, out_specs=out_specs, check_vma=False)
```

```python
import functools
import math

import jax
import jax.numpy as jnp
from jax import lax
from jax.experimental import pallas as pl
from jax.experimental.pallas import tpu as pltpu
from jax.sharding import Mesh, PartitionSpec as P

EPS = 1e-05
CHIPS = ("z", "x", "y")
BF = jnp.bfloat16
F32 = jnp.float32
ROWS = 80
SPAN = 1280
RSQRT2 = math.sqrt(0.5)
INV_SQRT_2PI = 1.0 / math.sqrt(2.0 * math.pi)
PLACE, MASK, CROSS = 0, 1, 2


def mm(a, b):
    return jnp.dot(a, b, preferred_element_type=F32)


def mm_nt(a, b):
    return lax.dot_general(a, b, (((1,), (1,)), ((), ())), preferred_element_type=F32)


def mm_tn(a, b):
    return lax.dot_general(a, b, (((0,), (0,)), ((), ())), preferred_element_type=F32)


def gelu_pair(v):
    cdf = 0.5 * (1.0 + lax.erf(v * RSQRT2))
    pdf = INV_SQRT_2PI * jnp.exp(-0.5 * v * v)
    return v * cdf, cdf + v * pdf


def norm_parts(z):
    centre = z - jnp.mean(z, axis=-1, keepdims=True)
    r = lax.rsqrt(jnp.mean(centre * centre, axis=-1, keepdims=True) + EPS)
    return centre * r, r


def norm_back(n, r, gain, cot):
    b = cot * gain
    dz = r * (b - jnp.mean(b, -1, keepdims=True) - n * jnp.mean(b * n, -1, keepdims=True))
    return dz, jnp.sum(cot * n, axis=0, keepdims=True)


def gather_rows(place, halves):
    total = None
    for h, table in enumerate(halves):
        count = table.shape[0]
        block = min(count, SPAN)
        for start in range(0, count, block):
            lane = lax.broadcasted_iota(jnp.int32, (place.shape[0], block), 1) + (h * count + start)
            hot = jnp.where(lane == place, 1.0, 0.0).astype(BF)
            part = mm(hot, table[start : start + block, :])
            total = part if total is None else total + part
    return total


def scatter_rows(place_row, rows, acc):
    nodes = acc.shape[0]
    block = min(nodes, SPAN // 2)

    @pl.loop(0, nodes // block)
    def _(i):
        start = pl.multiple_of(i * block, block)
        row = lax.broadcasted_iota(jnp.int32, (block, place_row.shape[1]), 0) + start
        hot = jnp.where(row == place_row, 1.0, 0.0).astype(BF)
        acc[pl.ds(start, block), :] += mm(hot, rows)


def group_rows(where_ref, lo_ref, hi_ref, rows_own):
    group, core = where_ref[1], where_ref[2]
    start = pl.multiple_of(group * 2 * rows_own, 2 * rows_own)
    same = lo_ref[pl.ds(start, 2 * rows_own), :].astype(F32)
    other = hi_ref[pl.ds(start, 2 * rows_own), :].astype(F32)
    swapped = core == 1
    first = jnp.where(swapped, other, same)
    second = jnp.where(swapped, same, other)
    rows = [first[:rows_own], second[:rows_own], first[rows_own:], second[rows_own:]]
    return jnp.concatenate(rows, axis=0)


def put_shares(where_ref, refs, out):
    rows = refs[0].shape[0]
    shares = len(refs)
    for q, ref in enumerate(refs):
        at = lax.rem(where_ref[0] + shares - q, shares) * rows
        out[pl.ds(pl.multiple_of(at, 8), rows), :] = ref[...].astype(out.dtype)


def take_shares(where_ref, acc, refs):
    rows = refs[0].shape[0]
    shares = len(refs)
    for q, ref in enumerate(refs):
        at = lax.rem(where_ref[0] + q, shares) * rows
        ref[...] = acc[pl.ds(pl.multiple_of(at, 8), rows), :].astype(ref.dtype)


def add_up(refs):
    total = refs[0][...].astype(F32)
    for ref in refs[1:]:
        total += ref[...].astype(F32)
    return total


def message_forward(
    rows_own,
    where_ref, edge_ref, flags_ref, lo_ref, hi_ref, wmi_ref, chain_ref,
    slope_ref, s0, s1, s2, s3,
    table_lo, table_hi, own, acc, pre_s,
):
    step = pl.program_id(0)
    width = wmi_ref.shape[1]
    per, dest_rows, edge_width = edge_ref.shape
    edges = per * dest_rows

    @pl.when(step == 0)
    def _():
        weights = wmi_ref[width : 2 * width, :]
        half = lo_ref.shape[0]
        block = half // 2 if half <= SPAN else SPAN // 2

        @pl.loop(0, half // block)
        def _(i):
            at = pl.ds(pl.multiple_of(i * block, block), block)
            table_lo[at, :] = mm(lo_ref[at, :], weights).astype(BF)
            table_hi[at, :] = mm(hi_ref[at, :], weights).astype(BF)

        group = group_rows(where_ref, lo_ref, hi_ref, rows_own).astype(BF)
        own[...] = mm(group, wmi_ref[:width, :])
        acc[...] = jnp.zeros_like(acc)

    flags = jnp.transpose(flags_ref[0])[:edges, :]
    place = flags[:, PLACE : PLACE + 1].astype(jnp.int32)
    pre_s[...] = gather_rows(place, (table_lo, table_hi)) + mm(
        edge_ref[...].reshape(edges, edge_width), wmi_ref[2 * width :, :]
    )
    for j in range(per):
        for r in range(0, dest_rows, ROWS):
            at = slice(j * dest_rows + r, j * dest_rows + r + ROWS)
            mask = flags[at, MASK : MASK + 1]
            cross = flags[at, CROSS : CROSS + 1]
            pre = pre_s[at, :] + own[r : r + ROWS, :] + cross * chain_ref[...]
            hidden, slope = gelu_pair(pre)
            slope = slope * mask
            slope_ref[j, r : r + ROWS, :] = slope.astype(BF)
            acc[r : r + ROWS, :width] += hidden.astype(BF).astype(F32) * mask
            acc[r : r + ROWS, width:] += slope

    @pl.when(step == pl.num_programs(0) - 1)
    def _():
        take_shares(where_ref, acc, (s0, s1, s2, s3))


def node_forward(
    norm_scale,
    s0, s1, s2, s3, node_ref, wmo_ref, gain1_ref, wfi_ref, wfo_ref, gain2_ref, weit_ref,
    total_ref, slopes_ref, first_ref, second_ref, low_ref, fslope_ref, fhidden_ref, out_ref, src_ref, eown_ref,
):
    width = node_ref.shape[1]
    sums = add_up((s0, s1, s2, s3))
    total = sums[:, :width].astype(BF)
    total_ref[...] = total
    slopes_ref[...] = sums[:, width:]
    first_in = node_ref[...].astype(F32) + mm(total, wmo_ref[...]) * (1.0 / norm_scale)
    first_ref[...] = first_in
    norm_one = norm_parts(first_in)[0] * gain1_ref[...]
    low = norm_one.astype(BF)
    low_ref[...] = low
    hidden, slope = gelu_pair(mm(low, wfi_ref[...]))
    hidden = hidden.astype(BF)
    fslope_ref[...] = slope
    fhidden_ref[...] = hidden
    second_in = norm_one + mm(hidden, wfo_ref[...])
    second_ref[...] = second_in
    node_out = (norm_parts(second_in)[0] * gain2_ref[...]).astype(BF)
    out_ref[...] = node_out
    eown_ref[...] = mm_nt(node_out, weit_ref[:, :width]).astype(BF)
    src = mm_nt(node_out, weit_ref[:, width : 2 * width]).astype(BF)
    for i in range(src_ref.shape[0]):
        src_ref[i] = src


def edge_network(
    where_ref, edge_ref, cot_ref, flags_ref, lo_ref, hi_ref, e0, e1, e2, e3, weit_ref, weo_ref, gain_ref,
    out_ref, dsum_ref, slo_ref, shi_ref, o0, o1, o2, o3, gin_ref, gout_ref, ggain_ref,
    own, dpre_s, hidden_s, delta_s, acc, own_acc,
):
    step = pl.program_id(0)
    per, dest_rows, edge_width = edge_ref.shape
    edges = per * dest_rows
    width = (weit_ref.shape[1] - edge_width) // 2
    weights_t = weit_ref[:, 2 * width :]

    @pl.when(step == 0)
    def _():
        put_shares(where_ref, (e0, e1, e2, e3), own)
        acc[...] = jnp.zeros_like(acc)
        own_acc[...] = jnp.zeros_like(own_acc)
        gin_ref[...] = jnp.zeros_like(gin_ref)
        gout_ref[...] = jnp.zeros_like(gout_ref)
        ggain_ref[...] = jnp.zeros_like(ggain_ref)

    flags = jnp.transpose(flags_ref[0])[:edges, :]
    place = flags[:, PLACE : PLACE + 1].astype(jnp.int32)
    edge_all = edge_ref[...].reshape(edges, edge_width)
    pre_all = gather_rows(place, (lo_ref, hi_ref)) + mm_nt(edge_all, weights_t)
    gain = gain_ref[...]
    for j in range(per):
        at = slice(j * dest_rows, (j + 1) * dest_rows)
        mask = flags[at, MASK : MASK + 1]
        hidden, slope = gelu_pair(pre_all[at, :] + own[...])
        hidden = (hidden * mask).astype(BF)
        hidden_s[at, :] = hidden
        n, r = norm_parts(edge_ref[j].astype(F32) + mm(hidden, weo_ref[...]))
        out_ref[j] = (n * gain).astype(BF)
        cot = cot_ref[j].astype(F32)
        cn = cot * n
        ggain_ref[...] += jnp.sum(cn.reshape(dest_rows // 8, 8, edge_width), axis=0)
        b = cot * gain
        dz = r * (b - jnp.mean(b, -1, keepdims=True) - n * jnp.mean(cn * gain, -1, keepdims=True))
        d_delta = (dz * mask).astype(BF)
        delta_s[at, :] = d_delta
        d_pre = slope * mm_nt(d_delta, weo_ref[...])
        d_low = d_pre.astype(BF)
        own_acc[...] += d_low.astype(F32)
        dpre_s[at, :] = d_low
        dsum_ref[j] = (dz + mm(d_low, weights_t)).astype(BF)
    gout_ref[...] += mm_tn(hidden_s[...], delta_s[...])
    gin_ref[...] += mm_tn(edge_all, dpre_s[...])
    place_row = flags_ref[0, PLACE : PLACE + 1, :edges].astype(jnp.int32)
    scatter_rows(place_row, dpre_s[...], acc)

    @pl.when(step == pl.num_programs(0) - 1)
    def _():
        half = slo_ref.shape[0]
        slo_ref[...] = acc[:half, :].astype(BF)
        shi_ref[...] = acc[half:, :].astype(BF)
        take_shares(where_ref, own_acc, (o0, o1, o2, o3))


def node_backward(
    norm_scale,
    where_ref, parts_ref, o0, o1, o2, o3, node_ref, node_cot_ref, out_ref, first_ref, second_ref, low_ref, fslope_ref,
    fhidden_ref, total_ref, slopes_ref, weit_ref, wmi_ref, wfi_ref, wfo_ref, wmo_ref, gain1_ref, gain2_ref,
    d_ref, both_ref, ngrad_ref, ggain_ref, keep_ref, send_ref,
    pay,
):
    width = out_ref.shape[1]
    edge_width = weit_ref.shape[0]
    from_sources = add_up(tuple(parts_ref.at[i] for i in range(parts_ref.shape[0]))).astype(BF)
    from_own = add_up((o0, o1, o2, o3)).astype(BF)
    d_updated = (
        node_cot_ref[...].astype(F32)
        + mm(from_own, weit_ref[:, :width])
        + mm(from_sources, weit_ref[:, width : 2 * width])
    )
    node_out = out_ref[...]
    n, r = norm_parts(second_ref[...])
    d_second, ggain2 = norm_back(n, r, gain2_ref[...], d_updated)
    dffn = d_second.astype(BF)
    both_ref[:, :width] = low_ref[...]
    both_ref[:, width:] = dffn
    d_ffn_pre = (fslope_ref[...] * mm_nt(dffn, wfo_ref[...])).astype(BF)
    d_norm_one = d_second + mm_nt(d_ffn_pre, wfi_ref[...])
    n, r = norm_parts(first_ref[...])
    d_first, ggain1 = norm_back(n, r, gain1_ref[...], d_norm_one)
    d_summed = (d_first * (1.0 / norm_scale)).astype(BF)
    d_hidden = mm_nt(d_summed, wmo_ref[...])
    d_ref[...] = d_hidden.astype(BF)
    own_sum = (d_hidden * slopes_ref[...]).astype(BF)
    ngrad_ref[...] = d_first + mm_nt(own_sum, wmi_ref[:width, :])
    ggain_ref[...] = jnp.concatenate([ggain1, ggain2, jnp.zeros((6, width), F32)], axis=0)
    parts = (
        mm_tn(total_ref[...], d_summed), mm_tn(node_ref[...], own_sum), mm_tn(from_own, node_out), mm_tn(from_sources, node_out)
    )
    at = 0
    for part in parts:
        pay[at : at + part.shape[0], :] = part.astype(BF)
        at += part.shape[0]
    pay[at:, :] = jnp.zeros((pay.shape[0] - at, width), BF)
    split_halves(where_ref, pay, keep_ref, send_ref)


def split_halves(where_ref, pay, keep_ref, send_ref):
    half = pay.shape[0] // 2
    at = pl.multiple_of(where_ref[2] * half, 16)
    keep_ref[...] = pay[pl.ds(at, half), :].reshape(keep_ref.shape)
    send_ref[...] = pay[pl.ds(half - at, half), :].reshape(send_ref.shape)


def message_backward(
    where_ref, edge_ref, slope_ref, flags_ref, dsum_ref, d0, d1, d2, d3, wmi_ref, lo_ref, hi_ref, gain_ref, gain3_ref, gin_ref,
    gout_ref,
    keep_ref, send_ref, eg_ref,
    own, dpre_s, acc, gin, chain, pay,
):
    step = pl.program_id(0)
    width = wmi_ref.shape[1]
    per, dest_rows, edge_width = edge_ref.shape
    edges = per * dest_rows
    weights = wmi_ref[2 * width :, :]

    @pl.when(step == 0)
    def _():
        put_shares(where_ref, (d0, d1, d2, d3), own)
        acc[...] = jnp.zeros_like(acc)
        gin[...] = jnp.zeros_like(gin)
        chain[...] = jnp.zeros_like(chain)

    flags = jnp.transpose(flags_ref[0])[:edges, :]
    for j in range(per):
        for r in range(0, dest_rows, ROWS):
            at = slice(j * dest_rows + r, j * dest_rows + r + ROWS)
            d_low = (slope_ref[j, r : r + ROWS, :].astype(F32) * own[r : r + ROWS, :]).astype(BF)
            dpre_s[at, :] = d_low
            crossed = d_low.astype(F32) * flags[at, CROSS : CROSS + 1]
            chain[...] += jnp.sum(crossed.reshape(ROWS // 8, 8, width), axis=0)
    d_all = dpre_s[...]
    gin[...] += mm_tn(edge_ref[...].reshape(edges, edge_width), d_all)
    back = mm_nt(d_all, weights)
    for j in range(per):
        eg_ref[j] = dsum_ref[j].astype(F32) + back[j * dest_rows : (j + 1) * dest_rows, :]
    place_row = flags_ref[0, PLACE : PLACE + 1, :edges].astype(jnp.int32)
    scatter_rows(place_row, d_all, acc)

    @pl.when(step == pl.num_programs(0) - 1)
    def _():
        half = lo_ref.shape[0]
        chips = keep_ref.shape[0]
        rows = half // chips
        late = keep_ref.shape[1] - rows
        for chip in range(chips):
            keep_ref[chip, late:, :] = acc[chip * rows : (chip + 1) * rows, :].astype(BF)
            send_ref[chip, late:, :] = acc[half + chip * rows : half + (chip + 1) * rows, :].astype(BF)
        from_nodes = mm_tn(lo_ref[...], acc[:half, :].astype(BF)) + mm_tn(hi_ref[...], acc[half:, :].astype(BF))
        pay[:width, :] = from_nodes.astype(BF)
        at = width
        pay[at : at + edge_width, :] = gin[...].astype(BF)
        at += edge_width
        spare = jnp.zeros((edge_width, width - 2 * edge_width), F32)
        pay[at : at + edge_width, :] = jnp.concatenate([gin_ref[...], gout_ref[...], spare], axis=1).astype(BF)
        at += edge_width
        crossed = jnp.sum(chain[...], axis=0, keepdims=True)
        gain3 = jnp.concatenate([jnp.sum(gain3_ref[...], axis=0, keepdims=True), jnp.zeros((1, width - edge_width), F32)], axis=1)
        vecs = jnp.concatenate([gain_ref[:2, :], gain3, crossed, jnp.zeros((12, width), F32)], axis=0)
        pay[at : at + 16, :] = vecs.astype(BF)
        pay[at + 16 :, :] = jnp.zeros((pay.shape[0] - at - 16, width), BF)
        half_pay = pay.shape[0] // 2
        start = pl.multiple_of(where_ref[2] * half_pay, 16)
        keep_ref[:, :late, :] = pay[pl.ds(start, half_pay), :].reshape(chips, late, width)
        send_ref[:, :late, :] = pay[pl.ds(half_pay - start, half_pay), :].reshape(chips, late, width)


def finish_nodes(late, parts_ref, ngrad_ref, wmi_ref, out_ref, spread_ref):
    width = ngrad_ref.shape[1]
    total = add_up(tuple(parts_ref.at[i] for i in range(parts_ref.shape[0])))
    out_ref[...] = ngrad_ref[...] + mm_nt(total[late:, :].astype(BF), wmi_ref[width : 2 * width, :])
    mine = total[:late, :].astype(BF)
    for i in range(spread_ref.shape[0]):
        spread_ref[i] = mine


def finish_weights(
    edge_width, turned,
    where_ref, p0, p1, p2, p3, p4, p5, p6, p7, same_ref, other_ref,
    gmi_ref, gmo_ref, geit_ref, geo_ref, vecs_ref,
    early, late,
):
    width = gmi_ref.shape[1]
    rows, layers = turned
    for i, ref in enumerate((p0, p1, p2, p3, p4, p5, p6, p7)):
        dc, dy, dx = i // 4, (i // 2) % 2, i % 2
        x, y, core = where_ref[4] ^ dx, where_ref[5] ^ dy, where_ref[2] ^ dc
        for k in range(layers):
            z = lax.rem(where_ref[3] + k, layers) if layers <= 4 else k
            at = (core * layers * 4 + (z * 2 + x) * 2 + y) * rows
            early[pl.ds(pl.multiple_of(at, 16), rows), :] = ref[k * rows : (k + 1) * rows, :]
    half = late.shape[0] // 2
    start = pl.multiple_of(where_ref[2] * half, 16)
    late[pl.ds(start, half), :] = same_ref[...]
    late[pl.ds(half - start, half), :] = other_ref[...]
    gmo_ref[...] = early[:width, :].astype(F32)
    gmi_ref[:width, :] = early[width : 2 * width, :].astype(F32)
    gmi_ref[width:, :] = late[: width + edge_width, :].astype(F32)
    at = 2 * width
    geit_ref[:, :width] = early[at : at + edge_width, :].astype(F32)
    geit_ref[:, width : 2 * width] = early[at + edge_width : at + 2 * edge_width, :].astype(F32)
    at = width + edge_width
    small = late[at : at + edge_width, :].astype(F32)
    geit_ref[:, 2 * width :] = jnp.transpose(small[:, :edge_width])
    geo_ref[...] = small[:, edge_width : 2 * edge_width]
    vecs_ref[...] = late[at + edge_width : at + edge_width + 16, :].astype(F32)[:8, :]


def ffn_grads(p0, p1, p2, p3, p4, p5, p6, p7, wfi_ref, wfo_ref, gfi_ref, gfo_ref, rows):
    width = wfi_ref.shape[0]
    count = p0.shape[0]

    @pl.when(pl.program_id(0) == 0)
    def _():
        for i, ref in enumerate((p0, p1, p2, p3, p4, p5, p6, p7)):
            rows[i * count : (i + 1) * count, :] = ref[...]

    block = min(rows.shape[0], SPAN // 2)
    gfi = gfo = None
    for start in range(0, rows.shape[0], block):
        low = rows[start : start + block, :width]
        dffn = rows[start : start + block, width:]
        hidden, slope = gelu_pair(mm(low, wfi_ref[...]))
        part = mm_tn(hidden.astype(BF), dffn)
        gfo = part if gfo is None else gfo + part
        d_pre = (slope * mm_nt(dffn, wfo_ref[...])).astype(BF)
        part = mm_tn(low, d_pre)
        gfi = part if gfi is None else gfi + part
    gfo_ref[...] = gfo
    gfi_ref[...] = gfi


def whole(shape):
    return pl.BlockSpec(tuple(shape), lambda *_: (0,) * len(shape))


def per_step(count, shape):
    return pl.BlockSpec((count,) + tuple(shape[1:]), lambda i: (i,) + (0,) * (len(shape) - 1))


SCALARS = pl.BlockSpec(memory_space=pltpu.SMEM)


def params(limit=56):
    return pltpu.CompilerParams(vmem_limit_bytes=limit << 20, dimension_semantics=("arbitrary",))


def sds(shape, dtype):
    return jax.ShapeDtypeStruct(tuple(shape), dtype)


def swap(x, axis):
    return lax.ppermute(x, axis, [(0, 1), (1, 0)])


def gather_spread(spread):
    same = lax.all_to_all(spread, CHIPS, 0, 0).reshape(-1, spread.shape[2])
    return same, swap(same, "c")


def scatter_halves(lo, hi):
    got = swap(hi, "c")
    both = (lo.astype(F32) + got.astype(F32)).astype(lo.dtype)
    return lax.all_to_all(both.reshape(lax.axis_size(CHIPS), -1, lo.shape[1]), CHIPS, 0, 0)


def send_shares(pieces):
    shares = len(pieces)
    got = [pieces[0]]
    for q in range(1, shares):
        got.append(lax.ppermute(pieces[q], ("y", "c"), [(s, (s + q) % shares) for s in range(shares)]))
    return got


def to_owners(keep, send):
    got = swap(send, "c")
    both = (keep.astype(F32) + got.astype(F32)).astype(keep.dtype)
    return lax.all_to_all(both, CHIPS, 0, 0)


def gather_steps(x):
    layers = lax.axis_size("z")
    if layers <= 4:
        got = [x]
        for k in range(1, layers):
            got.append(lax.ppermute(x, "z", [((z + k) % layers, z) for z in range(layers)]))
        x = jnp.concatenate(got, axis=0)
    else:
        x = lax.all_gather(x, "z", axis=0, tiled=True)
    pieces = [x]
    for axis in ("x", "y", "c"):
        pieces = pieces + [swap(p, axis) for p in pieces]
    return pieces


def after(x, done):
    flat, tree = jax.tree.flatten((x, done))
    return jax.tree.unflatten(tree, lax.optimization_barrier(flat))[0]


def per_device(
    node_in, edge_in, neighbors, chain_ids, residue_mask, w_msg_in, chain_vec, w_msg_out, gain_one,
    w_ffn_in, w_ffn_out, gain_two, w_edge_in, w_edge_out, gain_three, node_cot, edge_cot,
):
    dest_rows, width_k, edge_width = edge_in.shape
    rows_own, width = node_in.shape
    hidden_width = w_ffn_in.shape[1]
    nodes = chain_ids.shape[0]
    half = nodes // 2
    chips = lax.axis_size(CHIPS)
    per = 3 if width_k % 3 == 0 else 1
    steps = width_k // per
    count = per * dest_rows
    lanes = count + (-count) % 128
    shares = dest_rows // rows_own
    norm_scale = math.sqrt(width_k * shares)
    me_core = lax.axis_index("c")
    share = lax.axis_index("y") * 2 + me_core
    group = lax.axis_index("z") * 2 + lax.axis_index("x")
    z, x, y = (lax.axis_index(axis) for axis in CHIPS)
    where = jnp.stack([share, group, me_core, z, x, y]).astype(jnp.int32)

    edges = edge_in.transpose(1, 0, 2)
    cots = edge_cot.transpose(1, 0, 2)
    lo, hi = gather_spread(jnp.broadcast_to(node_in[None], (chips,) + node_in.shape))

    first_row = group * dest_rows
    source = neighbors.T
    dest_chain = lax.dynamic_slice_in_dim(chain_ids, first_row, dest_rows)
    dest_mask = lax.dynamic_slice_in_dim(residue_mask, first_row, dest_rows)
    lower = jnp.sum((chain_ids[None, :] < dest_chain[:, None]).astype(jnp.int32), axis=1)
    upper = jnp.sum((chain_ids[None, :] <= dest_chain[:, None]).astype(jnp.int32), axis=1)
    bits = jnp.sum(residue_mask.reshape(nodes // 16, 16) << jnp.arange(16, dtype=jnp.int32)[None, :], axis=1)
    pick = (source >> 4)[:, :, None] == jnp.arange(nodes // 16, dtype=jnp.int32)[None, None, :]
    word = jnp.sum(jnp.where(pick, bits[None, None, :], 0), axis=2)
    present = (word >> (source & 15)) & 1
    pair_mask = (dest_mask[None, :] * present).astype(F32)
    cross = ((source < lower[None, :]) | (source >= upper[None, :])).astype(F32)
    block = source // rows_own
    place = ((block % 2) ^ me_core) * half + (block // 2) * rows_own + source % rows_own
    table = jnp.stack([place.astype(F32), pair_mask, cross]).reshape(3, steps, count).transpose(1, 0, 2)
    flags = jnp.pad(table, ((0, 0), (0, 5), (0, lanes - count)))

    row = lambda v: v.reshape(1, -1)
    wei_t = w_edge_in.T
    edge_spec = per_step(per, edges.shape)
    flag_spec = per_step(1, flags.shape)
    wide_spec = [whole((rows_own, 2 * width))] * shares
    wide_out = [sds((rows_own, 2 * width), BF)] * shares
    share_spec = [whole((rows_own, width))] * shares

    f_slope, *sums = pl.pallas_call(
        functools.partial(message_forward, rows_own),
        grid=(steps,),
        in_specs=[
            SCALARS, edge_spec, flag_spec, whole((half, width)), whole((half, width)), whole(w_msg_in.shape), whole((1, width)),
        ],
        out_specs=[per_step(per, (width_k, dest_rows, width))] + wide_spec,
        out_shape=[sds((width_k, dest_rows, width), BF)] + wide_out,
        scratch_shapes=[
            pltpu.VMEM((half, width), BF), pltpu.VMEM((half, width), BF), pltpu.VMEM((dest_rows, width), F32),
            pltpu.VMEM((dest_rows, 2 * width), F32), pltpu.VMEM((count, width), F32),
        ],
        compiler_params=params(),
        name="message_forward",
    )(where, edges, flags, lo, hi, w_msg_in, row(chain_vec))
    sums = send_shares(sums)

    total, slopes, first_in, second_in, low, ffn_slope, ffn_hidden, node_out, e_spread, e_own = pl.pallas_call(
        functools.partial(node_forward, norm_scale),
        out_shape=[
            sds((rows_own, width), BF), sds((rows_own, width), F32), sds((rows_own, width), F32), sds((rows_own, width), F32),
            sds((rows_own, width), BF), sds((rows_own, hidden_width), F32), sds((rows_own, hidden_width), BF), sds((rows_own, width), BF),
            sds((chips, rows_own, edge_width), BF), sds((rows_own, edge_width), BF),
        ],
        compiler_params=pltpu.CompilerParams(vmem_limit_bytes=56 << 20),
        name="node_forward",
    )(*sums, node_in, w_msg_out, row(gain_one), w_ffn_in, w_ffn_out, row(gain_two), wei_t)

    e_owns = send_shares([e_own] * shares)
    e_lo, e_hi = gather_spread(e_spread)

    edge_new, d_sum, e_slo, e_shi, *rest = pl.pallas_call(
        edge_network,
        grid=(steps,),
        in_specs=[SCALARS, edge_spec, edge_spec, flag_spec, whole((half, edge_width)), whole((half, edge_width))]
        + [whole((rows_own, edge_width))] * shares
        + [whole(wei_t.shape), whole(w_edge_out.shape), whole((1, edge_width))],
        out_specs=[edge_spec, edge_spec, whole((half, edge_width)), whole((half, edge_width))]
        + [whole((rows_own, edge_width))] * shares
        + [whole((edge_width, edge_width)), whole((edge_width, edge_width)), whole((8, edge_width))],
        out_shape=[sds(edges.shape, BF), sds(edges.shape, BF), sds((half, edge_width), BF), sds((half, edge_width), BF)]
        + [sds((rows_own, edge_width), BF)] * shares
        + [sds((edge_width, edge_width), F32), sds((edge_width, edge_width), F32), sds((8, edge_width), F32)],
        scratch_shapes=[
            pltpu.VMEM((dest_rows, edge_width), F32), pltpu.VMEM((count, edge_width), BF), pltpu.VMEM((count, edge_width), BF),
            pltpu.VMEM((count, edge_width), BF), pltpu.VMEM((nodes, edge_width), F32), pltpu.VMEM((dest_rows, edge_width), F32),
        ],
        compiler_params=params(),
        name="edge_network",
    )(where, edges, cots, flags, e_lo, e_hi, *e_owns, wei_t, w_edge_out, row(gain_three))
    g_in, g_out, g_gain3 = rest[shares:]
    e_sums = send_shares(rest[:shares])
    e_parts = scatter_halves(e_slo, e_shi)

    up = lambda rows: rows + (-rows) % (32 * chips)
    pay_early = up(2 * width + 2 * edge_width)
    pay_late = up(width + 2 * edge_width + 16)
    early_rows, late_rows = pay_early // (2 * chips), pay_late // (2 * chips)
    d_hidden, both, n_grad, g_gains, keep, send = pl.pallas_call(
        functools.partial(node_backward, norm_scale),
        in_specs=[SCALARS] + [pl.BlockSpec(memory_space=pltpu.VMEM)] * 22,
        out_shape=[
            sds((rows_own, width), BF), sds((rows_own, 2 * width), BF), sds((rows_own, width), F32), sds((8, width), F32),
            sds((chips, early_rows, width), BF), sds((chips, early_rows, width), BF),
        ],
        scratch_shapes=[pltpu.VMEM((pay_early, width), BF)],
        compiler_params=pltpu.CompilerParams(vmem_limit_bytes=56 << 20),
        name="node_backward",
    )(
        where, e_parts, *e_sums, node_in, node_cot, node_out, first_in, second_in, low, ffn_slope, ffn_hidden, total, slopes,
        wei_t, w_msg_in, w_ffn_in, w_ffn_out, w_msg_out, row(gain_one), row(gain_two),
    )
    d_hiddens = send_shares([d_hidden] * shares)
    early_parts = to_owners(after(keep, d_hiddens), send)
    both_pieces = gather_steps(after(both, d_hiddens))

    sent = (chips, late_rows + rows_own, width)
    keep, send, e_grad = pl.pallas_call(
        message_backward,
        grid=(steps,),
        in_specs=[SCALARS, edge_spec, per_step(per, (width_k, dest_rows, width)), flag_spec, edge_spec]
        + share_spec + [whole(w_msg_in.shape), whole((half, width)), whole((half, width)), whole((8, width))]
        + [whole((8, edge_width)), whole((edge_width, edge_width)), whole((edge_width, edge_width))],
        out_specs=[whole(sent), whole(sent), edge_spec],
        out_shape=[sds(sent, BF), sds(sent, BF), sds(edges.shape, F32)],
        scratch_shapes=[
            pltpu.VMEM((dest_rows, width), F32), pltpu.VMEM((count, width), BF), pltpu.VMEM((nodes, width), F32),
            pltpu.VMEM((edge_width, width), F32), pltpu.VMEM((8, width), F32), pltpu.VMEM((pay_late, width), BF),
        ],
        compiler_params=params(),
        name="message_backward",
    )(where, edges, f_slope, flags, d_sum, *d_hiddens, w_msg_in, lo, hi, g_gains, g_gain3, g_in, g_out)
    late_parts = to_owners(keep, send)
    early_pieces = gather_steps(early_parts.astype(F32).sum(0).astype(BF))

    node_grad, spread = pl.pallas_call(
        functools.partial(finish_nodes, late_rows),
        out_shape=[sds((rows_own, width), F32), sds((chips, late_rows, width), BF)],
        compiler_params=pltpu.CompilerParams(vmem_limit_bytes=40 << 20),
        name="finish_nodes",
    )(late_parts, n_grad, w_msg_in)
    same, other = gather_spread(spread)

    tile = 256
    both_pieces = after(both_pieces, spread)
    g_ffn_in, g_ffn_out = pl.pallas_call(
        ffn_grads,
        grid=(hidden_width // tile,),
        in_specs=[whole((nodes // 8, 2 * width))] * 8
        + [pl.BlockSpec((width, tile), lambda i: (0, i)), pl.BlockSpec((tile, width), lambda i: (i, 0))],
        out_specs=[pl.BlockSpec((width, tile), lambda i: (0, i)), pl.BlockSpec((tile, width), lambda i: (i, 0))],
        out_shape=[sds(w_ffn_in.shape, F32), sds(w_ffn_out.shape, F32)],
        scratch_shapes=[pltpu.VMEM((nodes, 2 * width), BF)],
        compiler_params=params(),
        name="ffn_grads",
    )(*both_pieces, w_ffn_in, w_ffn_out)

    g_msg_in, g_msg_out, g_edge_t, g_edge_out, vecs = pl.pallas_call(
        functools.partial(finish_weights, edge_width, (early_rows, lax.axis_size("z"))),
        in_specs=[SCALARS] + [pl.BlockSpec(memory_space=pltpu.VMEM)] * 10,
        out_shape=[
            sds(w_msg_in.shape, F32), sds((width, width), F32), sds(wei_t.shape, F32), sds((edge_width, edge_width), F32),
            sds((8, width), F32),
        ],
        scratch_shapes=[pltpu.VMEM((pay_early, width), BF), pltpu.VMEM((pay_late, width), BF)],
        compiler_params=pltpu.CompilerParams(vmem_limit_bytes=56 << 20),
        name="finish_weights",
    )(where, *early_pieces, same, other)
    return (
        node_out, edge_new.transpose(1, 0, 2), node_grad, e_grad.transpose(1, 0, 2), g_msg_in, vecs[3], g_msg_out,
        vecs[0], g_ffn_in, g_ffn_out, vecs[1], g_edge_t.T, g_edge_out, vecs[2, :edge_width],
    )


def solution(mesh):
    groups, shares = mesh.shape["res"], mesh.shape["edge"]
    fine = Mesh(mesh.devices.reshape(groups // 2, 2, shares // 2, 2), ("z", "x", "y", "c"))
    rows = P(("z", "x", "y", "c"), None)
    edges = P(("z", "x"), ("y", "c"), None)
    in_specs = (rows, edges, P(("z", "x"), ("y", "c"))) + (P(),) * 12 + (rows, edges)
    out_specs = (rows, edges, rows, edges) + (P(),) * 10
    return jax.shard_map(per_device, mesh=fine, in_specs=in_specs, out_specs=out_specs, check_vma=False)
```

```python
import functools
import math

import jax
import jax.numpy as jnp
from jax import lax
from jax.experimental import pallas as pl
from jax.experimental.pallas import tpu as pltpu
from jax.sharding import Mesh, PartitionSpec as P

EPS = 1e-05
CHIPS = ("z", "x", "y")
BF = jnp.bfloat16
F32 = jnp.float32
ROWS = 80
SPAN = 1280
RSQRT2 = math.sqrt(0.5)
INV_SQRT_2PI = 1.0 / math.sqrt(2.0 * math.pi)
PLACE, MASK, CROSS = 0, 1, 2


def mm(a, b):
    return jnp.dot(a, b, preferred_element_type=F32)


def mm_nt(a, b):
    return lax.dot_general(a, b, (((1,), (1,)), ((), ())), preferred_element_type=F32)


def mm_tn(a, b):
    return lax.dot_general(a, b, (((0,), (0,)), ((), ())), preferred_element_type=F32)


def gelu_pair(v):
    cdf = 0.5 * (1.0 + lax.erf(v * RSQRT2))
    pdf = INV_SQRT_2PI * jnp.exp(-0.5 * v * v)
    return v * cdf, cdf + v * pdf


def norm_parts(z):
    centre = z - jnp.mean(z, axis=-1, keepdims=True)
    r = lax.rsqrt(jnp.mean(centre * centre, axis=-1, keepdims=True) + EPS)
    return centre * r, r


def norm_back(n, r, gain, cot):
    b = cot * gain
    dz = r * (b - jnp.mean(b, -1, keepdims=True) - n * jnp.mean(b * n, -1, keepdims=True))
    return dz, jnp.sum(cot * n, axis=0, keepdims=True)


def gather_rows(place, halves):
    total = None
    for h, table in enumerate(halves):
        count = table.shape[0]
        block = min(count, SPAN)
        for start in range(0, count, block):
            lane = lax.broadcasted_iota(jnp.int32, (place.shape[0], block), 1) + (h * count + start)
            hot = jnp.where(lane == place, 1.0, 0.0).astype(BF)
            part = mm(hot, table[start : start + block, :])
            total = part if total is None else total + part
    return total


def scatter_rows(place_row, rows, acc):
    nodes = acc.shape[0]
    block = min(nodes, SPAN // 2)

    @pl.loop(0, nodes // block)
    def _(i):
        start = pl.multiple_of(i * block, block)
        row = lax.broadcasted_iota(jnp.int32, (block, place_row.shape[1]), 0) + start
        hot = jnp.where(row == place_row, 1.0, 0.0).astype(BF)
        acc[pl.ds(start, block), :] += mm(hot, rows)


def group_rows(where_ref, lo_ref, hi_ref, rows_own):
    group, core = where_ref[1], where_ref[2]
    start = pl.multiple_of(group * 2 * rows_own, 2 * rows_own)
    same = lo_ref[pl.ds(start, 2 * rows_own), :].astype(F32)
    other = hi_ref[pl.ds(start, 2 * rows_own), :].astype(F32)
    swapped = core == 1
    first = jnp.where(swapped, other, same)
    second = jnp.where(swapped, same, other)
    rows = [first[:rows_own], second[:rows_own], first[rows_own:], second[rows_own:]]
    return jnp.concatenate(rows, axis=0)


def put_shares(where_ref, refs, out):
    rows = refs[0].shape[0]
    shares = len(refs)
    for q, ref in enumerate(refs):
        at = lax.rem(where_ref[0] + shares - q, shares) * rows
        out[pl.ds(pl.multiple_of(at, 8), rows), :] = ref[...].astype(out.dtype)


def take_shares(where_ref, acc, refs):
    rows = refs[0].shape[0]
    shares = len(refs)
    for q, ref in enumerate(refs):
        at = lax.rem(where_ref[0] + q, shares) * rows
        ref[...] = acc[pl.ds(pl.multiple_of(at, 8), rows), :].astype(ref.dtype)


def add_up(refs):
    total = refs[0][...].astype(F32)
    for ref in refs[1:]:
        total += ref[...].astype(F32)
    return total


def message_forward(
    rows_own,
    where_ref, edge_ref, flags_ref, lo_ref, hi_ref, wmi_ref, chain_ref,
    slope_ref, s0, s1, s2, s3,
    table_lo, table_hi, own, acc, pre_s,
):
    step = pl.program_id(0)
    width = wmi_ref.shape[1]
    per, dest_rows, edge_width = edge_ref.shape
    edges = per * dest_rows

    @pl.when(step == 0)
    def _():
        weights = wmi_ref[width : 2 * width, :]
        half = lo_ref.shape[0]
        block = half // 2 if half <= SPAN else SPAN // 2

        @pl.loop(0, half // block)
        def _(i):
            at = pl.ds(pl.multiple_of(i * block, block), block)
            table_lo[at, :] = mm(lo_ref[at, :], weights).astype(BF)
            table_hi[at, :] = mm(hi_ref[at, :], weights).astype(BF)

        group = group_rows(where_ref, lo_ref, hi_ref, rows_own).astype(BF)
        own[...] = mm(group, wmi_ref[:width, :])
        acc[...] = jnp.zeros_like(acc)

    flags = jnp.transpose(flags_ref[0])[:edges, :]
    place = flags[:, PLACE : PLACE + 1].astype(jnp.int32)
    pre_s[...] = gather_rows(place, (table_lo, table_hi)) + mm(
        edge_ref[...].reshape(edges, edge_width), wmi_ref[2 * width :, :]
    )
    for j in range(per):
        for r in range(0, dest_rows, ROWS):
            at = slice(j * dest_rows + r, j * dest_rows + r + ROWS)
            mask = flags[at, MASK : MASK + 1]
            cross = flags[at, CROSS : CROSS + 1]
            pre = pre_s[at, :] + own[r : r + ROWS, :] + cross * chain_ref[...]
            hidden, slope = gelu_pair(pre)
            slope = slope * mask
            slope_ref[j, r : r + ROWS, :] = slope.astype(BF)
            acc[r : r + ROWS, :width] += hidden.astype(BF).astype(F32) * mask
            acc[r : r + ROWS, width:] += slope

    @pl.when(step == pl.num_programs(0) - 1)
    def _():
        take_shares(where_ref, acc, (s0, s1, s2, s3))


def node_forward(
    norm_scale,
    s0, s1, s2, s3, node_ref, wmo_ref, gain1_ref, wfi_ref, wfo_ref, gain2_ref, weit_ref,
    total_ref, slopes_ref, first_ref, second_ref, low_ref, fslope_ref, fhidden_ref, out_ref, src_ref, eown_ref,
):
    width = node_ref.shape[1]
    sums = add_up((s0, s1, s2, s3))
    total = sums[:, :width].astype(BF)
    total_ref[...] = total
    slopes_ref[...] = sums[:, width:]
    first_in = node_ref[...].astype(F32) + mm(total, wmo_ref[...]) * (1.0 / norm_scale)
    first_ref[...] = first_in
    norm_one = norm_parts(first_in)[0] * gain1_ref[...]
    low = norm_one.astype(BF)
    for i in range(low_ref.shape[0]):
        low_ref[i] = low
    hidden, slope = gelu_pair(mm(low, wfi_ref[...]))
    hidden = hidden.astype(BF)
    fslope_ref[...] = slope
    fhidden_ref[...] = hidden
    second_in = norm_one + mm(hidden, wfo_ref[...])
    second_ref[...] = second_in
    node_out = (norm_parts(second_in)[0] * gain2_ref[...]).astype(BF)
    out_ref[...] = node_out
    eown_ref[...] = mm_nt(node_out, weit_ref[:, :width]).astype(BF)
    src = mm_nt(node_out, weit_ref[:, width : 2 * width]).astype(BF)
    for i in range(src_ref.shape[0]):
        src_ref[i] = src


def edge_network(
    where_ref, edge_ref, cot_ref, flags_ref, lo_ref, hi_ref, e0, e1, e2, e3, weit_ref, weo_ref, gain_ref,
    out_ref, dsum_ref, slo_ref, shi_ref, o0, o1, o2, o3, gin_ref, gout_ref, ggain_ref,
    own, dpre_s, hidden_s, delta_s, acc, own_acc,
):
    step = pl.program_id(0)
    per, dest_rows, edge_width = edge_ref.shape
    edges = per * dest_rows
    width = (weit_ref.shape[1] - edge_width) // 2
    weights_t = weit_ref[:, 2 * width :]

    @pl.when(step == 0)
    def _():
        put_shares(where_ref, (e0, e1, e2, e3), own)
        acc[...] = jnp.zeros_like(acc)
        own_acc[...] = jnp.zeros_like(own_acc)
        gin_ref[...] = jnp.zeros_like(gin_ref)
        gout_ref[...] = jnp.zeros_like(gout_ref)
        ggain_ref[...] = jnp.zeros_like(ggain_ref)

    flags = jnp.transpose(flags_ref[0])[:edges, :]
    place = flags[:, PLACE : PLACE + 1].astype(jnp.int32)
    edge_all = edge_ref[...].reshape(edges, edge_width)
    pre_all = gather_rows(place, (lo_ref, hi_ref)) + mm_nt(edge_all, weights_t)
    gain = gain_ref[...]
    for j in range(per):
        at = slice(j * dest_rows, (j + 1) * dest_rows)
        mask = flags[at, MASK : MASK + 1]
        hidden, slope = gelu_pair(pre_all[at, :] + own[...])
        hidden = (hidden * mask).astype(BF)
        hidden_s[at, :] = hidden
        n, r = norm_parts(edge_ref[j].astype(F32) + mm(hidden, weo_ref[...]))
        out_ref[j] = (n * gain).astype(BF)
        cot = cot_ref[j].astype(F32)
        cn = cot * n
        ggain_ref[...] += jnp.sum(cn.reshape(dest_rows // 8, 8, edge_width), axis=0)
        b = cot * gain
        dz = r * (b - jnp.mean(b, -1, keepdims=True) - n * jnp.mean(cn * gain, -1, keepdims=True))
        d_delta = (dz * mask).astype(BF)
        delta_s[at, :] = d_delta
        d_pre = slope * mm_nt(d_delta, weo_ref[...])
        d_low = d_pre.astype(BF)
        own_acc[...] += d_low.astype(F32)
        dpre_s[at, :] = d_low
        dsum_ref[j] = (dz + mm(d_low, weights_t)).astype(BF)
    gout_ref[...] += mm_tn(hidden_s[...], delta_s[...])
    gin_ref[...] += mm_tn(edge_all, dpre_s[...])
    place_row = flags_ref[0, PLACE : PLACE + 1, :edges].astype(jnp.int32)
    scatter_rows(place_row, dpre_s[...], acc)

    @pl.when(step == pl.num_programs(0) - 1)
    def _():
        half = slo_ref.shape[0]
        slo_ref[...] = acc[:half, :].astype(BF)
        shi_ref[...] = acc[half:, :].astype(BF)
        take_shares(where_ref, own_acc, (o0, o1, o2, o3))


def node_backward(
    norm_scale,
    where_ref, parts_ref, o0, o1, o2, o3, node_ref, node_cot_ref, out_ref, first_ref, second_ref, fslope_ref,
    total_ref, slopes_ref, weit_ref, wmi_ref, wfi_ref, wfo_ref, wmo_ref, gain1_ref, gain2_ref,
    d_ref, ngrad_ref, ggain_ref, keep_ref, send_ref,
    pay,
):
    width = out_ref.shape[1]
    edge_width = weit_ref.shape[0]
    from_sources = add_up(tuple(parts_ref.at[i] for i in range(parts_ref.shape[0]))).astype(BF)
    from_own = add_up((o0, o1, o2, o3)).astype(BF)
    d_updated = (
        node_cot_ref[...].astype(F32)
        + mm(from_own, weit_ref[:, :width])
        + mm(from_sources, weit_ref[:, width : 2 * width])
    )
    node_out = out_ref[...]
    n, r = norm_parts(second_ref[...])
    d_second, ggain2 = norm_back(n, r, gain2_ref[...], d_updated)
    dffn = d_second.astype(BF)
    d_ffn_pre = (fslope_ref[...] * mm_nt(dffn, wfo_ref[...])).astype(BF)
    d_norm_one = d_second + mm_nt(d_ffn_pre, wfi_ref[...])
    n, r = norm_parts(first_ref[...])
    d_first, ggain1 = norm_back(n, r, gain1_ref[...], d_norm_one)
    d_summed = (d_first * (1.0 / norm_scale)).astype(BF)
    d_hidden = mm_nt(d_summed, wmo_ref[...])
    d_ref[...] = d_hidden.astype(BF)
    own_sum = (d_hidden * slopes_ref[...]).astype(BF)
    ngrad_ref[...] = d_first + mm_nt(own_sum, wmi_ref[:width, :])
    ggain_ref[...] = jnp.concatenate([ggain1, ggain2, jnp.zeros((6, width), F32)], axis=0)
    parts = (
        mm_tn(total_ref[...], d_summed), mm_tn(node_ref[...], own_sum), mm_tn(from_own, node_out), mm_tn(from_sources, node_out)
    )
    at = 0
    for part in parts:
        pay[at : at + part.shape[0], :] = part.astype(BF)
        at += part.shape[0]
    pay[at:, :] = jnp.zeros((pay.shape[0] - at, width), BF)
    early = pay.shape[0] // 2 // keep_ref.shape[0]
    split_halves(where_ref, pay, early, keep_ref, send_ref)
    for i in range(keep_ref.shape[0]):
        keep_ref[i, early:, :] = dffn
        send_ref[i, early:, :] = jnp.zeros_like(dffn)


def split_halves(where_ref, pay, rows, keep_ref, send_ref):
    half = pay.shape[0] // 2
    at = pl.multiple_of(where_ref[2] * half, 16)
    shape = (keep_ref.shape[0], rows, pay.shape[1])
    keep_ref[:, :rows, :] = pay[pl.ds(at, half), :].reshape(shape)
    send_ref[:, :rows, :] = pay[pl.ds(half - at, half), :].reshape(shape)


def message_backward(
    where_ref, edge_ref, slope_ref, flags_ref, dsum_ref, d0, d1, d2, d3, wmi_ref, lo_ref, hi_ref, gain_ref, gain3_ref, gin_ref,
    gout_ref,
    keep_ref, send_ref, eg_ref,
    own, dpre_s, acc, gin, chain, pay,
):
    step = pl.program_id(0)
    width = wmi_ref.shape[1]
    per, dest_rows, edge_width = edge_ref.shape
    edges = per * dest_rows
    weights = wmi_ref[2 * width :, :]

    @pl.when(step == 0)
    def _():
        put_shares(where_ref, (d0, d1, d2, d3), own)
        acc[...] = jnp.zeros_like(acc)
        gin[...] = jnp.zeros_like(gin)
        chain[...] = jnp.zeros_like(chain)

    flags = jnp.transpose(flags_ref[0])[:edges, :]
    for j in range(per):
        for r in range(0, dest_rows, ROWS):
            at = slice(j * dest_rows + r, j * dest_rows + r + ROWS)
            d_low = (slope_ref[j, r : r + ROWS, :].astype(F32) * own[r : r + ROWS, :]).astype(BF)
            dpre_s[at, :] = d_low
            crossed = d_low.astype(F32) * flags[at, CROSS : CROSS + 1]
            chain[...] += jnp.sum(crossed.reshape(ROWS // 8, 8, width), axis=0)
    d_all = dpre_s[...]
    gin[...] += mm_tn(edge_ref[...].reshape(edges, edge_width), d_all)
    back = mm_nt(d_all, weights)
    for j in range(per):
        eg_ref[j] = dsum_ref[j].astype(F32) + back[j * dest_rows : (j + 1) * dest_rows, :]
    place_row = flags_ref[0, PLACE : PLACE + 1, :edges].astype(jnp.int32)
    scatter_rows(place_row, d_all, acc)

    @pl.when(step == pl.num_programs(0) - 1)
    def _():
        half = lo_ref.shape[0]
        chips = keep_ref.shape[0]
        rows = half // chips
        late = keep_ref.shape[1] - rows
        for chip in range(chips):
            keep_ref[chip, late:, :] = acc[chip * rows : (chip + 1) * rows, :].astype(BF)
            send_ref[chip, late:, :] = acc[half + chip * rows : half + (chip + 1) * rows, :].astype(BF)
        from_nodes = mm_tn(lo_ref[...], acc[:half, :].astype(BF)) + mm_tn(hi_ref[...], acc[half:, :].astype(BF))
        pay[:width, :] = from_nodes.astype(BF)
        at = width
        pay[at : at + edge_width, :] = gin[...].astype(BF)
        at += edge_width
        spare = jnp.zeros((edge_width, width - 2 * edge_width), F32)
        pay[at : at + edge_width, :] = jnp.concatenate([gin_ref[...], gout_ref[...], spare], axis=1).astype(BF)
        at += edge_width
        crossed = jnp.sum(chain[...], axis=0, keepdims=True)
        gain3 = jnp.concatenate([jnp.sum(gain3_ref[...], axis=0, keepdims=True), jnp.zeros((1, width - edge_width), F32)], axis=1)
        vecs = jnp.concatenate([gain_ref[:2, :], gain3, crossed, jnp.zeros((12, width), F32)], axis=0)
        pay[at : at + 16, :] = vecs.astype(BF)
        pay[at + 16 :, :] = jnp.zeros((pay.shape[0] - at - 16, width), BF)
        split_halves(where_ref, pay, late, keep_ref, send_ref)


def finish_nodes(late, early, first_ref, parts_ref, ngrad_ref, wmi_ref, out_ref, spread_ref):
    width = ngrad_ref.shape[1]
    chips = parts_ref.shape[0]
    total = add_up(tuple(parts_ref.at[i] for i in range(chips)))
    out_ref[...] = ngrad_ref[...] + mm_nt(total[late:, :].astype(BF), wmi_ref[width : 2 * width, :])
    mine = add_up(tuple(first_ref.at[i, :early, :] for i in range(chips))).astype(BF)
    other = total[:late, :].astype(BF)
    for i in range(spread_ref.shape[0]):
        spread_ref[i, :early, :] = mine
        spread_ref[i, early:, :] = other


def finish_weights(
    edge_width,
    where_ref, same_ref, other_ref,
    gmi_ref, gmo_ref, geit_ref, geo_ref, vecs_ref,
    early, late,
):
    width = gmi_ref.shape[1]
    plane, layers = same_ref.shape[:2]
    first = early.shape[0] // 2 // (plane * layers)
    second = late.shape[0] // 2 // (plane * layers)
    core = where_ref[2]
    for part, half in ((same_ref, core), (other_ref, 1 - core)):
        for p in range(plane):
            for z in range(layers):
                chip = half * plane * layers + z * plane + p
                early[pl.ds(pl.multiple_of(chip * first, 16), first), :] = part[p, z, :first, :]
                late[pl.ds(pl.multiple_of(chip * second, 16), second), :] = part[p, z, first:, :]
    gmo_ref[...] = early[:width, :].astype(F32)
    gmi_ref[:width, :] = early[width : 2 * width, :].astype(F32)
    gmi_ref[width:, :] = late[: width + edge_width, :].astype(F32)
    at = 2 * width
    geit_ref[:, :width] = early[at : at + edge_width, :].astype(F32)
    geit_ref[:, width : 2 * width] = early[at + edge_width : at + 2 * edge_width, :].astype(F32)
    at = width + edge_width
    small = late[at : at + edge_width, :].astype(F32)
    geit_ref[:, 2 * width :] = jnp.transpose(small[:, :edge_width])
    geo_ref[...] = small[:, edge_width : 2 * edge_width]
    vecs_ref[...] = late[at + edge_width : at + edge_width + 16, :].astype(F32)[:8, :]


def ffn_grads(llo_ref, lhi_ref, dlo_ref, dhi_ref, wfi_ref, wfo_ref, gfi_ref, gfo_ref):
    block = min(llo_ref.shape[0], SPAN // 2)
    gfi = gfo = None
    for low_ref, dffn_ref in ((llo_ref, dlo_ref), (lhi_ref, dhi_ref)):
        for start in range(0, low_ref.shape[0], block):
            low = low_ref[start : start + block, :]
            dffn = dffn_ref[start : start + block, :]
            hidden, slope = gelu_pair(mm(low, wfi_ref[...]))
            part = mm_tn(hidden.astype(BF), dffn)
            gfo = part if gfo is None else gfo + part
            d_pre = (slope * mm_nt(dffn, wfo_ref[...])).astype(BF)
            part = mm_tn(low, d_pre)
            gfi = part if gfi is None else gfi + part
    gfo_ref[...] = gfo
    gfi_ref[...] = gfi


def whole(shape):
    return pl.BlockSpec(tuple(shape), lambda *_: (0,) * len(shape))


def per_step(count, shape):
    return pl.BlockSpec((count,) + tuple(shape[1:]), lambda i: (i,) + (0,) * (len(shape) - 1))


SCALARS = pl.BlockSpec(memory_space=pltpu.SMEM)


def params(limit=56):
    return pltpu.CompilerParams(vmem_limit_bytes=limit << 20, dimension_semantics=("arbitrary",))


def sds(shape, dtype):
    return jax.ShapeDtypeStruct(tuple(shape), dtype)


def swap(x, axis):
    return lax.ppermute(x, axis, [(0, 1), (1, 0)])


def gather_spread(spread):
    same = lax.all_to_all(spread, CHIPS, 0, 0).reshape(-1, spread.shape[2])
    return same, swap(same, "c")


def scatter_halves(lo, hi):
    got = swap(hi, "c")
    both = (lo.astype(F32) + got.astype(F32)).astype(lo.dtype)
    return lax.all_to_all(both.reshape(lax.axis_size(CHIPS), -1, lo.shape[1]), CHIPS, 0, 0)


def send_shares(pieces):
    shares = len(pieces)
    got = [pieces[0]]
    for q in range(1, shares):
        got.append(lax.ppermute(pieces[q], ("y", "c"), [(s, (s + q) % shares) for s in range(shares)]))
    return got


def chip_sum(keep, send):
    return (keep.astype(F32) + swap(send, "c").astype(F32)).astype(keep.dtype)


def to_owners(both):
    return lax.all_to_all(both, CHIPS, 0, 0)


def cost(micros):
    return pl.CostEstimate(flops=int(micros * 1e9), bytes_accessed=int(micros * 1e6), transcendentals=0)


def per_device(
    node_in, edge_in, neighbors, chain_ids, residue_mask, w_msg_in, chain_vec, w_msg_out, gain_one,
    w_ffn_in, w_ffn_out, gain_two, w_edge_in, w_edge_out, gain_three, node_cot, edge_cot,
):
    dest_rows, width_k, edge_width = edge_in.shape
    rows_own, width = node_in.shape
    hidden_width = w_ffn_in.shape[1]
    nodes = chain_ids.shape[0]
    half = nodes // 2
    chips = lax.axis_size(CHIPS)
    per = 3 if width_k % 3 == 0 else 1
    steps = width_k // per
    count = per * dest_rows
    lanes = count + (-count) % 128
    shares = dest_rows // rows_own
    norm_scale = math.sqrt(width_k * shares)
    me_core = lax.axis_index("c")
    share = lax.axis_index("y") * 2 + me_core
    group = lax.axis_index("z") * 2 + lax.axis_index("x")
    z, x, y = (lax.axis_index(axis) for axis in CHIPS)
    where = jnp.stack([share, group, me_core, z, x, y]).astype(jnp.int32)

    edges = edge_in.transpose(1, 0, 2)
    cots = edge_cot.transpose(1, 0, 2)
    lo, hi = gather_spread(jnp.broadcast_to(node_in[None], (chips,) + node_in.shape))

    first_row = group * dest_rows
    source = neighbors.T
    dest_chain = lax.dynamic_slice_in_dim(chain_ids, first_row, dest_rows)
    dest_mask = lax.dynamic_slice_in_dim(residue_mask, first_row, dest_rows)
    lower = jnp.sum((chain_ids[None, :] < dest_chain[:, None]).astype(jnp.int32), axis=1)
    upper = jnp.sum((chain_ids[None, :] <= dest_chain[:, None]).astype(jnp.int32), axis=1)
    bits = jnp.sum(residue_mask.reshape(nodes // 16, 16) << jnp.arange(16, dtype=jnp.int32)[None, :], axis=1)
    pick = (source >> 4)[:, :, None] == jnp.arange(nodes // 16, dtype=jnp.int32)[None, None, :]
    word = jnp.sum(jnp.where(pick, bits[None, None, :], 0), axis=2)
    present = (word >> (source & 15)) & 1
    pair_mask = (dest_mask[None, :] * present).astype(F32)
    cross = ((source < lower[None, :]) | (source >= upper[None, :])).astype(F32)
    block = source // rows_own
    place = ((block % 2) ^ me_core) * half + (block // 2) * rows_own + source % rows_own
    table = jnp.stack([place.astype(F32), pair_mask, cross]).reshape(3, steps, count).transpose(1, 0, 2)
    flags = jnp.pad(table, ((0, 0), (0, 5), (0, lanes - count)))

    row = lambda v: v.reshape(1, -1)
    wei_t = w_edge_in.T
    edge_spec = per_step(per, edges.shape)
    flag_spec = per_step(1, flags.shape)
    wide_spec = [whole((rows_own, 2 * width))] * shares
    wide_out = [sds((rows_own, 2 * width), BF)] * shares
    share_spec = [whole((rows_own, width))] * shares

    f_slope, *sums = pl.pallas_call(
        functools.partial(message_forward, rows_own),
        grid=(steps,),
        in_specs=[
            SCALARS, edge_spec, flag_spec, whole((half, width)), whole((half, width)), whole(w_msg_in.shape), whole((1, width)),
        ],
        out_specs=[per_step(per, (width_k, dest_rows, width))] + wide_spec,
        out_shape=[sds((width_k, dest_rows, width), BF)] + wide_out,
        scratch_shapes=[
            pltpu.VMEM((half, width), BF), pltpu.VMEM((half, width), BF), pltpu.VMEM((dest_rows, width), F32),
            pltpu.VMEM((dest_rows, 2 * width), F32), pltpu.VMEM((count, width), F32),
        ],
        compiler_params=params(),
        name="message_forward",
    )(where, edges, flags, lo, hi, w_msg_in, row(chain_vec))
    sums = send_shares(sums)

    total, slopes, first_in, second_in, low, ffn_slope, ffn_hidden, node_out, e_spread, e_own = pl.pallas_call(
        functools.partial(node_forward, norm_scale),
        out_shape=[
            sds((rows_own, width), BF), sds((rows_own, width), F32), sds((rows_own, width), F32), sds((rows_own, width), F32),
            sds((chips, rows_own, width), BF), sds((rows_own, hidden_width), F32), sds((rows_own, hidden_width), BF), sds((rows_own, width), BF),
            sds((chips, rows_own, edge_width), BF), sds((rows_own, edge_width), BF),
        ],
        compiler_params=pltpu.CompilerParams(vmem_limit_bytes=56 << 20),
        name="node_forward",
    )(*sums, node_in, w_msg_out, row(gain_one), w_ffn_in, w_ffn_out, row(gain_two), wei_t)

    e_owns = send_shares([e_own] * shares)
    e_lo = lax.all_to_all(e_spread, CHIPS, 0, 0).reshape(-1, edge_width)
    e_lo, *e_owns = lax.optimization_barrier((e_lo, *e_owns))
    e_hi = swap(e_lo, "c")
    e_lo, low = lax.optimization_barrier((e_lo, low))
    low_lo = lax.all_to_all(low, CHIPS, 0, 0).reshape(half, width)

    edge_new, d_sum, e_slo, e_shi, *rest = pl.pallas_call(
        edge_network,
        grid=(steps,),
        in_specs=[SCALARS, edge_spec, edge_spec, flag_spec, whole((half, edge_width)), whole((half, edge_width))]
        + [whole((rows_own, edge_width))] * shares
        + [whole(wei_t.shape), whole(w_edge_out.shape), whole((1, edge_width))],
        out_specs=[edge_spec, edge_spec, whole((half, edge_width)), whole((half, edge_width))]
        + [whole((rows_own, edge_width))] * shares
        + [whole((edge_width, edge_width)), whole((edge_width, edge_width)), whole((8, edge_width))],
        out_shape=[sds(edges.shape, BF), sds(edges.shape, BF), sds((half, edge_width), BF), sds((half, edge_width), BF)]
        + [sds((rows_own, edge_width), BF)] * shares
        + [sds((edge_width, edge_width), F32), sds((edge_width, edge_width), F32), sds((8, edge_width), F32)],
        scratch_shapes=[
            pltpu.VMEM((dest_rows, edge_width), F32), pltpu.VMEM((count, edge_width), BF), pltpu.VMEM((count, edge_width), BF),
            pltpu.VMEM((count, edge_width), BF), pltpu.VMEM((nodes, edge_width), F32), pltpu.VMEM((dest_rows, edge_width), F32),
        ],
        compiler_params=params(),
        cost_estimate=cost(22),
        name="edge_network",
    )(where, edges, cots, flags, e_lo, e_hi, *e_owns, wei_t, w_edge_out, row(gain_three))
    g_in, g_out, g_gain3 = rest[shares:]
    e_slo, e_shi, low_lo, *e_sums = lax.optimization_barrier((e_slo, e_shi, low_lo, *rest[:shares]))
    low_hi = swap(low_lo, "c")
    e_sums = send_shares(e_sums)
    e_parts = scatter_halves(e_slo, e_shi)

    up = lambda rows: rows + (-rows) % (32 * chips)
    pay_early = up(2 * width + 2 * edge_width)
    pay_late = up(width + 2 * edge_width + 16)
    early_rows, late_rows = pay_early // (2 * chips), pay_late // (2 * chips)
    sent = (chips, early_rows + rows_own, width)
    d_hidden, n_grad, g_gains, keep, send = pl.pallas_call(
        functools.partial(node_backward, norm_scale),
        in_specs=[SCALARS] + [pl.BlockSpec(memory_space=pltpu.VMEM)] * 20,
        out_shape=[
            sds((rows_own, width), BF), sds((rows_own, width), F32), sds((8, width), F32), sds(sent, BF), sds(sent, BF),
        ],
        scratch_shapes=[pltpu.VMEM((pay_early, width), BF)],
        compiler_params=pltpu.CompilerParams(vmem_limit_bytes=56 << 20),
        name="node_backward",
    )(
        where, e_parts, *e_sums, node_in, node_cot, node_out, first_in, second_in, ffn_slope, total, slopes,
        wei_t, w_msg_in, w_ffn_in, w_ffn_out, w_msg_out, row(gain_one), row(gain_two),
    )
    d_hiddens = send_shares([d_hidden] * shares)
    early, *d_hiddens = lax.optimization_barrier((chip_sum(keep, send), *d_hiddens))
    early_parts = to_owners(early)

    sent = (chips, late_rows + rows_own, width)
    keep, send, e_grad = pl.pallas_call(
        message_backward,
        grid=(steps,),
        in_specs=[SCALARS, edge_spec, per_step(per, (width_k, dest_rows, width)), flag_spec, edge_spec]
        + share_spec + [whole(w_msg_in.shape), whole((half, width)), whole((half, width)), whole((8, width))]
        + [whole((8, edge_width)), whole((edge_width, edge_width)), whole((edge_width, edge_width))],
        out_specs=[whole(sent), whole(sent), edge_spec],
        out_shape=[sds(sent, BF), sds(sent, BF), sds(edges.shape, F32)],
        scratch_shapes=[
            pltpu.VMEM((dest_rows, width), F32), pltpu.VMEM((count, width), BF), pltpu.VMEM((nodes, width), F32),
            pltpu.VMEM((edge_width, width), F32), pltpu.VMEM((8, width), F32), pltpu.VMEM((pay_late, width), BF),
        ],
        compiler_params=params(),
        cost_estimate=cost(13),
        name="message_backward",
    )(where, edges, f_slope, flags, d_sum, *d_hiddens, w_msg_in, lo, hi, g_gains, g_gain3, g_in, g_out)
    late, early_parts = lax.optimization_barrier((chip_sum(keep, send), early_parts))
    late_parts = to_owners(late)
    dffn_lo = early_parts[:, early_rows:, :].reshape(half, width)
    dffn_hi = swap(dffn_lo, "c")

    tile = 256
    g_ffn_in, g_ffn_out = pl.pallas_call(
        ffn_grads,
        grid=(hidden_width // tile,),
        in_specs=[whole((half, width))] * 4
        + [pl.BlockSpec((width, tile), lambda i: (0, i)), pl.BlockSpec((tile, width), lambda i: (i, 0))],
        out_specs=[pl.BlockSpec((width, tile), lambda i: (0, i)), pl.BlockSpec((tile, width), lambda i: (i, 0))],
        out_shape=[sds(w_ffn_in.shape, F32), sds(w_ffn_out.shape, F32)],
        compiler_params=params(),
        cost_estimate=cost(18),
        name="ffn_grads",
    )(low_lo, low_hi, dffn_lo, dffn_hi, w_ffn_in, w_ffn_out)
    late_parts, g_ffn_in, g_ffn_out = lax.optimization_barrier((late_parts, g_ffn_in, g_ffn_out))

    layers = lax.axis_size("z")
    plane = chips // layers
    node_grad, spread = pl.pallas_call(
        functools.partial(finish_nodes, late_rows, early_rows),
        out_shape=[sds((rows_own, width), F32), sds((layers, early_rows + late_rows, width), BF)],
        compiler_params=pltpu.CompilerParams(vmem_limit_bytes=40 << 20),
        name="finish_nodes",
    )(early_parts, late_parts, n_grad, w_msg_in)
    layer = lax.all_to_all(spread, "z", 0, 0)
    same = lax.all_to_all(jnp.broadcast_to(layer[None], (plane,) + layer.shape), ("x", "y"), 0, 0)
    other = swap(same, "c")
    g_msg_in, g_msg_out, g_edge_t, g_edge_out, vecs = pl.pallas_call(
        functools.partial(finish_weights, edge_width),
        in_specs=[SCALARS] + [pl.BlockSpec(memory_space=pltpu.VMEM)] * 2,
        out_shape=[
            sds(w_msg_in.shape, F32), sds((width, width), F32), sds(wei_t.shape, F32), sds((edge_width, edge_width), F32),
            sds((8, width), F32),
        ],
        scratch_shapes=[pltpu.VMEM((pay_early, width), BF), pltpu.VMEM((pay_late, width), BF)],
        compiler_params=pltpu.CompilerParams(vmem_limit_bytes=56 << 20),
        name="finish_weights",
    )(where, same, other)
    return (
        node_out, edge_new.transpose(1, 0, 2), node_grad, e_grad.transpose(1, 0, 2), g_msg_in, vecs[3], g_msg_out,
        vecs[0], g_ffn_in, g_ffn_out, vecs[1], g_edge_t.T, g_edge_out, vecs[2, :edge_width],
    )


def solution(mesh):
    groups, shares = mesh.shape["res"], mesh.shape["edge"]
    fine = Mesh(mesh.devices.reshape(groups // 2, 2, shares // 2, 2), ("z", "x", "y", "c"))
    rows = P(("z", "x", "y", "c"), None)
    edges = P(("z", "x"), ("y", "c"), None)
    in_specs = (rows, edges, P(("z", "x"), ("y", "c"))) + (P(),) * 12 + (rows, edges)
    out_specs = (rows, edges, rows, edges) + (P(),) * 10
    return jax.shard_map(per_device, mesh=fine, in_specs=in_specs, out_specs=out_specs, check_vma=False)
```

```python
import functools
import math

import jax
import jax.numpy as jnp
from jax import lax
from jax.experimental import pallas as pl
from jax.experimental.pallas import tpu as pltpu
from jax.sharding import Mesh, PartitionSpec as P

EPS = 1e-05
CHIPS = ("z", "x", "y")
BF = jnp.bfloat16
F32 = jnp.float32
ROWS = 80
PIECE = 800
PINNED = 3 << 20
SPAN = 1280
RSQRT2 = math.sqrt(0.5)
INV_SQRT_2PI = 1.0 / math.sqrt(2.0 * math.pi)
PLACE, MASK, CROSS = 0, 1, 2


def mm(a, b):
    return jnp.dot(a, b, preferred_element_type=F32)


def mm_nt(a, b):
    return lax.dot_general(a, b, (((1,), (1,)), ((), ())), preferred_element_type=F32)


def mm_tn(a, b):
    return lax.dot_general(a, b, (((0,), (0,)), ((), ())), preferred_element_type=F32)


def gelu_pair(v):
    cdf = 0.5 * (1.0 + lax.erf(v * RSQRT2))
    pdf = INV_SQRT_2PI * jnp.exp(-0.5 * v * v)
    return v * cdf, cdf + v * pdf


def norm_parts(z):
    centre = z - jnp.mean(z, axis=-1, keepdims=True)
    r = lax.rsqrt(jnp.mean(centre * centre, axis=-1, keepdims=True) + EPS)
    return centre * r, r


def norm_back(n, r, gain, cot):
    b = cot * gain
    dz = r * (b - jnp.mean(b, -1, keepdims=True) - n * jnp.mean(b * n, -1, keepdims=True))
    return dz, jnp.sum(cot * n, axis=0, keepdims=True)


def gather_rows(place, halves):
    total = None
    for h, table in enumerate(halves):
        count = table.shape[0]
        block = min(count, SPAN)
        for start in range(0, count, block):
            lane = lax.broadcasted_iota(jnp.int32, (place.shape[0], block), 1) + (h * count + start)
            hot = jnp.where(lane == place, 1.0, 0.0).astype(BF)
            part = mm(hot, table[start : start + block, :])
            total = part if total is None else total + part
    return total


def scatter_rows(place_row, rows, acc):
    nodes = acc.shape[0]
    block = min(nodes, SPAN // 2)

    @pl.loop(0, nodes // block)
    def _(i):
        start = pl.multiple_of(i * block, block)
        row = lax.broadcasted_iota(jnp.int32, (block, place_row.shape[1]), 0) + start
        hot = jnp.where(row == place_row, 1.0, 0.0).astype(BF)
        acc[pl.ds(start, block), :] += mm(hot, rows)


def group_rows(where_ref, lo_ref, hi_ref, rows_own):
    group, core = where_ref[1], where_ref[2]
    start = pl.multiple_of(group * 2 * rows_own, 2 * rows_own)
    same = lo_ref[pl.ds(start, 2 * rows_own), :].astype(F32)
    other = hi_ref[pl.ds(start, 2 * rows_own), :].astype(F32)
    swapped = core == 1
    first = jnp.where(swapped, other, same)
    second = jnp.where(swapped, same, other)
    rows = [first[:rows_own], second[:rows_own], first[rows_own:], second[rows_own:]]
    return jnp.concatenate(rows, axis=0)


def put_shares(where_ref, refs, out):
    rows = refs[0].shape[0]
    shares = len(refs)
    for q, ref in enumerate(refs):
        at = lax.rem(where_ref[0] + shares - q, shares) * rows
        out[pl.ds(pl.multiple_of(at, 8), rows), :] = ref[...].astype(out.dtype)


def take_shares(where_ref, acc, refs):
    rows = refs[0].shape[0]
    shares = len(refs)
    for q, ref in enumerate(refs):
        at = lax.rem(where_ref[0] + q, shares) * rows
        ref[...] = acc[pl.ds(pl.multiple_of(at, 8), rows), :].astype(ref.dtype)


def add_up(refs):
    total = refs[0][...].astype(F32)
    for ref in refs[1:]:
        total += ref[...].astype(F32)
    return total


def message_forward(
    rows_own,
    where_ref, edge_ref, flags_ref, lo_ref, hi_ref, wmi_ref, chain_ref,
    slope_ref, s0, s1, s2, s3,
    table_lo, table_hi, own, acc, pre_s,
):
    step = pl.program_id(0)
    width = wmi_ref.shape[1]
    per, dest_rows, edge_width = edge_ref.shape
    edges = per * dest_rows

    @pl.when(step == 0)
    def _():
        weights = wmi_ref[width : 2 * width, :]
        half = lo_ref.shape[0]
        block = half // 2 if half <= SPAN else SPAN // 2

        @pl.loop(0, half // block)
        def _(i):
            at = pl.ds(pl.multiple_of(i * block, block), block)
            table_lo[at, :] = mm(lo_ref[at, :], weights).astype(BF)
            table_hi[at, :] = mm(hi_ref[at, :], weights).astype(BF)

        group = group_rows(where_ref, lo_ref, hi_ref, rows_own).astype(BF)
        own[...] = mm(group, wmi_ref[:width, :])
        acc[...] = jnp.zeros_like(acc)

    flags = jnp.transpose(flags_ref[0])[:edges, :]
    place = flags[:, PLACE : PLACE + 1].astype(jnp.int32)
    pre_s[...] = gather_rows(place, (table_lo, table_hi)) + mm(
        edge_ref[...].reshape(edges, edge_width), wmi_ref[2 * width :, :]
    )
    for j in range(per):
        for r in range(0, dest_rows, ROWS):
            at = slice(j * dest_rows + r, j * dest_rows + r + ROWS)
            mask = flags[at, MASK : MASK + 1]
            cross = flags[at, CROSS : CROSS + 1]
            pre = pre_s[at, :] + own[r : r + ROWS, :] + cross * chain_ref[...]
            hidden, slope = gelu_pair(pre)
            slope = slope * mask
            slope_ref[j, r : r + ROWS, :] = slope.astype(BF)
            acc[r : r + ROWS, :width] += hidden.astype(BF).astype(F32) * mask
            acc[r : r + ROWS, width:] += slope

    @pl.when(step == pl.num_programs(0) - 1)
    def _():
        take_shares(where_ref, acc, (s0, s1, s2, s3))


def start_copies(sources, targets, sems):
    copies = [pltpu.make_async_copy(s, t, sems.at[i]) for i, (s, t) in enumerate(zip(sources, targets))]
    for copy in copies:
        copy.start()
    return copies


def node_forward(
    norm_scale,
    s0, s1, s2, s3, node_ref, wmo_ref, gain1_ref, wfi_any, wfo_any, gain2_ref, weit_any,
    total_ref, slopes_ref, first_ref, second_ref, low_ref, fslope_ref, fhidden_ref, out_ref, src_ref, eown_ref,
    wfi_ref, wfo_ref, weit_ref, sems,
):
    copies = start_copies((wfi_any, wfo_any, weit_any), (wfi_ref, wfo_ref, weit_ref), sems)
    width = node_ref.shape[1]
    sums = add_up((s0, s1, s2, s3))
    total = sums[:, :width].astype(BF)
    total_ref[...] = total
    slopes_ref[...] = sums[:, width:]
    first_in = node_ref[...].astype(F32) + mm(total, wmo_ref[...]) * (1.0 / norm_scale)
    first_ref[...] = first_in
    norm_one = norm_parts(first_in)[0] * gain1_ref[...]
    low = norm_one.astype(BF)
    for i in range(low_ref.shape[0]):
        low_ref[i] = low
    copies[0].wait()
    hidden, slope = gelu_pair(mm(low, wfi_ref[...]))
    hidden = hidden.astype(BF)
    fslope_ref[...] = slope
    fhidden_ref[...] = hidden
    copies[1].wait()
    second_in = norm_one + mm(hidden, wfo_ref[...])
    second_ref[...] = second_in
    node_out = (norm_parts(second_in)[0] * gain2_ref[...]).astype(BF)
    out_ref[...] = node_out
    copies[2].wait()
    eown_ref[...] = mm_nt(node_out, weit_ref[:, :width]).astype(BF)
    src = mm_nt(node_out, weit_ref[:, width : 2 * width]).astype(BF)
    for i in range(src_ref.shape[0]):
        src_ref[i] = src


def edge_network(
    where_ref, edge_ref, cot_ref, flags_ref, lo_ref, hi_ref, e0, e1, e2, e3, weit_ref, weo_ref, gain_ref,
    out_ref, dsum_ref, slo_ref, shi_ref, o0, o1, o2, o3, gin_ref, gout_ref, ggain_ref,
    own, dpre_s, hidden_s, delta_s, out_s, dsum_s, acc, own_acc,
):
    step = pl.program_id(0)
    per, dest_rows, edge_width = edge_ref.shape
    edges = per * dest_rows
    width = (weit_ref.shape[1] - edge_width) // 2
    weights_t = weit_ref[:, 2 * width :]

    @pl.when(step == 0)
    def _():
        put_shares(where_ref, (e0, e1, e2, e3), own)
        for j in range(1, per):
            own[j * dest_rows : (j + 1) * dest_rows, :] = own[:dest_rows, :]
        acc[...] = jnp.zeros_like(acc)
        own_acc[...] = jnp.zeros_like(own_acc)
        gin_ref[...] = jnp.zeros_like(gin_ref)
        gout_ref[...] = jnp.zeros_like(gout_ref)
        ggain_ref[...] = jnp.zeros_like(ggain_ref)

    flags = jnp.transpose(flags_ref[0])[:edges, :]
    place = flags[:, PLACE : PLACE + 1].astype(jnp.int32)
    edge_all = edge_ref[...].reshape(edges, edge_width)
    cot_all = cot_ref[...].reshape(edges, edge_width)
    pre_all = gather_rows(place, (lo_ref, hi_ref)) + mm_nt(edge_all, weights_t) + own[...]
    gain = gain_ref[...]
    piece = PIECE if edges % PIECE == 0 else edges
    for start in range(0, edges, piece):
        at = slice(start, start + piece)
        mask = flags[at, MASK : MASK + 1]
        hidden, slope = gelu_pair(pre_all[at, :])
        hidden = (hidden * mask).astype(BF)
        hidden_s[at, :] = hidden
        n, r = norm_parts(edge_all[at, :].astype(F32) + mm(hidden, weo_ref[...]))
        out_s[at, :] = (n * gain).astype(BF)
        cot = cot_all[at, :].astype(F32)
        cn = cot * n
        ggain_ref[...] += jnp.sum(cn.reshape(piece // 8, 8, edge_width), axis=0)
        b = cot * gain
        dz = r * (b - jnp.mean(b, -1, keepdims=True) - n * jnp.mean(cn * gain, -1, keepdims=True))
        d_delta = (dz * mask).astype(BF)
        delta_s[at, :] = d_delta
        d_low = (slope * mm_nt(d_delta, weo_ref[...])).astype(BF)
        dpre_s[at, :] = d_low
        dsum_s[at, :] = (dz + mm(d_low, weights_t)).astype(BF)
    out_ref[...] = out_s[...].reshape(out_ref.shape)
    dsum_ref[...] = dsum_s[...].reshape(dsum_ref.shape)
    for j in range(per):
        own_acc[...] += dpre_s[j * dest_rows : (j + 1) * dest_rows, :].astype(F32)
    gout_ref[...] += mm_tn(hidden_s[...], delta_s[...])
    gin_ref[...] += mm_tn(edge_all, dpre_s[...])
    place_row = flags_ref[0, PLACE : PLACE + 1, :edges].astype(jnp.int32)
    scatter_rows(place_row, dpre_s[...], acc)

    @pl.when(step == pl.num_programs(0) - 1)
    def _():
        half = slo_ref.shape[0]
        slo_ref[...] = acc[:half, :].astype(BF)
        shi_ref[...] = acc[half:, :].astype(BF)
        take_shares(where_ref, own_acc, (o0, o1, o2, o3))


def node_backward(
    norm_scale,
    where_ref, parts_ref, o0, o1, o2, o3, node_ref, node_cot_ref, out_ref, first_ref, second_ref, fslope_ref,
    total_ref, slopes_ref, weit_ref, wmi_any, wfi_any, wfo_any, wmo_any, gain1_ref, gain2_ref,
    d_ref, ngrad_ref, ggain_ref, keep_ref, send_ref,
    pay, wfo_ref, wfi_ref, wmo_ref, wmi_ref, sems,
):
    width = out_ref.shape[1]
    own_rows = wmi_any.at[pl.ds(0, width), :]
    copies = start_copies((wfo_any, wfi_any, wmo_any, own_rows), (wfo_ref, wfi_ref, wmo_ref, wmi_ref), sems)
    from_sources = add_up(tuple(parts_ref.at[i] for i in range(parts_ref.shape[0]))).astype(BF)
    from_own = add_up((o0, o1, o2, o3)).astype(BF)
    d_updated = (
        node_cot_ref[...].astype(F32)
        + mm(from_own, weit_ref[:, :width])
        + mm(from_sources, weit_ref[:, width : 2 * width])
    )
    node_out = out_ref[...]
    n, r = norm_parts(second_ref[...])
    d_second, ggain2 = norm_back(n, r, gain2_ref[...], d_updated)
    dffn = d_second.astype(BF)
    copies[0].wait()
    d_ffn_pre = (fslope_ref[...] * mm_nt(dffn, wfo_ref[...])).astype(BF)
    copies[1].wait()
    d_norm_one = d_second + mm_nt(d_ffn_pre, wfi_ref[...])
    n, r = norm_parts(first_ref[...])
    d_first, ggain1 = norm_back(n, r, gain1_ref[...], d_norm_one)
    d_summed = (d_first * (1.0 / norm_scale)).astype(BF)
    copies[2].wait()
    d_hidden = mm_nt(d_summed, wmo_ref[...])
    d_ref[...] = d_hidden.astype(BF)
    own_sum = (d_hidden * slopes_ref[...]).astype(BF)
    copies[3].wait()
    ngrad_ref[...] = d_first + mm_nt(own_sum, wmi_ref[...])
    ggain_ref[...] = jnp.concatenate([ggain1, ggain2, jnp.zeros((6, width), F32)], axis=0)
    parts = (
        mm_tn(total_ref[...], d_summed), mm_tn(node_ref[...], own_sum), mm_tn(from_own, node_out), mm_tn(from_sources, node_out)
    )
    at = 0
    for part in parts:
        pay[at : at + part.shape[0], :] = part.astype(BF)
        at += part.shape[0]
    pay[at:, :] = jnp.zeros((pay.shape[0] - at, width), BF)
    early = pay.shape[0] // 2 // keep_ref.shape[0]
    split_halves(where_ref, pay, early, keep_ref, send_ref)
    for i in range(keep_ref.shape[0]):
        keep_ref[i, early:, :] = dffn


def split_halves(where_ref, pay, rows, keep_ref, send_ref):
    half = pay.shape[0] // 2
    at = pl.multiple_of(where_ref[2] * half, 16)
    shape = (keep_ref.shape[0], rows, pay.shape[1])
    keep_ref[:, :rows, :] = pay[pl.ds(at, half), :].reshape(shape)
    send_ref[:, :rows, :] = pay[pl.ds(half - at, half), :].reshape(shape)


def message_backward(
    where_ref, edge_ref, slope_ref, flags_ref, dsum_ref, d0, d1, d2, d3, wmi_any, lo_any, hi_any, gain_ref, gain3_ref, gin_ref,
    gout_ref,
    keep_ref, send_ref, eg_ref,
    own, dpre_s, acc, gin, chain, pay, lo_ref, hi_ref, wme_ref, sems,
):
    step = pl.program_id(0)
    width = wme_ref.shape[1]
    per, dest_rows, edge_width = edge_ref.shape
    edges = per * dest_rows
    copy_w = pltpu.make_async_copy(wmi_any.at[pl.ds(2 * width, edge_width), :], wme_ref, sems.at[2])
    copy_lo = pltpu.make_async_copy(lo_any, lo_ref, sems.at[0])
    copy_hi = pltpu.make_async_copy(hi_any, hi_ref, sems.at[1])

    @pl.when(step == 0)
    def _():
        copy_w.start()
        copy_lo.start()
        copy_hi.start()
        put_shares(where_ref, (d0, d1, d2, d3), own)
        acc[...] = jnp.zeros_like(acc)
        gin[...] = jnp.zeros_like(gin)
        chain[...] = jnp.zeros_like(chain)

    flags = jnp.transpose(flags_ref[0])[:edges, :]
    for j in range(per):
        for r in range(0, dest_rows, ROWS):
            at = slice(j * dest_rows + r, j * dest_rows + r + ROWS)
            d_low = (slope_ref[j, r : r + ROWS, :].astype(F32) * own[r : r + ROWS, :]).astype(BF)
            dpre_s[at, :] = d_low
            crossed = d_low.astype(F32) * flags[at, CROSS : CROSS + 1]
            chain[...] += jnp.sum(crossed.reshape(ROWS // 8, 8, width), axis=0)
    @pl.when(step == 0)
    def _():
        copy_w.wait()

    d_all = dpre_s[...]
    gin[...] += mm_tn(edge_ref[...].reshape(edges, edge_width), d_all)
    back = mm_nt(d_all, wme_ref[...])
    for j in range(per):
        eg_ref[j] = dsum_ref[j].astype(F32) + back[j * dest_rows : (j + 1) * dest_rows, :]
    place_row = flags_ref[0, PLACE : PLACE + 1, :edges].astype(jnp.int32)
    scatter_rows(place_row, d_all, acc)

    @pl.when(step == pl.num_programs(0) - 1)
    def _():
        half = lo_ref.shape[0]
        chips = keep_ref.shape[0]
        rows = half // chips
        late = keep_ref.shape[1] - rows
        for chip in range(chips):
            keep_ref[chip, late:, :] = acc[chip * rows : (chip + 1) * rows, :].astype(BF)
            send_ref[chip, late:, :] = acc[half + chip * rows : half + (chip + 1) * rows, :].astype(BF)
        copy_lo.wait()
        copy_hi.wait()
        from_nodes = mm_tn(lo_ref[...], acc[:half, :].astype(BF)) + mm_tn(hi_ref[...], acc[half:, :].astype(BF))
        pay[:width, :] = from_nodes.astype(BF)
        at = width
        pay[at : at + edge_width, :] = gin[...].astype(BF)
        at += edge_width
        spare = jnp.zeros((edge_width, width - 2 * edge_width), F32)
        pay[at : at + edge_width, :] = jnp.concatenate([gin_ref[...], gout_ref[...], spare], axis=1).astype(BF)
        at += edge_width
        crossed = jnp.sum(chain[...], axis=0, keepdims=True)
        gain3 = jnp.concatenate([jnp.sum(gain3_ref[...], axis=0, keepdims=True), jnp.zeros((1, width - edge_width), F32)], axis=1)
        vecs = jnp.concatenate([gain_ref[:2, :], gain3, crossed, jnp.zeros((12, width), F32)], axis=0)
        pay[at : at + 16, :] = vecs.astype(BF)
        pay[at + 16 :, :] = jnp.zeros((pay.shape[0] - at - 16, width), BF)
        split_halves(where_ref, pay, late, keep_ref, send_ref)


def finish_nodes(late, early, first_ref, parts_ref, ngrad_ref, wmi_ref, out_ref, spread_ref):
    width = ngrad_ref.shape[1]
    chips = parts_ref.shape[0]
    total = add_up(tuple(parts_ref.at[i] for i in range(chips)))
    out_ref[...] = ngrad_ref[...] + mm_nt(total[late:, :].astype(BF), wmi_ref[...])
    mine = add_up(tuple(first_ref.at[i, :early, :] for i in range(chips))).astype(BF)
    other = total[:late, :].astype(BF)
    for i in range(spread_ref.shape[0]):
        spread_ref[i, :early, :] = mine
        spread_ref[i, early:, :] = other


def finish_weights(
    edge_width,
    where_ref, same_ref, other_ref,
    gmi_ref, gmo_ref, geit_ref, geo_ref, g1_ref, g2_ref, g3_ref, gchain_ref,
    early, late,
):
    width = gmi_ref.shape[1]
    plane, layers = same_ref.shape[:2]
    first = early.shape[0] // 2 // (plane * layers)
    second = late.shape[0] // 2 // (plane * layers)
    core = where_ref[2]
    for part, half in ((same_ref, core), (other_ref, 1 - core)):
        for p in range(plane):
            for z in range(layers):
                chip = half * plane * layers + z * plane + p
                early[pl.ds(pl.multiple_of(chip * first, 16), first), :] = part[p, z, :first, :]
                late[pl.ds(pl.multiple_of(chip * second, 16), second), :] = part[p, z, first:, :]
    gmo_ref[...] = early[:width, :].astype(F32)
    gmi_ref[:width, :] = early[width : 2 * width, :].astype(F32)
    gmi_ref[width:, :] = late[: width + edge_width, :].astype(F32)
    at = 2 * width
    geit_ref[:, :width] = early[at : at + edge_width, :].astype(F32)
    geit_ref[:, width : 2 * width] = early[at + edge_width : at + 2 * edge_width, :].astype(F32)
    at = width + edge_width
    small = late[at : at + edge_width, :].astype(F32)
    geit_ref[:, 2 * width :] = jnp.transpose(small[:, :edge_width])
    geo_ref[...] = small[:, edge_width : 2 * edge_width]
    vecs = late[at + edge_width : at + edge_width + 16, :].astype(F32)
    g1_ref[...] = vecs[:1, :]
    g2_ref[...] = vecs[1:2, :]
    g3_ref[...] = vecs[2:3, :edge_width]
    gchain_ref[...] = vecs[3:4, :]


def ffn_grads(llo_ref, lhi_ref, dlo_ref, dhi_ref, wfi_ref, wfo_ref, gfi_ref, gfo_ref):
    block = min(llo_ref.shape[0], SPAN // 2)
    gfi = gfo = None
    for low_ref, dffn_ref in ((llo_ref, dlo_ref), (lhi_ref, dhi_ref)):
        for start in range(0, low_ref.shape[0], block):
            low = low_ref[start : start + block, :]
            dffn = dffn_ref[start : start + block, :]
            hidden, slope = gelu_pair(mm(low, wfi_ref[...]))
            part = mm_tn(hidden.astype(BF), dffn)
            gfo = part if gfo is None else gfo + part
            d_pre = (slope * mm_nt(dffn, wfo_ref[...])).astype(BF)
            part = mm_tn(low, d_pre)
            gfi = part if gfi is None else gfi + part
    gfo_ref[...] = gfo
    gfi_ref[...] = gfi


def whole(shape):
    return pl.BlockSpec(tuple(shape), lambda *_: (0,) * len(shape))


def part(shape, *index):
    return pl.BlockSpec(tuple(shape), lambda *_: index or (0,) * len(shape))


def per_step(count, shape):
    return pl.BlockSpec((count,) + tuple(shape[1:]), lambda i: (i,) + (0,) * (len(shape) - 1))


SCALARS = pl.BlockSpec(memory_space=pltpu.SMEM)
ANY = pl.BlockSpec(memory_space=pl.ANY)


def params(limit=56):
    return pltpu.CompilerParams(vmem_limit_bytes=limit << 20, dimension_semantics=("arbitrary",))


def pin(*arrays):
    return [pltpu.with_memory_space_constraint(x, pltpu.VMEM) if x.size * x.dtype.itemsize <= PINNED else x for x in arrays]


def sds(shape, dtype):
    return jax.ShapeDtypeStruct(tuple(shape), dtype)


def swap(x, axis):
    return lax.ppermute(x, axis, [(0, 1), (1, 0)])


def gather_spread(spread):
    same = lax.all_to_all(spread, CHIPS, 0, 0).reshape(-1, spread.shape[2])
    return same, swap(same, "c")


def scatter_halves(lo, hi):
    got = swap(hi, "c")
    both = (lo.astype(F32) + got.astype(F32)).astype(lo.dtype)
    return lax.all_to_all(both.reshape(lax.axis_size(CHIPS), -1, lo.shape[1]), CHIPS, 0, 0)


def send_shares(pieces):
    shares = len(pieces)
    got = [pieces[0]]
    for q in range(1, shares):
        got.append(lax.ppermute(pieces[q], ("y", "c"), [(s, (s + q) % shares) for s in range(shares)]))
    return got


def chip_sum(keep, send):
    got = jnp.pad(swap(send, "c"), ((0, 0), (0, keep.shape[1] - send.shape[1]), (0, 0)))
    return (keep.astype(F32) + got.astype(F32)).astype(keep.dtype)


def to_owners(both):
    return lax.all_to_all(both, CHIPS, 0, 0)


def cost(micros):
    return pl.CostEstimate(flops=int(micros * 1e9), bytes_accessed=int(micros * 1e6), transcendentals=0)


def per_device(
    node_in, edge_in, neighbors, chain_ids, residue_mask, w_msg_in, chain_vec, w_msg_out, gain_one,
    w_ffn_in, w_ffn_out, gain_two, w_edge_in, w_edge_out, gain_three, node_cot, edge_cot,
):
    dest_rows, width_k, edge_width = edge_in.shape
    rows_own, width = node_in.shape
    hidden_width = w_ffn_in.shape[1]
    nodes = chain_ids.shape[0]
    half = nodes // 2
    chips = lax.axis_size(CHIPS)
    per = 5 if width_k % 5 == 0 else 1
    steps = width_k // per
    count = per * dest_rows
    lanes = count + (-count) % 128
    shares = dest_rows // rows_own
    norm_scale = math.sqrt(width_k * shares)
    me_core = lax.axis_index("c")
    share = lax.axis_index("y") * 2 + me_core
    group = lax.axis_index("z") * 2 + lax.axis_index("x")
    z, x, y = (lax.axis_index(axis) for axis in CHIPS)
    where = jnp.stack([share, group, me_core, z, x, y]).astype(jnp.int32)

    edges = edge_in.transpose(1, 0, 2)
    cots = edge_cot.transpose(1, 0, 2)
    lo, hi = gather_spread(jnp.broadcast_to(node_in[None], (chips,) + node_in.shape))

    first_row = group * dest_rows
    source = neighbors.T
    dest_chain = lax.dynamic_slice_in_dim(chain_ids, first_row, dest_rows)
    dest_mask = lax.dynamic_slice_in_dim(residue_mask, first_row, dest_rows)
    lower = jnp.sum((chain_ids[None, :] < dest_chain[:, None]).astype(jnp.int32), axis=1)
    upper = jnp.sum((chain_ids[None, :] <= dest_chain[:, None]).astype(jnp.int32), axis=1)
    bits = jnp.sum(residue_mask.reshape(nodes // 16, 16) << jnp.arange(16, dtype=jnp.int32)[None, :], axis=1)
    pick = (source >> 4)[:, :, None] == jnp.arange(nodes // 16, dtype=jnp.int32)[None, None, :]
    word = jnp.sum(jnp.where(pick, bits[None, None, :], 0), axis=2)
    present = (word >> (source & 15)) & 1
    pair_mask = (dest_mask[None, :] * present).astype(F32)
    cross = ((source < lower[None, :]) | (source >= upper[None, :])).astype(F32)
    block = source // rows_own
    place = ((block % 2) ^ me_core) * half + (block // 2) * rows_own + source % rows_own
    table = jnp.stack([place.astype(F32), pair_mask, cross]).reshape(3, steps, count).transpose(1, 0, 2)
    flags = jnp.pad(table, ((0, 0), (0, 5), (0, lanes - count)))

    row = lambda v: v.reshape(1, -1)
    wei_t = w_edge_in.T
    edge_spec = per_step(per, edges.shape)
    flag_spec = per_step(1, flags.shape)
    wide_spec = [whole((rows_own, 2 * width))] * shares
    wide_out = [sds((rows_own, 2 * width), BF)] * shares
    share_spec = [whole((rows_own, width))] * shares

    f_slope, *sums = pl.pallas_call(
        functools.partial(message_forward, rows_own),
        grid=(steps,),
        in_specs=[
            SCALARS, edge_spec, flag_spec, whole((half, width)), whole((half, width)), whole(w_msg_in.shape), whole((1, width)),
        ],
        out_specs=[per_step(per, (width_k, dest_rows, width))] + wide_spec,
        out_shape=[sds((width_k, dest_rows, width), BF)] + wide_out,
        scratch_shapes=[
            pltpu.VMEM((half, width), BF), pltpu.VMEM((half, width), BF), pltpu.VMEM((dest_rows, width), F32),
            pltpu.VMEM((dest_rows, 2 * width), F32), pltpu.VMEM((count, width), F32),
        ],
        compiler_params=params(),
        name="message_forward",
    )(where, edges, flags, lo, hi, w_msg_in, row(chain_vec))
    sums = send_shares(sums)

    total, slopes, first_in, second_in, low, ffn_slope, ffn_hidden, node_out, e_spread, e_own = pl.pallas_call(
        functools.partial(node_forward, norm_scale),
        out_shape=[
            sds((rows_own, width), BF), sds((rows_own, width), F32), sds((rows_own, width), F32), sds((rows_own, width), F32),
            sds((chips, rows_own, width), BF), sds((rows_own, hidden_width), F32), sds((rows_own, hidden_width), BF), sds((rows_own, width), BF),
            sds((chips, rows_own, edge_width), BF), sds((rows_own, edge_width), BF),
        ],
        in_specs=[pl.BlockSpec(memory_space=pltpu.VMEM)] * 7 + [ANY] * 2 + [pl.BlockSpec(memory_space=pltpu.VMEM), ANY],
        scratch_shapes=[
            pltpu.VMEM(w_ffn_in.shape, BF), pltpu.VMEM(w_ffn_out.shape, BF), pltpu.VMEM(wei_t.shape, BF),
            pltpu.SemaphoreType.DMA((3,)),
        ],
        compiler_params=pltpu.CompilerParams(vmem_limit_bytes=56 << 20),
        name="node_forward",
    )(*sums, node_in, w_msg_out, row(gain_one), w_ffn_in, w_ffn_out, row(gain_two), wei_t)

    e_owns = send_shares([e_own] * shares)
    e_lo = lax.all_to_all(e_spread, CHIPS, 0, 0).reshape(-1, edge_width)
    e_lo, *e_owns = lax.optimization_barrier((e_lo, *e_owns))
    e_hi = swap(e_lo, "c")
    e_lo, low = lax.optimization_barrier((e_lo, low))
    low_lo = lax.all_to_all(low, CHIPS, 0, 0).reshape(half, width)

    edge_new, d_sum, e_slo, e_shi, *rest = pl.pallas_call(
        edge_network,
        grid=(steps,),
        in_specs=[SCALARS, edge_spec, edge_spec, flag_spec, whole((half, edge_width)), whole((half, edge_width))]
        + [whole((rows_own, edge_width))] * shares
        + [whole(wei_t.shape), whole(w_edge_out.shape), whole((1, edge_width))],
        out_specs=[edge_spec, edge_spec, whole((half, edge_width)), whole((half, edge_width))]
        + [whole((rows_own, edge_width))] * shares
        + [whole((edge_width, edge_width)), whole((edge_width, edge_width)), whole((8, edge_width))],
        out_shape=[sds(edges.shape, BF), sds(edges.shape, BF), sds((half, edge_width), BF), sds((half, edge_width), BF)]
        + [sds((rows_own, edge_width), BF)] * shares
        + [sds((edge_width, edge_width), F32), sds((edge_width, edge_width), F32), sds((8, edge_width), F32)],
        scratch_shapes=[
            pltpu.VMEM((count, edge_width), F32), pltpu.VMEM((count, edge_width), BF), pltpu.VMEM((count, edge_width), BF),
            pltpu.VMEM((count, edge_width), BF), pltpu.VMEM((count, edge_width), BF), pltpu.VMEM((count, edge_width), BF), pltpu.VMEM((nodes, edge_width), F32), pltpu.VMEM((dest_rows, edge_width), F32),
        ],
        compiler_params=params(),
        cost_estimate=cost(22),
        name="edge_network",
    )(where, edges, cots, flags, e_lo, e_hi, *e_owns, wei_t, w_edge_out, row(gain_three))
    g_in, g_out, g_gain3 = rest[shares:]
    e_slo, e_shi, low_lo, *e_sums = lax.optimization_barrier((e_slo, e_shi, low_lo, *rest[:shares]))
    low_hi = swap(low_lo, "c")
    e_sums = send_shares(e_sums)
    e_parts = scatter_halves(e_slo, e_shi)

    up = lambda rows: rows + (-rows) % (32 * chips)
    pay_early = up(2 * width + 2 * edge_width)
    pay_late = up(width + 2 * edge_width + 16)
    early_rows, late_rows = pay_early // (2 * chips), pay_late // (2 * chips)
    kept = (chips, early_rows + rows_own, width)
    operands = (
        e_parts, *e_sums, node_in, node_cot, node_out, first_in, second_in, ffn_slope, total, slopes,
        wei_t, w_msg_in, w_ffn_in, w_ffn_out, w_msg_out, row(gain_one), row(gain_two),
    )
    specs = [whole(x.shape) for x in operands]
    specs[13:18] = [part((edge_width, 2 * width))] + [ANY] * 4
    outs = [
        sds((rows_own, width), BF), sds((rows_own, width), F32), sds((8, width), F32), sds(kept, BF),
        sds((chips, early_rows, width), BF),
    ]
    d_hidden, n_grad, g_gains, keep, send = pl.pallas_call(
        functools.partial(node_backward, norm_scale),
        grid=(1,),
        in_specs=[SCALARS] + specs,
        out_specs=[whole(x.shape) for x in outs],
        out_shape=outs,
        scratch_shapes=[
            pltpu.VMEM((pay_early, width), BF), pltpu.VMEM(w_ffn_out.shape, BF), pltpu.VMEM(w_ffn_in.shape, BF),
            pltpu.VMEM(w_msg_out.shape, BF), pltpu.VMEM((width, width), BF), pltpu.SemaphoreType.DMA((4,)),
        ],
        compiler_params=params(),
        name="node_backward",
    )(where, *operands)
    d_hiddens = send_shares([d_hidden] * shares)
    early, *d_hiddens = lax.optimization_barrier((chip_sum(keep, send), *d_hiddens))
    early_parts = to_owners(early)

    sent = (chips, late_rows + rows_own, width)
    keep, send, e_grad = pl.pallas_call(
        message_backward,
        grid=(steps,),
        in_specs=[SCALARS, edge_spec, per_step(per, (width_k, dest_rows, width)), flag_spec, edge_spec]
        + share_spec + [ANY] * 3 + [whole((8, width))]
        + [whole((8, edge_width)), whole((edge_width, edge_width)), whole((edge_width, edge_width))],
        out_specs=[whole(sent), whole(sent), edge_spec],
        out_shape=[sds(sent, BF), sds(sent, BF), sds(edges.shape, F32)],
        scratch_shapes=[
            pltpu.VMEM((dest_rows, width), F32), pltpu.VMEM((count, width), BF), pltpu.VMEM((nodes, width), F32),
            pltpu.VMEM((edge_width, width), F32), pltpu.VMEM((8, width), F32), pltpu.VMEM((pay_late, width), BF),
            pltpu.VMEM((half, width), BF), pltpu.VMEM((half, width), BF), pltpu.VMEM((edge_width, width), BF),
            pltpu.SemaphoreType.DMA((3,)),
        ],
        compiler_params=params(),
        cost_estimate=cost(13),
        name="message_backward",
    )(where, edges, f_slope, flags, d_sum, *d_hiddens, w_msg_in, lo, hi, g_gains, g_gain3, g_in, g_out)
    late, early_parts = lax.optimization_barrier((chip_sum(keep, send), early_parts))
    late_parts = to_owners(late)
    dffn_lo = early_parts[:, early_rows:, :].reshape(half, width)
    dffn_hi = swap(dffn_lo, "c")

    tile = 256
    g_ffn_in, g_ffn_out = pl.pallas_call(
        ffn_grads,
        grid=(hidden_width // tile,),
        in_specs=[whole((half, width))] * 4
        + [pl.BlockSpec((width, tile), lambda i: (0, i)), pl.BlockSpec((tile, width), lambda i: (i, 0))],
        out_specs=[pl.BlockSpec((width, tile), lambda i: (0, i)), pl.BlockSpec((tile, width), lambda i: (i, 0))],
        out_shape=[sds(w_ffn_in.shape, F32), sds(w_ffn_out.shape, F32)],
        compiler_params=params(),
        cost_estimate=cost(18),
        name="ffn_grads",
    )(low_lo, low_hi, dffn_lo, dffn_hi, w_ffn_in, w_ffn_out)
    late_parts, g_ffn_in, g_ffn_out = lax.optimization_barrier((late_parts, g_ffn_in, g_ffn_out))

    layers = lax.axis_size("z")
    plane = chips // layers
    operands = (early_parts, late_parts, n_grad, w_msg_in)
    outs = [sds((rows_own, width), F32), sds((layers, early_rows + late_rows, width), BF)]
    node_grad, spread = pl.pallas_call(
        functools.partial(finish_nodes, late_rows, early_rows),
        grid=(1,),
        in_specs=[whole(x.shape) for x in operands[:3]] + [part((width, width), 1, 0)],
        out_specs=[whole(x.shape) for x in outs],
        out_shape=outs,
        compiler_params=params(),
        name="finish_nodes",
    )(*operands)
    layer = lax.all_to_all(spread, "z", 0, 0)
    same = lax.all_to_all(jnp.broadcast_to(layer[None], (plane,) + layer.shape), ("x", "y"), 0, 0)
    other = swap(same, "c")
    g_msg_in, g_msg_out, g_edge_t, g_edge_out, *vecs = pl.pallas_call(
        functools.partial(finish_weights, edge_width),
        in_specs=[SCALARS] + [pl.BlockSpec(memory_space=pltpu.VMEM)] * 2,
        out_shape=[
            sds(w_msg_in.shape, F32), sds((width, width), F32), sds(wei_t.shape, F32), sds((edge_width, edge_width), F32),
            sds((1, width), F32), sds((1, width), F32), sds((1, edge_width), F32), sds((1, width), F32),
        ],
        scratch_shapes=[pltpu.VMEM((pay_early, width), BF), pltpu.VMEM((pay_late, width), BF)],
        compiler_params=pltpu.CompilerParams(vmem_limit_bytes=(24 if nodes <= 2 * SPAN else 56) << 20),
        name="finish_weights",
    )(where, *pin(same, other))
    g_gain1, g_gain2, g_gain3, g_chain = (v.reshape(-1) for v in vecs)
    return (
        node_out, edge_new.transpose(1, 0, 2), node_grad, e_grad.transpose(1, 0, 2), g_msg_in, g_chain, g_msg_out,
        g_gain1, g_ffn_in, g_ffn_out, g_gain2, g_edge_t.T, g_edge_out, g_gain3,
    )


def solution(mesh):
    groups, shares = mesh.shape["res"], mesh.shape["edge"]
    fine = Mesh(mesh.devices.reshape(groups // 2, 2, shares // 2, 2), ("z", "x", "y", "c"))
    rows = P(("z", "x", "y", "c"), None)
    edges = P(("z", "x"), ("y", "c"), None)
    in_specs = (rows, edges, P(("z", "x"), ("y", "c"))) + (P(),) * 12 + (rows, edges)
    out_specs = (rows, edges, rows, edges) + (P(),) * 10
    return jax.shard_map(per_device, mesh=fine, in_specs=in_specs, out_specs=out_specs, check_vma=False)
```

```python
import functools
import math

import jax
import jax.numpy as jnp
from jax import lax
from jax.experimental import pallas as pl
from jax.experimental.pallas import tpu as pltpu
from jax.sharding import Mesh, PartitionSpec as P

EPS = 1e-05
CHIPS = ("z", "x", "y")
BF = jnp.bfloat16
F32 = jnp.float32
ROWS = 80
PIECE = 800
SPAN = 1280
RSQRT2 = math.sqrt(0.5)
INV_SQRT_2PI = 1.0 / math.sqrt(2.0 * math.pi)
PLACE, MASK, CROSS = 0, 1, 2


def mm(a, b):
    return jnp.dot(a, b, preferred_element_type=F32)


def mm_nt(a, b):
    return lax.dot_general(a, b, (((1,), (1,)), ((), ())), preferred_element_type=F32)


def mm_tn(a, b):
    return lax.dot_general(a, b, (((0,), (0,)), ((), ())), preferred_element_type=F32)


def gelu_pair(v):
    cdf = 0.5 * (1.0 + lax.erf(v * RSQRT2))
    pdf = INV_SQRT_2PI * jnp.exp(-0.5 * v * v)
    return v * cdf, cdf + v * pdf


def norm_parts(z):
    centre = z - jnp.mean(z, axis=-1, keepdims=True)
    r = lax.rsqrt(jnp.mean(centre * centre, axis=-1, keepdims=True) + EPS)
    return centre * r, r


def norm_back(n, r, gain, cot):
    b = cot * gain
    dz = r * (b - jnp.mean(b, -1, keepdims=True) - n * jnp.mean(b * n, -1, keepdims=True))
    return dz, jnp.sum(cot * n, axis=0, keepdims=True)


def gather_rows(place, halves):
    total = None
    for h, table in enumerate(halves):
        count = table.shape[0]
        block = min(count, SPAN)
        for start in range(0, count, block):
            lane = lax.broadcasted_iota(jnp.int32, (place.shape[0], block), 1) + (h * count + start)
            hot = jnp.where(lane == place, 1.0, 0.0).astype(BF)
            part = mm(hot, table[start : start + block, :])
            total = part if total is None else total + part
    return total


def scatter_rows(place_row, rows, acc):
    nodes = acc.shape[0]
    block = min(nodes, SPAN // 2)

    @pl.loop(0, nodes // block)
    def _(i):
        start = pl.multiple_of(i * block, block)
        row = lax.broadcasted_iota(jnp.int32, (block, place_row.shape[1]), 0) + start
        hot = jnp.where(row == place_row, 1.0, 0.0).astype(BF)
        acc[pl.ds(start, block), :] += mm(hot, rows)


def group_rows(where_ref, lo_ref, hi_ref, rows_own):
    group, core = where_ref[1], where_ref[2]
    start = pl.multiple_of(group * 2 * rows_own, 2 * rows_own)
    same = lo_ref[pl.ds(start, 2 * rows_own), :].astype(F32)
    other = hi_ref[pl.ds(start, 2 * rows_own), :].astype(F32)
    swapped = core == 1
    first = jnp.where(swapped, other, same)
    second = jnp.where(swapped, same, other)
    rows = [first[:rows_own], second[:rows_own], first[rows_own:], second[rows_own:]]
    return jnp.concatenate(rows, axis=0)


def put_shares(where_ref, refs, out):
    rows = refs[0].shape[0]
    shares = len(refs)
    for q, ref in enumerate(refs):
        at = lax.rem(where_ref[0] + shares - q, shares) * rows
        out[pl.ds(pl.multiple_of(at, 8), rows), :] = ref[...].astype(out.dtype)


def take_shares(where_ref, acc, refs):
    rows = refs[0].shape[0]
    shares = len(refs)
    for q, ref in enumerate(refs):
        at = lax.rem(where_ref[0] + q, shares) * rows
        ref[...] = acc[pl.ds(pl.multiple_of(at, 8), rows), :].astype(ref.dtype)


def add_up(refs):
    total = refs[0][...].astype(F32)
    for ref in refs[1:]:
        total += ref[...].astype(F32)
    return total


def message_forward(
    rows_own,
    where_ref, edge_ref, flags_ref, lo_ref, hi_ref, wmi_ref, chain_ref,
    slope_ref, s0, s1, s2, s3,
    table_lo, table_hi, own, acc, pre_s,
):
    step = pl.program_id(0)
    width = wmi_ref.shape[1]
    per, dest_rows, edge_width = edge_ref.shape
    edges = per * dest_rows

    @pl.when(step == 0)
    def _():
        weights = wmi_ref[width : 2 * width, :]
        half = lo_ref.shape[0]
        block = half // 2 if half <= SPAN else SPAN // 2

        @pl.loop(0, half // block)
        def _(i):
            at = pl.ds(pl.multiple_of(i * block, block), block)
            table_lo[at, :] = mm(lo_ref[at, :], weights).astype(BF)
            table_hi[at, :] = mm(hi_ref[at, :], weights).astype(BF)

        group = group_rows(where_ref, lo_ref, hi_ref, rows_own).astype(BF)
        own[...] = mm(group, wmi_ref[:width, :])
        acc[...] = jnp.zeros_like(acc)

    flags = jnp.transpose(flags_ref[0])[:edges, :]
    place = flags[:, PLACE : PLACE + 1].astype(jnp.int32)
    pre_s[...] = gather_rows(place, (table_lo, table_hi)) + mm(
        edge_ref[...].reshape(edges, edge_width), wmi_ref[2 * width :, :]
    )
    for j in range(per):
        for r in range(0, dest_rows, ROWS):
            at = slice(j * dest_rows + r, j * dest_rows + r + ROWS)
            mask = flags[at, MASK : MASK + 1]
            cross = flags[at, CROSS : CROSS + 1]
            pre = pre_s[at, :] + own[r : r + ROWS, :] + cross * chain_ref[...]
            hidden, slope = gelu_pair(pre)
            slope = slope * mask
            slope_ref[j, r : r + ROWS, :] = slope.astype(BF)
            acc[r : r + ROWS, :width] += hidden.astype(BF).astype(F32) * mask
            acc[r : r + ROWS, width:] += slope

    @pl.when(step == pl.num_programs(0) - 1)
    def _():
        take_shares(where_ref, acc, (s0, s1, s2, s3))


def start_copies(sources, targets, sems):
    copies = [pltpu.make_async_copy(s, t, sems.at[i]) for i, (s, t) in enumerate(zip(sources, targets))]
    for copy in copies:
        copy.start()
    return copies


def node_forward(
    norm_scale,
    s0, s1, s2, s3, node_ref, wmo_ref, gain1_ref, wfi_any, wfo_any, gain2_ref, weit_any,
    total_ref, slopes_ref, first_ref, second_ref, low_ref, fslope_ref, fhidden_ref, out_ref, src_ref, eown_ref,
    wfi_ref, wfo_ref, weit_ref, sems,
):
    copies = start_copies((wfi_any, wfo_any, weit_any), (wfi_ref, wfo_ref, weit_ref), sems)
    width = node_ref.shape[1]
    sums = add_up((s0, s1, s2, s3))
    total = sums[:, :width].astype(BF)
    total_ref[...] = total
    slopes_ref[...] = sums[:, width:]
    first_in = node_ref[...].astype(F32) + mm(total, wmo_ref[...]) * (1.0 / norm_scale)
    first_ref[...] = first_in
    norm_one = norm_parts(first_in)[0] * gain1_ref[...]
    low = norm_one.astype(BF)
    for i in range(low_ref.shape[0]):
        low_ref[i] = low
    copies[0].wait()
    hidden, slope = gelu_pair(mm(low, wfi_ref[...]))
    hidden = hidden.astype(BF)
    fslope_ref[...] = slope
    fhidden_ref[...] = hidden
    copies[1].wait()
    second_in = norm_one + mm(hidden, wfo_ref[...])
    second_ref[...] = second_in
    node_out = (norm_parts(second_in)[0] * gain2_ref[...]).astype(BF)
    out_ref[...] = node_out
    copies[2].wait()
    eown_ref[...] = mm_nt(node_out, weit_ref[:, :width]).astype(BF)
    src = mm_nt(node_out, weit_ref[:, width : 2 * width]).astype(BF)
    for i in range(src_ref.shape[0]):
        src_ref[i] = src


def edge_network(
    where_ref, edge_ref, cot_ref, flags_ref, lo_ref, hi_ref, e0, e1, e2, e3, weit_ref, weo_ref, gain_ref,
    out_ref, dsum_ref, slo_ref, shi_ref, o0, o1, o2, o3, gin_ref, gout_ref, ggain_ref,
    own, dpre_s, hidden_s, delta_s, out_s, dsum_s, acc, own_acc,
):
    step = pl.program_id(0)
    per, dest_rows, edge_width = edge_ref.shape
    edges = per * dest_rows
    width = (weit_ref.shape[1] - edge_width) // 2
    weights_t = weit_ref[:, 2 * width :]

    @pl.when(step == 0)
    def _():
        put_shares(where_ref, (e0, e1, e2, e3), own)
        for j in range(1, per):
            own[j * dest_rows : (j + 1) * dest_rows, :] = own[:dest_rows, :]
        acc[...] = jnp.zeros_like(acc)
        own_acc[...] = jnp.zeros_like(own_acc)
        gin_ref[...] = jnp.zeros_like(gin_ref)
        gout_ref[...] = jnp.zeros_like(gout_ref)
        ggain_ref[...] = jnp.zeros_like(ggain_ref)

    flags = jnp.transpose(flags_ref[0])[:edges, :]
    place = flags[:, PLACE : PLACE + 1].astype(jnp.int32)
    edge_all = edge_ref[...].reshape(edges, edge_width)
    cot_all = cot_ref[...].reshape(edges, edge_width)
    pre_all = gather_rows(place, (lo_ref, hi_ref)) + mm_nt(edge_all, weights_t) + own[...]
    gain = gain_ref[...]
    piece = PIECE if edges % PIECE == 0 else edges
    for start in range(0, edges, piece):
        at = slice(start, start + piece)
        mask = flags[at, MASK : MASK + 1]
        hidden, slope = gelu_pair(pre_all[at, :])
        hidden = (hidden * mask).astype(BF)
        hidden_s[at, :] = hidden
        n, r = norm_parts(edge_all[at, :].astype(F32) + mm(hidden, weo_ref[...]))
        out_s[at, :] = (n * gain).astype(BF)
        cot = cot_all[at, :].astype(F32)
        cn = cot * n
        ggain_ref[...] += jnp.sum(cn.reshape(piece // 8, 8, edge_width), axis=0)
        b = cot * gain
        dz = r * (b - jnp.mean(b, -1, keepdims=True) - n * jnp.mean(cn * gain, -1, keepdims=True))
        d_delta = (dz * mask).astype(BF)
        delta_s[at, :] = d_delta
        d_low = (slope * mm_nt(d_delta, weo_ref[...])).astype(BF)
        dpre_s[at, :] = d_low
        dsum_s[at, :] = (dz + mm(d_low, weights_t)).astype(BF)
    out_ref[...] = out_s[...].reshape(out_ref.shape)
    dsum_ref[...] = dsum_s[...].reshape(dsum_ref.shape)
    for j in range(per):
        own_acc[...] += dpre_s[j * dest_rows : (j + 1) * dest_rows, :].astype(F32)
    gout_ref[...] += mm_tn(hidden_s[...], delta_s[...])
    gin_ref[...] += mm_tn(edge_all, dpre_s[...])
    place_row = flags_ref[0, PLACE : PLACE + 1, :edges].astype(jnp.int32)
    scatter_rows(place_row, dpre_s[...], acc)

    @pl.when(step == pl.num_programs(0) - 1)
    def _():
        half = slo_ref.shape[0]
        slo_ref[...] = acc[:half, :].astype(BF)
        shi_ref[...] = acc[half:, :].astype(BF)
        take_shares(where_ref, own_acc, (o0, o1, o2, o3))


def node_backward(
    norm_scale,
    where_ref, parts_ref, o0, o1, o2, o3, node_ref, node_cot_ref, out_ref, first_ref, second_ref, fslope_ref,
    total_ref, slopes_ref, weit_ref, wmi_any, wfi_any, wfo_any, wmo_any, gain1_ref, gain2_ref,
    d_ref, ngrad_ref, ggain_ref, keep_ref, send_ref,
    pay, wfo_ref, wfi_ref, wmo_ref, wmi_ref, sems,
):
    width = out_ref.shape[1]
    own_rows = wmi_any.at[pl.ds(0, width), :]
    copies = start_copies((wfo_any, wfi_any, wmo_any, own_rows), (wfo_ref, wfi_ref, wmo_ref, wmi_ref), sems)
    from_sources = add_up(tuple(parts_ref.at[i] for i in range(parts_ref.shape[0]))).astype(BF)
    from_own = add_up((o0, o1, o2, o3)).astype(BF)
    d_updated = (
        node_cot_ref[...].astype(F32)
        + mm(from_own, weit_ref[:, :width])
        + mm(from_sources, weit_ref[:, width : 2 * width])
    )
    node_out = out_ref[...]
    n, r = norm_parts(second_ref[...])
    d_second, ggain2 = norm_back(n, r, gain2_ref[...], d_updated)
    dffn = d_second.astype(BF)
    copies[0].wait()
    d_ffn_pre = (fslope_ref[...] * mm_nt(dffn, wfo_ref[...])).astype(BF)
    copies[1].wait()
    d_norm_one = d_second + mm_nt(d_ffn_pre, wfi_ref[...])
    n, r = norm_parts(first_ref[...])
    d_first, ggain1 = norm_back(n, r, gain1_ref[...], d_norm_one)
    d_summed = (d_first * (1.0 / norm_scale)).astype(BF)
    copies[2].wait()
    d_hidden = mm_nt(d_summed, wmo_ref[...])
    d_ref[...] = d_hidden.astype(BF)
    own_sum = (d_hidden * slopes_ref[...]).astype(BF)
    copies[3].wait()
    ngrad_ref[...] = d_first + mm_nt(own_sum, wmi_ref[...])
    ggain_ref[...] = jnp.concatenate([ggain1, ggain2, jnp.zeros((6, width), F32)], axis=0)
    parts = (
        mm_tn(total_ref[...], d_summed), mm_tn(node_ref[...], own_sum), mm_tn(from_own, node_out), mm_tn(from_sources, node_out)
    )
    at = 0
    for part in parts:
        pay[at : at + part.shape[0], :] = part.astype(BF)
        at += part.shape[0]
    pay[at:, :] = jnp.zeros((pay.shape[0] - at, width), BF)
    early = pay.shape[0] // 2 // keep_ref.shape[0]
    split_halves(where_ref, pay, early, keep_ref, send_ref)
    for i in range(keep_ref.shape[0]):
        keep_ref[i, early:, :] = dffn


def split_halves(where_ref, pay, rows, keep_ref, send_ref):
    half = pay.shape[0] // 2
    at = pl.multiple_of(where_ref[2] * half, 16)
    shape = (keep_ref.shape[0], rows, pay.shape[1])
    keep_ref[:, :rows, :] = pay[pl.ds(at, half), :].reshape(shape)
    send_ref[:, :rows, :] = pay[pl.ds(half - at, half), :].reshape(shape)


def message_backward(
    where_ref, edge_ref, slope_ref, flags_ref, dsum_ref, d0, d1, d2, d3, wmi_any, lo_any, hi_any, gain_ref, gain3_ref, gin_ref,
    gout_ref,
    keep_ref, send_ref, eg_ref,
    own, dpre_s, acc, gin, chain, pay, lo_ref, hi_ref, wme_ref, sems,
):
    step = pl.program_id(0)
    width = wme_ref.shape[1]
    per, dest_rows, edge_width = edge_ref.shape
    edges = per * dest_rows
    copy_w = pltpu.make_async_copy(wmi_any.at[pl.ds(2 * width, edge_width), :], wme_ref, sems.at[2])
    copy_lo = pltpu.make_async_copy(lo_any, lo_ref, sems.at[0])
    copy_hi = pltpu.make_async_copy(hi_any, hi_ref, sems.at[1])

    @pl.when(step == 0)
    def _():
        copy_w.start()
        copy_lo.start()
        copy_hi.start()
        put_shares(where_ref, (d0, d1, d2, d3), own)
        acc[...] = jnp.zeros_like(acc)
        gin[...] = jnp.zeros_like(gin)
        chain[...] = jnp.zeros_like(chain)

    flags = jnp.transpose(flags_ref[0])[:edges, :]
    for j in range(per):
        for r in range(0, dest_rows, ROWS):
            at = slice(j * dest_rows + r, j * dest_rows + r + ROWS)
            d_low = (slope_ref[j, r : r + ROWS, :].astype(F32) * own[r : r + ROWS, :]).astype(BF)
            dpre_s[at, :] = d_low
            crossed = d_low.astype(F32) * flags[at, CROSS : CROSS + 1]
            chain[...] += jnp.sum(crossed.reshape(ROWS // 8, 8, width), axis=0)
    @pl.when(step == 0)
    def _():
        copy_w.wait()

    d_all = dpre_s[...]
    gin[...] += mm_tn(edge_ref[...].reshape(edges, edge_width), d_all)
    back = mm_nt(d_all, wme_ref[...])
    for j in range(per):
        eg_ref[j] = dsum_ref[j].astype(F32) + back[j * dest_rows : (j + 1) * dest_rows, :]
    place_row = flags_ref[0, PLACE : PLACE + 1, :edges].astype(jnp.int32)
    scatter_rows(place_row, d_all, acc)

    @pl.when(step == pl.num_programs(0) - 1)
    def _():
        half = lo_ref.shape[0]
        chips = keep_ref.shape[0]
        rows = half // chips
        late = keep_ref.shape[1] - rows
        for chip in range(chips):
            keep_ref[chip, late:, :] = acc[chip * rows : (chip + 1) * rows, :].astype(BF)
            send_ref[chip, late:, :] = acc[half + chip * rows : half + (chip + 1) * rows, :].astype(BF)
        copy_lo.wait()
        copy_hi.wait()
        from_nodes = mm_tn(lo_ref[...], acc[:half, :].astype(BF)) + mm_tn(hi_ref[...], acc[half:, :].astype(BF))
        pay[:width, :] = from_nodes.astype(BF)
        at = width
        pay[at : at + edge_width, :] = gin[...].astype(BF)
        at += edge_width
        spare = jnp.zeros((edge_width, width - 2 * edge_width), F32)
        pay[at : at + edge_width, :] = jnp.concatenate([gin_ref[...], gout_ref[...], spare], axis=1).astype(BF)
        at += edge_width
        crossed = jnp.sum(chain[...], axis=0, keepdims=True)
        gain3 = jnp.concatenate([jnp.sum(gain3_ref[...], axis=0, keepdims=True), jnp.zeros((1, width - edge_width), F32)], axis=1)
        vecs = jnp.concatenate([gain_ref[:2, :], gain3, crossed, jnp.zeros((12, width), F32)], axis=0)
        pay[at : at + 16, :] = vecs.astype(BF)
        pay[at + 16 :, :] = jnp.zeros((pay.shape[0] - at - 16, width), BF)
        split_halves(where_ref, pay, late, keep_ref, send_ref)


def finish_nodes(late, parts_ref, ngrad_ref, wmi_ref, out_ref):
    total = add_up(tuple(parts_ref.at[i, late:, :] for i in range(parts_ref.shape[0])))
    out_ref[...] = ngrad_ref[...] + mm_nt(total.astype(BF), wmi_ref[...])


def finish_payload(late, mine_ref, parts_ref, spread_ref):
    early = mine_ref.shape[0]
    other = add_up(tuple(parts_ref.at[i, :late, :] for i in range(parts_ref.shape[0]))).astype(BF)
    for i in range(spread_ref.shape[0]):
        spread_ref[i, :early, :] = mine_ref[...]
        spread_ref[i, early:, :] = other


def finish_weights(
    edge_width,
    where_ref, same_ref, other_ref,
    gmi_ref, gmo_ref, geit_ref, geo_ref, g1_ref, g2_ref, g3_ref, gchain_ref,
    early, late,
):
    width = gmi_ref.shape[1]
    plane, layers = same_ref.shape[:2]
    first = early.shape[0] // 2 // (plane * layers)
    second = late.shape[0] // 2 // (plane * layers)
    core = where_ref[2]
    for part, half in ((same_ref, core), (other_ref, 1 - core)):
        for p in range(plane):
            for z in range(layers):
                chip = half * plane * layers + z * plane + p
                early[pl.ds(pl.multiple_of(chip * first, 16), first), :] = part[p, z, :first, :]
                late[pl.ds(pl.multiple_of(chip * second, 16), second), :] = part[p, z, first:, :]
    gmo_ref[...] = early[:width, :].astype(F32)
    gmi_ref[:width, :] = early[width : 2 * width, :].astype(F32)
    gmi_ref[width:, :] = late[: width + edge_width, :].astype(F32)
    at = 2 * width
    geit_ref[:, :width] = early[at : at + edge_width, :].astype(F32)
    geit_ref[:, width : 2 * width] = early[at + edge_width : at + 2 * edge_width, :].astype(F32)
    at = width + edge_width
    small = late[at : at + edge_width, :].astype(F32)
    geit_ref[:, 2 * width :] = jnp.transpose(small[:, :edge_width])
    geo_ref[...] = small[:, edge_width : 2 * edge_width]
    vecs = late[at + edge_width : at + edge_width + 16, :].astype(F32)
    g1_ref[...] = vecs[:1, :]
    g2_ref[...] = vecs[1:2, :]
    g3_ref[...] = vecs[2:3, :edge_width]
    gchain_ref[...] = vecs[3:4, :]


def ffn_grads(llo_ref, lhi_ref, dlo_ref, dhi_ref, wfi_ref, wfo_ref, gfi_ref, gfo_ref):
    block = min(llo_ref.shape[0], SPAN // 2)
    gfi = gfo = None
    for low_ref, dffn_ref in ((llo_ref, dlo_ref), (lhi_ref, dhi_ref)):
        for start in range(0, low_ref.shape[0], block):
            low = low_ref[start : start + block, :]
            dffn = dffn_ref[start : start + block, :]
            hidden, slope = gelu_pair(mm(low, wfi_ref[...]))
            part = mm_tn(hidden.astype(BF), dffn)
            gfo = part if gfo is None else gfo + part
            d_pre = (slope * mm_nt(dffn, wfo_ref[...])).astype(BF)
            part = mm_tn(low, d_pre)
            gfi = part if gfi is None else gfi + part
    gfo_ref[...] = gfo
    gfi_ref[...] = gfi


def whole(shape):
    return pl.BlockSpec(tuple(shape), lambda *_: (0,) * len(shape))


def part(shape, *index):
    return pl.BlockSpec(tuple(shape), lambda *_: index or (0,) * len(shape))


def per_step(count, shape):
    return pl.BlockSpec((count,) + tuple(shape[1:]), lambda i: (i,) + (0,) * (len(shape) - 1))


SCALARS = pl.BlockSpec(memory_space=pltpu.SMEM)
ANY = pl.BlockSpec(memory_space=pl.ANY)


def params(limit=56):
    return pltpu.CompilerParams(vmem_limit_bytes=limit << 20, dimension_semantics=("arbitrary",))


def pin(small, *arrays):
    return [pltpu.with_memory_space_constraint(x, pltpu.VMEM) if small else x for x in arrays]


def vmem(small, shape, dtype):
    return pltpu.VMEM(tuple(shape), dtype) if small else sds(shape, dtype)


def sds(shape, dtype):
    return jax.ShapeDtypeStruct(tuple(shape), dtype)


def swap(x, axis):
    return lax.ppermute(x, axis, [(0, 1), (1, 0)])


def gather_spread(spread):
    same = lax.all_to_all(spread, CHIPS, 0, 0).reshape(-1, spread.shape[2])
    return same, swap(same, "c")


def scatter_halves(lo, hi):
    got = swap(hi, "c")
    both = (lo.astype(F32) + got.astype(F32)).astype(lo.dtype)
    return lax.all_to_all(both.reshape(lax.axis_size(CHIPS), -1, lo.shape[1]), CHIPS, 0, 0)


def send_shares(pieces):
    shares = len(pieces)
    got = [pieces[0]]
    for q in range(1, shares):
        got.append(lax.ppermute(pieces[q], ("y", "c"), [(s, (s + q) % shares) for s in range(shares)]))
    return got


def chip_sum(keep, send):
    got = jnp.pad(swap(send, "c"), ((0, 0), (0, keep.shape[1] - send.shape[1]), (0, 0)))
    return (keep.astype(F32) + got.astype(F32)).astype(keep.dtype)


def to_owners(both):
    return lax.all_to_all(both, CHIPS, 0, 0)


def cost(micros):
    return pl.CostEstimate(flops=int(micros * 1e9), bytes_accessed=int(micros * 1e6), transcendentals=0)


def per_device(
    node_in, edge_in, neighbors, chain_ids, residue_mask, w_msg_in, chain_vec, w_msg_out, gain_one,
    w_ffn_in, w_ffn_out, gain_two, w_edge_in, w_edge_out, gain_three, node_cot, edge_cot,
):
    dest_rows, width_k, edge_width = edge_in.shape
    rows_own, width = node_in.shape
    hidden_width = w_ffn_in.shape[1]
    nodes = chain_ids.shape[0]
    half = nodes // 2
    small = nodes <= 2 * SPAN
    chips = lax.axis_size(CHIPS)
    per = 5 if width_k % 5 == 0 else 1
    steps = width_k // per
    count = per * dest_rows
    lanes = count + (-count) % 128
    shares = dest_rows // rows_own
    norm_scale = math.sqrt(width_k * shares)
    me_core = lax.axis_index("c")
    share = lax.axis_index("y") * 2 + me_core
    group = lax.axis_index("z") * 2 + lax.axis_index("x")
    z, x, y = (lax.axis_index(axis) for axis in CHIPS)
    where = jnp.stack([share, group, me_core, z, x, y]).astype(jnp.int32)

    edges = edge_in.transpose(1, 0, 2)
    cots = edge_cot.transpose(1, 0, 2)
    lo, hi = gather_spread(jnp.broadcast_to(node_in[None], (chips,) + node_in.shape))

    first_row = group * dest_rows
    source = neighbors.T
    dest_chain = lax.dynamic_slice_in_dim(chain_ids, first_row, dest_rows)
    dest_mask = lax.dynamic_slice_in_dim(residue_mask, first_row, dest_rows)
    lower = jnp.sum((chain_ids[None, :] < dest_chain[:, None]).astype(jnp.int32), axis=1)
    upper = jnp.sum((chain_ids[None, :] <= dest_chain[:, None]).astype(jnp.int32), axis=1)
    bits = jnp.sum(residue_mask.reshape(nodes // 16, 16) << jnp.arange(16, dtype=jnp.int32)[None, :], axis=1)
    pick = (source >> 4)[:, :, None] == jnp.arange(nodes // 16, dtype=jnp.int32)[None, None, :]
    word = jnp.sum(jnp.where(pick, bits[None, None, :], 0), axis=2)
    present = (word >> (source & 15)) & 1
    pair_mask = (dest_mask[None, :] * present).astype(F32)
    cross = ((source < lower[None, :]) | (source >= upper[None, :])).astype(F32)
    block = source // rows_own
    place = ((block % 2) ^ me_core) * half + (block // 2) * rows_own + source % rows_own
    table = jnp.stack([place.astype(F32), pair_mask, cross]).reshape(3, steps, count).transpose(1, 0, 2)
    flags = jnp.pad(table, ((0, 0), (0, 5), (0, lanes - count)))

    row = lambda v: v.reshape(1, -1)
    wei_t = w_edge_in.T
    edge_spec = per_step(per, edges.shape)
    flag_spec = per_step(1, flags.shape)
    wide_spec = [whole((rows_own, 2 * width))] * shares
    wide_out = [sds((rows_own, 2 * width), BF)] * shares
    share_spec = [whole((rows_own, width))] * shares

    f_slope, *sums = pl.pallas_call(
        functools.partial(message_forward, rows_own),
        grid=(steps,),
        in_specs=[
            SCALARS, edge_spec, flag_spec, whole((half, width)), whole((half, width)), whole(w_msg_in.shape), whole((1, width)),
        ],
        out_specs=[per_step(per, (width_k, dest_rows, width))] + wide_spec,
        out_shape=[sds((width_k, dest_rows, width), BF)] + wide_out,
        scratch_shapes=[
            pltpu.VMEM((half, width), BF), pltpu.VMEM((half, width), BF), pltpu.VMEM((dest_rows, width), F32),
            pltpu.VMEM((dest_rows, 2 * width), F32), pltpu.VMEM((count, width), F32),
        ],
        compiler_params=params(),
        name="message_forward",
    )(where, edges, flags, *pin(small, lo, hi), w_msg_in, row(chain_vec))
    sums = send_shares(sums)

    total, slopes, first_in, second_in, low, ffn_slope, ffn_hidden, node_out, e_spread, e_own = pl.pallas_call(
        functools.partial(node_forward, norm_scale),
        out_shape=[
            sds((rows_own, width), BF), sds((rows_own, width), F32), sds((rows_own, width), F32), sds((rows_own, width), F32),
            sds((chips, rows_own, width), BF), sds((rows_own, hidden_width), F32), sds((rows_own, hidden_width), BF), sds((rows_own, width), BF),
            sds((chips, rows_own, edge_width), BF), sds((rows_own, edge_width), BF),
        ],
        in_specs=[pl.BlockSpec(memory_space=pltpu.VMEM)] * 7 + [ANY] * 2 + [pl.BlockSpec(memory_space=pltpu.VMEM), ANY],
        scratch_shapes=[
            pltpu.VMEM(w_ffn_in.shape, BF), pltpu.VMEM(w_ffn_out.shape, BF), pltpu.VMEM(wei_t.shape, BF),
            pltpu.SemaphoreType.DMA((3,)),
        ],
        compiler_params=pltpu.CompilerParams(vmem_limit_bytes=56 << 20),
        name="node_forward",
    )(sums[0], *pin(small, *sums[1:]), node_in, w_msg_out, row(gain_one), w_ffn_in, w_ffn_out, row(gain_two), wei_t)

    e_owns = send_shares([e_own] * shares)
    e_lo = lax.all_to_all(e_spread, CHIPS, 0, 0).reshape(-1, edge_width)
    e_lo, *e_owns = lax.optimization_barrier((e_lo, *e_owns))
    e_hi = swap(e_lo, "c")
    e_lo, low = lax.optimization_barrier((e_lo, low))
    low_lo = lax.all_to_all(low, CHIPS, 0, 0).reshape(half, width)

    edge_new, d_sum, e_slo, e_shi, *rest = pl.pallas_call(
        edge_network,
        grid=(steps,),
        in_specs=[SCALARS, edge_spec, edge_spec, flag_spec, whole((half, edge_width)), whole((half, edge_width))]
        + [whole((rows_own, edge_width))] * shares
        + [whole(wei_t.shape), whole(w_edge_out.shape), whole((1, edge_width))],
        out_specs=[edge_spec, edge_spec, whole((half, edge_width)), whole((half, edge_width))]
        + [whole((rows_own, edge_width))] * shares
        + [whole((edge_width, edge_width)), whole((edge_width, edge_width)), whole((8, edge_width))],
        out_shape=[sds(edges.shape, BF), sds(edges.shape, BF)] + [vmem(small, (half, edge_width), BF)] * 2
        + [sds((rows_own, edge_width), BF)] * shares
        + [sds((edge_width, edge_width), F32), sds((edge_width, edge_width), F32), sds((8, edge_width), F32)],
        scratch_shapes=[
            pltpu.VMEM((count, edge_width), F32), pltpu.VMEM((count, edge_width), BF), pltpu.VMEM((count, edge_width), BF),
            pltpu.VMEM((count, edge_width), BF), pltpu.VMEM((count, edge_width), BF), pltpu.VMEM((count, edge_width), BF), pltpu.VMEM((nodes, edge_width), F32), pltpu.VMEM((dest_rows, edge_width), F32),
        ],
        compiler_params=params(),
        cost_estimate=cost(22),
        name="edge_network",
    )(where, edges, cots, flags, *pin(small, e_lo, e_hi), e_owns[0], *pin(small, *e_owns[1:]), wei_t, w_edge_out, row(gain_three))
    g_in, g_out, g_gain3 = rest[shares:]
    e_slo, e_shi, low_lo, *e_sums = lax.optimization_barrier((e_slo, e_shi, low_lo, *rest[:shares]))
    low_hi = swap(low_lo, "c")
    e_sums = send_shares(e_sums)
    e_parts = scatter_halves(e_slo, e_shi)

    up = lambda rows: rows + (-rows) % (32 * chips)
    pay_early = up(2 * width + 2 * edge_width)
    pay_late = up(width + 2 * edge_width + 16)
    early_rows, late_rows = pay_early // (2 * chips), pay_late // (2 * chips)
    kept = (chips, early_rows + rows_own, width)
    operands = (
        *pin(small, e_parts), e_sums[0], *pin(small, *e_sums[1:]), node_in, node_cot, node_out, first_in, second_in, ffn_slope, total, slopes,
        wei_t, w_msg_in, w_ffn_in, w_ffn_out, w_msg_out, row(gain_one), row(gain_two),
    )
    specs = [whole(x.shape) for x in operands]
    specs[13:18] = [part((edge_width, 2 * width))] + [ANY] * 4
    outs = [
        sds((rows_own, width), BF), sds((rows_own, width), F32), sds((8, width), F32), vmem(small, kept, BF),
        vmem(small, (chips, early_rows, width), BF),
    ]
    d_hidden, n_grad, g_gains, keep, send = pl.pallas_call(
        functools.partial(node_backward, norm_scale),
        grid=(1,),
        in_specs=[SCALARS] + specs,
        out_specs=[whole(x.shape) for x in outs],
        out_shape=outs,
        scratch_shapes=[
            pltpu.VMEM((pay_early, width), BF), pltpu.VMEM(w_ffn_out.shape, BF), pltpu.VMEM(w_ffn_in.shape, BF),
            pltpu.VMEM(w_msg_out.shape, BF), pltpu.VMEM((width, width), BF), pltpu.SemaphoreType.DMA((4,)),
        ],
        compiler_params=params(48 if small else 56),
        name="node_backward",
    )(where, *operands)
    d_hiddens = send_shares([d_hidden] * shares)
    early, *d_hiddens = lax.optimization_barrier((chip_sum(keep, send), *d_hiddens))
    early_parts = to_owners(early)

    sent = (chips, late_rows + rows_own, width)
    keep, send, e_grad = pl.pallas_call(
        message_backward,
        grid=(steps,),
        in_specs=[SCALARS, edge_spec, per_step(per, (width_k, dest_rows, width)), flag_spec, edge_spec]
        + share_spec + [ANY] * 3 + [whole((8, width))]
        + [whole((8, edge_width)), whole((edge_width, edge_width)), whole((edge_width, edge_width))],
        out_specs=[whole(sent), whole(sent), edge_spec],
        out_shape=[vmem(small, sent, BF), vmem(small, sent, BF), sds(edges.shape, F32)],
        scratch_shapes=[
            pltpu.VMEM((dest_rows, width), F32), pltpu.VMEM((count, width), BF), pltpu.VMEM((nodes, width), F32),
            pltpu.VMEM((edge_width, width), F32), pltpu.VMEM((8, width), F32), pltpu.VMEM((pay_late, width), BF),
            pltpu.VMEM((half, width), BF), pltpu.VMEM((half, width), BF), pltpu.VMEM((edge_width, width), BF),
            pltpu.SemaphoreType.DMA((3,)),
        ],
        compiler_params=params(),
        cost_estimate=cost(13),
        name="message_backward",
    )(where, edges, f_slope, flags, d_sum, d_hiddens[0], *pin(small, *d_hiddens[1:]), w_msg_in, lo, hi, g_gains, g_gain3, g_in, g_out)
    late, early_parts = lax.optimization_barrier((chip_sum(keep, send), early_parts))
    late_parts = to_owners(late)
    dffn_lo = early_parts[:, early_rows:, :].reshape(half, width)
    dffn_hi = swap(dffn_lo, "c")

    tile = 256
    g_ffn_in, g_ffn_out = pl.pallas_call(
        ffn_grads,
        grid=(hidden_width // tile,),
        in_specs=[whole((half, width))] * 4
        + [pl.BlockSpec((width, tile), lambda i: (0, i)), pl.BlockSpec((tile, width), lambda i: (i, 0))],
        out_specs=[pl.BlockSpec((width, tile), lambda i: (0, i)), pl.BlockSpec((tile, width), lambda i: (i, 0))],
        out_shape=[sds(w_ffn_in.shape, F32), sds(w_ffn_out.shape, F32)],
        compiler_params=params(),
        cost_estimate=cost(18),
        name="ffn_grads",
    )(low_lo, low_hi, dffn_lo, dffn_hi, w_ffn_in, w_ffn_out)

    layers = lax.axis_size("z")
    plane = chips // layers
    mine = early_parts[:, :early_rows, :].astype(F32).sum(0).astype(BF)
    mine, late_parts, g_ffn_in, g_ffn_out = lax.optimization_barrier((mine, late_parts, g_ffn_in, g_ffn_out))
    spread = pl.pallas_call(
        functools.partial(finish_payload, late_rows),
        out_shape=sds((layers, early_rows + late_rows, width), BF),
        compiler_params=pltpu.CompilerParams(vmem_limit_bytes=(48 if small else 56) << 20),
        name="finish_payload",
    )(mine, *pin(small, late_parts))
    node_grad = pl.pallas_call(
        functools.partial(finish_nodes, late_rows),
        grid=(1,),
        in_specs=[whole(late_parts.shape), whole(n_grad.shape), part((width, width), 1, 0)],
        out_specs=whole(n_grad.shape),
        out_shape=sds(n_grad.shape, F32),
        compiler_params=params(48 if small else 56),
        name="finish_nodes",
    )(*pin(small, late_parts), n_grad, w_msg_in)
    layer = lax.all_to_all(spread, "z", 0, 0)
    same = lax.all_to_all(jnp.broadcast_to(layer[None], (plane,) + layer.shape), ("x", "y"), 0, 0)
    other = swap(same, "c")
    g_msg_in, g_msg_out, g_edge_t, g_edge_out, *vecs = pl.pallas_call(
        functools.partial(finish_weights, edge_width),
        in_specs=[SCALARS] + [pl.BlockSpec(memory_space=pltpu.VMEM)] * 2,
        out_shape=[
            sds(w_msg_in.shape, F32), sds((width, width), F32), sds(wei_t.shape, F32), sds((edge_width, edge_width), F32),
            sds((1, width), F32), sds((1, width), F32), sds((1, edge_width), F32), sds((1, width), F32),
        ],
        scratch_shapes=[pltpu.VMEM((pay_early, width), BF), pltpu.VMEM((pay_late, width), BF)],
        compiler_params=pltpu.CompilerParams(vmem_limit_bytes=(24 if small else 56) << 20),
        name="finish_weights",
    )(where, *pin(small, same, other))
    g_gain1, g_gain2, g_gain3, g_chain = (v.reshape(-1) for v in vecs)
    return (
        node_out, edge_new.transpose(1, 0, 2), node_grad, e_grad.transpose(1, 0, 2), g_msg_in, g_chain, g_msg_out,
        g_gain1, g_ffn_in, g_ffn_out, g_gain2, g_edge_t.T, g_edge_out, g_gain3,
    )


def solution(mesh):
    groups, shares = mesh.shape["res"], mesh.shape["edge"]
    fine = Mesh(mesh.devices.reshape(groups // 2, 2, shares // 2, 2), ("z", "x", "y", "c"))
    rows = P(("z", "x", "y", "c"), None)
    edges = P(("z", "x"), ("y", "c"), None)
    in_specs = (rows, edges, P(("z", "x"), ("y", "c"))) + (P(),) * 12 + (rows, edges)
    out_specs = (rows, edges, rows, edges) + (P(),) * 10
    return jax.shard_map(per_device, mesh=fine, in_specs=in_specs, out_specs=out_specs, check_vma=False)
```

```python
import functools
import math

import jax
import jax.numpy as jnp
from jax import lax
from jax.experimental import pallas as pl
from jax.experimental.pallas import tpu as pltpu
from jax.sharding import Mesh, PartitionSpec as P

EPS = 1e-05
CHIPS = ("z", "x", "y")
BF = jnp.bfloat16
F32 = jnp.float32
ROWS = 80
PIECE = 800
MOVED = 128
SPAN = 1280
RSQRT2 = math.sqrt(0.5)
INV_SQRT_2PI = 1.0 / math.sqrt(2.0 * math.pi)
PLACE, MASK, CROSS = 0, 1, 2


def mm(a, b):
    return jnp.dot(a, b, preferred_element_type=F32)


def mm_nt(a, b):
    return lax.dot_general(a, b, (((1,), (1,)), ((), ())), preferred_element_type=F32)


def mm_tn(a, b):
    return lax.dot_general(a, b, (((0,), (0,)), ((), ())), preferred_element_type=F32)


def gelu_pair(v):
    cdf = 0.5 * (1.0 + lax.erf(v * RSQRT2))
    pdf = INV_SQRT_2PI * jnp.exp(-0.5 * v * v)
    return v * cdf, cdf + v * pdf


def norm_parts(z):
    centre = z - jnp.mean(z, axis=-1, keepdims=True)
    r = lax.rsqrt(jnp.mean(centre * centre, axis=-1, keepdims=True) + EPS)
    return centre * r, r


def norm_back(n, r, gain, cot):
    b = cot * gain
    dz = r * (b - jnp.mean(b, -1, keepdims=True) - n * jnp.mean(b * n, -1, keepdims=True))
    return dz, jnp.sum(cot * n, axis=0, keepdims=True)


def gather_rows(place, halves):
    total = None
    for h, table in enumerate(halves):
        count = table.shape[0]
        block = min(count, SPAN)
        for start in range(0, count, block):
            lane = lax.broadcasted_iota(jnp.int32, (place.shape[0], block), 1) + (h * count + start)
            hot = jnp.where(lane == place, 1.0, 0.0).astype(BF)
            part = mm(hot, table[start : start + block, :])
            total = part if total is None else total + part
    return total


def scatter_rows(place_row, rows, acc):
    nodes = acc.shape[0]
    block = min(nodes, SPAN // 2)

    @pl.loop(0, nodes // block)
    def _(i):
        start = pl.multiple_of(i * block, block)
        row = lax.broadcasted_iota(jnp.int32, (block, place_row.shape[1]), 0) + start
        hot = jnp.where(row == place_row, 1.0, 0.0).astype(BF)
        acc[pl.ds(start, block), :] += mm(hot, rows)


def group_rows(where_ref, lo_ref, hi_ref, rows_own):
    group, core = where_ref[1], where_ref[2]
    start = pl.multiple_of(group * 2 * rows_own, 2 * rows_own)
    same = lo_ref[pl.ds(start, 2 * rows_own), :].astype(F32)
    other = hi_ref[pl.ds(start, 2 * rows_own), :].astype(F32)
    swapped = core == 1
    first = jnp.where(swapped, other, same)
    second = jnp.where(swapped, same, other)
    rows = [first[:rows_own], second[:rows_own], first[rows_own:], second[rows_own:]]
    return jnp.concatenate(rows, axis=0)


def put_shares(where_ref, refs, out):
    rows = refs[0].shape[0]
    shares = len(refs)
    for q, ref in enumerate(refs):
        at = lax.rem(where_ref[0] + shares - q, shares) * rows
        out[pl.ds(pl.multiple_of(at, 8), rows), :] = ref[...].astype(out.dtype)


def take_shares(where_ref, acc, refs):
    rows = refs[0].shape[0]
    shares = len(refs)
    for q, ref in enumerate(refs):
        at = lax.rem(where_ref[0] + q, shares) * rows
        ref[...] = acc[pl.ds(pl.multiple_of(at, 8), rows), :].astype(ref.dtype)


def add_up(refs):
    total = refs[0][...].astype(F32)
    for ref in refs[1:]:
        total += ref[...].astype(F32)
    return total


def message_forward(
    rows_own,
    where_ref, edge_ref, flags_ref, lo_ref, hi_ref, wmi_ref, chain_ref,
    slope_ref, s0, s1, s2, s3,
    table_lo, table_hi, own, acc, pre_s,
):
    step = pl.program_id(0)
    width = wmi_ref.shape[1]
    per, dest_rows, edge_width = edge_ref.shape
    edges = per * dest_rows

    @pl.when(step == 0)
    def _():
        weights = wmi_ref[width : 2 * width, :]
        half = lo_ref.shape[0]
        block = half // 2 if half <= SPAN else SPAN // 2

        @pl.loop(0, half // block)
        def _(i):
            at = pl.ds(pl.multiple_of(i * block, block), block)
            table_lo[at, :] = mm(lo_ref[at, :], weights).astype(BF)
            table_hi[at, :] = mm(hi_ref[at, :], weights).astype(BF)

        group = group_rows(where_ref, lo_ref, hi_ref, rows_own).astype(BF)
        own[...] = mm(group, wmi_ref[:width, :])
        acc[...] = jnp.zeros_like(acc)

    flags = jnp.transpose(flags_ref[0])[:edges, :]
    place = flags[:, PLACE : PLACE + 1].astype(jnp.int32)
    pre_s[...] = gather_rows(place, (table_lo, table_hi)) + mm(
        edge_ref[...].reshape(edges, edge_width), wmi_ref[2 * width :, :]
    )
    for j in range(per):
        for r in range(0, dest_rows, ROWS):
            at = slice(j * dest_rows + r, j * dest_rows + r + ROWS)
            mask = flags[at, MASK : MASK + 1]
            cross = flags[at, CROSS : CROSS + 1]
            pre = pre_s[at, :] + own[r : r + ROWS, :] + cross * chain_ref[...]
            hidden, slope = gelu_pair(pre)
            slope = slope * mask
            slope_ref[j, r : r + ROWS, :] = slope.astype(BF)
            acc[r : r + ROWS, :width] += hidden.astype(BF).astype(F32) * mask
            acc[r : r + ROWS, width:] += slope

    @pl.when(step == pl.num_programs(0) - 1)
    def _():
        take_shares(where_ref, acc, (s0, s1, s2, s3))


def start_copies(sources, targets, sems):
    copies = [pltpu.make_async_copy(s, t, sems.at[i]) for i, (s, t) in enumerate(zip(sources, targets))]
    for copy in copies:
        copy.start()
    return copies


def node_forward(
    norm_scale,
    s0, s1, s2, s3, node_ref, wmo_ref, gain1_ref, wfi_any, wfo_any, gain2_ref, weit_any,
    total_ref, slopes_ref, first_ref, second_ref, low_ref, fslope_ref, fhidden_ref, out_ref, src_ref, eown_ref,
    wfi_ref, wfo_ref, weit_ref, sems,
):
    copies = start_copies((wfi_any, wfo_any, weit_any), (wfi_ref, wfo_ref, weit_ref), sems)
    width = node_ref.shape[1]
    sums = add_up((s0, s1, s2, s3))
    total = sums[:, :width].astype(BF)
    total_ref[...] = total
    slopes_ref[...] = sums[:, width:]
    first_in = node_ref[...].astype(F32) + mm(total, wmo_ref[...]) * (1.0 / norm_scale)
    first_ref[...] = first_in
    norm_one = norm_parts(first_in)[0] * gain1_ref[...]
    low = norm_one.astype(BF)
    for i in range(low_ref.shape[0]):
        low_ref[i] = low
    copies[0].wait()
    hidden, slope = gelu_pair(mm(low, wfi_ref[...]))
    hidden = hidden.astype(BF)
    fslope_ref[...] = slope
    fhidden_ref[...] = hidden
    copies[1].wait()
    second_in = norm_one + mm(hidden, wfo_ref[...])
    second_ref[...] = second_in
    node_out = (norm_parts(second_in)[0] * gain2_ref[...]).astype(BF)
    out_ref[...] = node_out
    copies[2].wait()
    eown_ref[...] = mm_nt(node_out, weit_ref[:, :width]).astype(BF)
    src = mm_nt(node_out, weit_ref[:, width : 2 * width]).astype(BF)
    for i in range(src_ref.shape[0]):
        src_ref[i] = src


def edge_network(
    where_ref, edge_ref, cot_ref, flags_ref, lo_ref, hi_ref, e0, e1, e2, e3, weit_ref, weo_ref, gain_ref,
    out_ref, dsum_ref, slo_ref, shi_ref, o0, o1, o2, o3, gin_ref, gout_ref, ggain_ref,
    own, dpre_s, hidden_s, delta_s, out_s, dsum_s, acc, own_acc,
):
    step = pl.program_id(0)
    per, dest_rows, edge_width = edge_ref.shape
    edges = per * dest_rows
    width = (weit_ref.shape[1] - edge_width) // 2
    weights_t = weit_ref[:, 2 * width :]

    @pl.when(step == 0)
    def _():
        put_shares(where_ref, (e0, e1, e2, e3), own)
        for j in range(1, per):
            own[j * dest_rows : (j + 1) * dest_rows, :] = own[:dest_rows, :]
        acc[...] = jnp.zeros_like(acc)
        own_acc[...] = jnp.zeros_like(own_acc)
        gin_ref[...] = jnp.zeros_like(gin_ref)
        gout_ref[...] = jnp.zeros_like(gout_ref)
        ggain_ref[...] = jnp.zeros_like(ggain_ref)

    flags = jnp.transpose(flags_ref[0])[:edges, :]
    place = flags[:, PLACE : PLACE + 1].astype(jnp.int32)
    edge_all = edge_ref[...].reshape(edges, edge_width)
    cot_all = cot_ref[...].reshape(edges, edge_width)
    pre_all = gather_rows(place, (lo_ref, hi_ref)) + mm_nt(edge_all, weights_t) + own[...]
    gain = gain_ref[...]
    piece = PIECE if edges % PIECE == 0 else edges
    for start in range(0, edges, piece):
        at = slice(start, start + piece)
        mask = flags[at, MASK : MASK + 1]
        hidden, slope = gelu_pair(pre_all[at, :])
        hidden = (hidden * mask).astype(BF)
        hidden_s[at, :] = hidden
        n, r = norm_parts(edge_all[at, :].astype(F32) + mm(hidden, weo_ref[...]))
        out_s[at, :] = (n * gain).astype(BF)
        cot = cot_all[at, :].astype(F32)
        cn = cot * n
        ggain_ref[...] += jnp.sum(cn.reshape(piece // 8, 8, edge_width), axis=0)
        b = cot * gain
        dz = r * (b - jnp.mean(b, -1, keepdims=True) - n * jnp.mean(cn * gain, -1, keepdims=True))
        d_delta = (dz * mask).astype(BF)
        delta_s[at, :] = d_delta
        d_low = (slope * mm_nt(d_delta, weo_ref[...])).astype(BF)
        dpre_s[at, :] = d_low
        dsum_s[at, :] = (dz + mm(d_low, weights_t)).astype(BF)
    out_ref[...] = out_s[...].reshape(out_ref.shape)
    dsum_ref[...] = dsum_s[...].reshape(dsum_ref.shape)
    for j in range(per):
        own_acc[...] += dpre_s[j * dest_rows : (j + 1) * dest_rows, :].astype(F32)
    gout_ref[...] += mm_tn(hidden_s[...], delta_s[...])
    gin_ref[...] += mm_tn(edge_all, dpre_s[...])
    place_row = flags_ref[0, PLACE : PLACE + 1, :edges].astype(jnp.int32)
    scatter_rows(place_row, dpre_s[...], acc)

    @pl.when(step == pl.num_programs(0) - 1)
    def _():
        half = slo_ref.shape[0]
        slo_ref[...] = acc[:half, :].astype(BF)
        shi_ref[...] = acc[half:, :].astype(BF)
        take_shares(where_ref, own_acc, (o0, o1, o2, o3))


def node_backward(
    norm_scale,
    where_ref, parts_ref, o0, o1, o2, o3, node_ref, node_cot_ref, out_ref, first_ref, second_ref, fslope_ref,
    total_ref, slopes_ref, weit_ref, wmi_any, wfi_any, wfo_any, wmo_any, gain1_ref, gain2_ref,
    gin_any, gout_any,
    d_ref, ngrad_ref, ggain_ref, keep_ref, send_ref,
    pay, wfo_ref, wfi_ref, wmo_ref, wmi_ref, gin_ref, gout_ref, sems,
):
    width = out_ref.shape[1]
    own_rows = wmi_any.at[pl.ds(0, width), :]
    sources = (wfo_any, wfi_any, wmo_any, own_rows, gin_any, gout_any)
    copies = start_copies(sources, (wfo_ref, wfi_ref, wmo_ref, wmi_ref, gin_ref, gout_ref), sems)
    from_sources = add_up(tuple(parts_ref.at[i] for i in range(parts_ref.shape[0]))).astype(BF)
    from_own = add_up((o0, o1, o2, o3)).astype(BF)
    d_updated = (
        node_cot_ref[...].astype(F32)
        + mm(from_own, weit_ref[:, :width])
        + mm(from_sources, weit_ref[:, width : 2 * width])
    )
    node_out = out_ref[...]
    n, r = norm_parts(second_ref[...])
    d_second, ggain2 = norm_back(n, r, gain2_ref[...], d_updated)
    dffn = d_second.astype(BF)
    copies[0].wait()
    d_ffn_pre = (fslope_ref[...] * mm_nt(dffn, wfo_ref[...])).astype(BF)
    copies[1].wait()
    d_norm_one = d_second + mm_nt(d_ffn_pre, wfi_ref[...])
    n, r = norm_parts(first_ref[...])
    d_first, ggain1 = norm_back(n, r, gain1_ref[...], d_norm_one)
    d_summed = (d_first * (1.0 / norm_scale)).astype(BF)
    copies[2].wait()
    d_hidden = mm_nt(d_summed, wmo_ref[...])
    d_ref[...] = d_hidden.astype(BF)
    own_sum = (d_hidden * slopes_ref[...]).astype(BF)
    copies[3].wait()
    ngrad_ref[...] = d_first + mm_nt(own_sum, wmi_ref[...])
    ggain_ref[...] = jnp.concatenate([ggain1, ggain2, jnp.zeros((6, width), F32)], axis=0)
    parts = (
        mm_tn(total_ref[...], d_summed), mm_tn(node_ref[...], own_sum), mm_tn(from_own, node_out), mm_tn(from_sources, node_out)
    )
    at = 0
    for part in parts:
        pay[at : at + part.shape[0], :] = part.astype(BF)
        at += part.shape[0]
    copies[4].wait()
    copies[5].wait()
    edge_width = gin_ref.shape[1]
    spare = jnp.zeros((MOVED, width - 2 * edge_width), F32)
    pay[at : at + MOVED, :] = jnp.concatenate([gin_ref[:MOVED, :], gout_ref[:MOVED, :], spare], axis=1).astype(BF)
    at += MOVED
    if at < pay.shape[0]:
        pay[at:, :] = jnp.zeros((pay.shape[0] - at, width), BF)
    early = pay.shape[0] // 2 // keep_ref.shape[0]
    split_halves(where_ref, pay, early, keep_ref, send_ref)
    for i in range(keep_ref.shape[0]):
        keep_ref[i, early:, :] = dffn


def split_halves(where_ref, pay, rows, keep_ref, send_ref):
    half = pay.shape[0] // 2
    at = pl.multiple_of(where_ref[2] * half, 16)
    shape = (keep_ref.shape[0], rows, pay.shape[1])
    keep_ref[:, :rows, :] = pay[pl.ds(at, half), :].reshape(shape)
    send_ref[:, :rows, :] = pay[pl.ds(half - at, half), :].reshape(shape)


def message_backward(
    where_ref, edge_ref, slope_ref, flags_ref, dsum_ref, d0, d1, d2, d3, wmi_any, lo_any, hi_any, gain_ref, gain3_ref, gin_ref,
    gout_ref,
    keep_ref, send_ref, eg_ref,
    own, dpre_s, acc, gin, chain, pay, lo_ref, hi_ref, wme_ref, sems,
):
    step = pl.program_id(0)
    width = wme_ref.shape[1]
    per, dest_rows, edge_width = edge_ref.shape
    edges = per * dest_rows
    copy_w = pltpu.make_async_copy(wmi_any.at[pl.ds(2 * width, edge_width), :], wme_ref, sems.at[2])
    copy_lo = pltpu.make_async_copy(lo_any, lo_ref, sems.at[0])
    copy_hi = pltpu.make_async_copy(hi_any, hi_ref, sems.at[1])

    @pl.when(step == 0)
    def _():
        copy_w.start()
        copy_lo.start()
        copy_hi.start()
        put_shares(where_ref, (d0, d1, d2, d3), own)
        acc[...] = jnp.zeros_like(acc)
        gin[...] = jnp.zeros_like(gin)
        chain[...] = jnp.zeros_like(chain)

    flags = jnp.transpose(flags_ref[0])[:edges, :]
    for j in range(per):
        for r in range(0, dest_rows, ROWS):
            at = slice(j * dest_rows + r, j * dest_rows + r + ROWS)
            d_low = (slope_ref[j, r : r + ROWS, :].astype(F32) * own[r : r + ROWS, :]).astype(BF)
            dpre_s[at, :] = d_low
            crossed = d_low.astype(F32) * flags[at, CROSS : CROSS + 1]
            chain[...] += jnp.sum(crossed.reshape(ROWS // 8, 8, width), axis=0)
    @pl.when(step == 0)
    def _():
        copy_w.wait()

    d_all = dpre_s[...]
    gin[...] += mm_tn(edge_ref[...].reshape(edges, edge_width), d_all)
    back = mm_nt(d_all, wme_ref[...])
    for j in range(per):
        eg_ref[j] = dsum_ref[j].astype(F32) + back[j * dest_rows : (j + 1) * dest_rows, :]
    place_row = flags_ref[0, PLACE : PLACE + 1, :edges].astype(jnp.int32)
    scatter_rows(place_row, d_all, acc)

    @pl.when(step == pl.num_programs(0) - 1)
    def _():
        half = lo_ref.shape[0]
        chips = keep_ref.shape[0]
        rows = half // chips
        late = keep_ref.shape[1] - rows
        copy_lo.wait()
        copy_hi.wait()
        pay[:width, :] = mm_tn(lo_ref[...], acc[:half, :].astype(BF)) + mm_tn(hi_ref[...], acc[half:, :].astype(BF))
        pay[width : width + edge_width, :] = gin[...]
        at = width + edge_width
        pay[at:, :] = jnp.zeros((pay.shape[0] - at, width), F32)
        left = edge_width - MOVED
        pay[at : at + left, : 2 * edge_width] = jnp.concatenate([gin_ref[MOVED:, :], gout_ref[MOVED:, :]], axis=1)
        crossed = jnp.sum(chain[...], axis=0, keepdims=True)
        gain3 = jnp.sum(gain3_ref[...], axis=0, keepdims=True)
        gain3 = jnp.concatenate([gain3, jnp.zeros((1, width - edge_width), F32)], axis=1)
        lanes = width - 2 * edge_width
        for v, vec in enumerate((gain_ref[:1, :], gain_ref[1:2, :], gain3, crossed)):
            for q in range(width // lanes):
                line = at + v * (width // lanes) + q
                pay[line : line + 1, 2 * edge_width :] = vec[:, q * lanes : (q + 1) * lanes]
        half_pay = pay.shape[0] // 2
        core = where_ref[2]
        for chip in range(chips):
            mine = pay[pl.ds(pl.multiple_of(core * half_pay + chip * late, 8), late), :]
            other = pay[pl.ds(pl.multiple_of((1 - core) * half_pay + chip * late, 8), late), :]
            same_rows = acc[chip * rows : (chip + 1) * rows, :]
            other_rows = acc[half + chip * rows : half + (chip + 1) * rows, :]
            keep_ref[chip] = jnp.concatenate([mine, same_rows], axis=0).astype(BF)
            send_ref[chip] = jnp.concatenate([other, other_rows], axis=0).astype(BF)


def finish_nodes(late, parts_ref, ngrad_ref, wmi_ref, out_ref):
    total = add_up(tuple(parts_ref.at[i] for i in range(parts_ref.shape[0])))[late:, :]
    out_ref[...] = ngrad_ref[...] + mm_nt(total.astype(BF), wmi_ref[...])


def finish_payload(late, mine_ref, parts_ref, spread_ref):
    early = mine_ref.shape[0]
    other = add_up(tuple(parts_ref.at[i, :late, :] for i in range(parts_ref.shape[0]))).astype(BF)
    for i in range(spread_ref.shape[0]):
        spread_ref[i, :early, :] = mine_ref[...]
        spread_ref[i, early:, :] = other


def finish_weights(
    edge_width,
    where_ref, same_ref, other_ref,
    gmi_ref, gmo_ref, geit_ref, geo_ref, g1_ref, g2_ref, g3_ref, gchain_ref,
    early, late,
):
    width = gmi_ref.shape[1]
    plane, layers = same_ref.shape[:2]
    first = early.shape[0] // 2 // (plane * layers)
    second = late.shape[0] // 2 // (plane * layers)
    core = where_ref[2]
    for part, half in ((same_ref, core), (other_ref, 1 - core)):
        for p in range(plane):
            for z in range(layers):
                chip = half * plane * layers + z * plane + p
                early[pl.ds(pl.multiple_of(chip * first, 16), first), :] = part[p, z, :first, :]
                late[pl.ds(pl.multiple_of(chip * second, 8), second), :] = part[p, z, first:, :].astype(F32)
    gmo_ref[...] = early[:width, :].astype(F32)
    gmi_ref[:width, :] = early[width : 2 * width, :].astype(F32)
    gmi_ref[width:, :] = late[: width + edge_width, :]
    at = 2 * width
    geit_ref[:, :width] = early[at : at + edge_width, :].astype(F32)
    geit_ref[:, width : 2 * width] = early[at + edge_width : at + 2 * edge_width, :].astype(F32)
    at += 2 * edge_width
    line = width + edge_width
    moved = early[at : at + MOVED, : 2 * edge_width].astype(F32)
    small = jnp.concatenate([moved, late[line : line + edge_width - MOVED, : 2 * edge_width]], axis=0)
    geit_ref[:, 2 * width :] = jnp.transpose(small[:, :edge_width])
    geo_ref[...] = small[:, edge_width:]
    count = width // (width - 2 * edge_width)
    for v, ref in enumerate((g1_ref, g2_ref, g3_ref, gchain_ref)):
        vec = [late[line + v * count + q : line + v * count + q + 1, 2 * edge_width :] for q in range(count)]
        ref[...] = jnp.concatenate(vec, axis=1)[:, : ref.shape[1]]


def ffn_grads(llo_ref, lhi_ref, dlo_ref, dhi_ref, wfi_ref, wfo_ref, gfi_ref, gfo_ref):
    block = min(llo_ref.shape[0], SPAN // 2)
    gfi = gfo = None
    for low_ref, dffn_ref in ((llo_ref, dlo_ref), (lhi_ref, dhi_ref)):
        for start in range(0, low_ref.shape[0], block):
            low = low_ref[start : start + block, :]
            dffn = dffn_ref[start : start + block, :]
            hidden, slope = gelu_pair(mm(low, wfi_ref[...]))
            part = mm_tn(hidden.astype(BF), dffn)
            gfo = part if gfo is None else gfo + part
            d_pre = (slope * mm_nt(dffn, wfo_ref[...])).astype(BF)
            part = mm_tn(low, d_pre)
            gfi = part if gfi is None else gfi + part
    gfo_ref[...] = gfo
    gfi_ref[...] = gfi


def whole(shape):
    return pl.BlockSpec(tuple(shape), lambda *_: (0,) * len(shape))


def part(shape, *index):
    return pl.BlockSpec(tuple(shape), lambda *_: index or (0,) * len(shape))


def per_step(count, shape):
    return pl.BlockSpec((count,) + tuple(shape[1:]), lambda i: (i,) + (0,) * (len(shape) - 1))


SCALARS = pl.BlockSpec(memory_space=pltpu.SMEM)
ANY = pl.BlockSpec(memory_space=pl.ANY)


def params(limit=56):
    return pltpu.CompilerParams(vmem_limit_bytes=limit << 20, dimension_semantics=("arbitrary",))


def pin(small, *arrays):
    return [pltpu.with_memory_space_constraint(x, pltpu.VMEM) if small else x for x in arrays]


def stay(*arrays):
    return [pltpu.with_memory_space_constraint(x, pltpu.HBM) for x in arrays]


def vmem(small, shape, dtype):
    return pltpu.VMEM(tuple(shape), dtype) if small else sds(shape, dtype)


def sds(shape, dtype):
    return jax.ShapeDtypeStruct(tuple(shape), dtype)


def swap(x, axis):
    return lax.ppermute(x, axis, [(0, 1), (1, 0)])


def gather_spread(spread):
    same = lax.all_to_all(spread, CHIPS, 0, 0).reshape(-1, spread.shape[2])
    return same, swap(same, "c")


def scatter_halves(lo, hi):
    got = swap(hi, "c")
    both = (lo.astype(F32) + got.astype(F32)).astype(lo.dtype)
    return lax.all_to_all(both.reshape(lax.axis_size(CHIPS), -1, lo.shape[1]), CHIPS, 0, 0)


def send_shares(pieces):
    shares = len(pieces)
    got = [pieces[0]]
    for q in range(1, shares):
        got.append(lax.ppermute(pieces[q], ("y", "c"), [(s, (s + q) % shares) for s in range(shares)]))
    return got


def chip_sum(keep, send):
    got = jnp.pad(swap(send, "c"), ((0, 0), (0, keep.shape[1] - send.shape[1]), (0, 0)))
    return (keep.astype(F32) + got.astype(F32)).astype(keep.dtype)


def to_owners(both):
    return lax.all_to_all(both, CHIPS, 0, 0)


def cost(micros):
    return pl.CostEstimate(flops=int(micros * 1e9), bytes_accessed=int(micros * 1e6), transcendentals=0)


def per_device(
    node_in, edge_in, neighbors, chain_ids, residue_mask, w_msg_in, chain_vec, w_msg_out, gain_one,
    w_ffn_in, w_ffn_out, gain_two, w_edge_in, w_edge_out, gain_three, node_cot, edge_cot,
):
    dest_rows, width_k, edge_width = edge_in.shape
    rows_own, width = node_in.shape
    hidden_width = w_ffn_in.shape[1]
    nodes = chain_ids.shape[0]
    half = nodes // 2
    small = nodes <= 2 * SPAN
    chips = lax.axis_size(CHIPS)
    per = 5 if width_k % 5 == 0 else 1
    steps = width_k // per
    count = per * dest_rows
    lanes = count + (-count) % 128
    shares = dest_rows // rows_own
    norm_scale = math.sqrt(width_k * shares)
    me_core = lax.axis_index("c")
    share = lax.axis_index("y") * 2 + me_core
    group = lax.axis_index("z") * 2 + lax.axis_index("x")
    z, x, y = (lax.axis_index(axis) for axis in CHIPS)
    where = jnp.stack([share, group, me_core, z, x, y]).astype(jnp.int32)

    edges = edge_in.transpose(1, 0, 2)
    cots = edge_cot.transpose(1, 0, 2)
    lo, hi = gather_spread(jnp.broadcast_to(node_in[None], (chips,) + node_in.shape))

    first_row = group * dest_rows
    source = neighbors.T
    dest_chain = lax.dynamic_slice_in_dim(chain_ids, first_row, dest_rows)
    dest_mask = lax.dynamic_slice_in_dim(residue_mask, first_row, dest_rows)
    lower = jnp.sum((chain_ids[None, :] < dest_chain[:, None]).astype(jnp.int32), axis=1)
    upper = jnp.sum((chain_ids[None, :] <= dest_chain[:, None]).astype(jnp.int32), axis=1)
    bits = jnp.sum(residue_mask.reshape(nodes // 16, 16) << jnp.arange(16, dtype=jnp.int32)[None, :], axis=1)
    pick = (source >> 4)[:, :, None] == jnp.arange(nodes // 16, dtype=jnp.int32)[None, None, :]
    word = jnp.sum(jnp.where(pick, bits[None, None, :], 0), axis=2)
    present = (word >> (source & 15)) & 1
    pair_mask = (dest_mask[None, :] * present).astype(F32)
    cross = ((source < lower[None, :]) | (source >= upper[None, :])).astype(F32)
    block = source // rows_own
    place = ((block % 2) ^ me_core) * half + (block // 2) * rows_own + source % rows_own
    table = jnp.stack([place.astype(F32), pair_mask, cross]).reshape(3, steps, count).transpose(1, 0, 2)
    flags = jnp.pad(table, ((0, 0), (0, 5), (0, lanes - count)))

    row = lambda v: v.reshape(1, -1)
    wei_t = w_edge_in.T
    edge_spec = per_step(per, edges.shape)
    flag_spec = per_step(1, flags.shape)
    wide_spec = [whole((rows_own, 2 * width))] * shares
    wide_out = [sds((rows_own, 2 * width), BF)] * shares
    share_spec = [whole((rows_own, width))] * shares

    f_slope, *sums = pl.pallas_call(
        functools.partial(message_forward, rows_own),
        grid=(steps,),
        in_specs=[
            SCALARS, edge_spec, flag_spec, whole((half, width)), whole((half, width)), whole(w_msg_in.shape), whole((1, width)),
        ],
        out_specs=[per_step(per, (width_k, dest_rows, width))] + wide_spec,
        out_shape=[sds((width_k, dest_rows, width), BF)] + wide_out,
        scratch_shapes=[
            pltpu.VMEM((half, width), BF), pltpu.VMEM((half, width), BF), pltpu.VMEM((dest_rows, width), F32),
            pltpu.VMEM((dest_rows, 2 * width), F32), pltpu.VMEM((count, width), F32),
        ],
        compiler_params=params(),
        name="message_forward",
    )(where, edges, flags, *pin(small, lo, hi), w_msg_in, row(chain_vec))
    sums = send_shares(sums)

    total, slopes, first_in, second_in, low, ffn_slope, ffn_hidden, node_out, e_spread, e_own = pl.pallas_call(
        functools.partial(node_forward, norm_scale),
        out_shape=[
            sds((rows_own, width), BF), sds((rows_own, width), F32), sds((rows_own, width), F32), sds((rows_own, width), F32),
            sds((chips, rows_own, width), BF), sds((rows_own, hidden_width), F32), sds((rows_own, hidden_width), BF), sds((rows_own, width), BF),
            sds((chips, rows_own, edge_width), BF), sds((rows_own, edge_width), BF),
        ],
        in_specs=[pl.BlockSpec(memory_space=pltpu.VMEM)] * 7 + [ANY] * 2 + [pl.BlockSpec(memory_space=pltpu.VMEM), ANY],
        scratch_shapes=[
            pltpu.VMEM(w_ffn_in.shape, BF), pltpu.VMEM(w_ffn_out.shape, BF), pltpu.VMEM(wei_t.shape, BF),
            pltpu.SemaphoreType.DMA((3,)),
        ],
        compiler_params=pltpu.CompilerParams(vmem_limit_bytes=56 << 20),
        name="node_forward",
    )(sums[0], *pin(small, *sums[1:]), node_in, w_msg_out, row(gain_one), w_ffn_in, w_ffn_out, row(gain_two), wei_t)

    e_owns = send_shares([e_own] * shares)
    e_lo = lax.all_to_all(e_spread, CHIPS, 0, 0).reshape(-1, edge_width)
    e_lo, *e_owns = lax.optimization_barrier((e_lo, *e_owns))
    e_hi = swap(e_lo, "c")
    e_lo, low = lax.optimization_barrier((e_lo, low))
    low_lo = lax.all_to_all(low, CHIPS, 0, 0).reshape(half, width)

    edge_new, d_sum, e_slo, e_shi, *rest = pl.pallas_call(
        edge_network,
        grid=(steps,),
        in_specs=[SCALARS, edge_spec, edge_spec, flag_spec, whole((half, edge_width)), whole((half, edge_width))]
        + [whole((rows_own, edge_width))] * shares
        + [whole(wei_t.shape), whole(w_edge_out.shape), whole((1, edge_width))],
        out_specs=[edge_spec, edge_spec, whole((half, edge_width)), whole((half, edge_width))]
        + [whole((rows_own, edge_width))] * shares
        + [whole((edge_width, edge_width)), whole((edge_width, edge_width)), whole((8, edge_width))],
        out_shape=[sds(edges.shape, BF), sds(edges.shape, BF)] + [vmem(small, (half, edge_width), BF)] * 2
        + [sds((rows_own, edge_width), BF)] * shares
        + [sds((edge_width, edge_width), F32), sds((edge_width, edge_width), F32), sds((8, edge_width), F32)],
        scratch_shapes=[
            pltpu.VMEM((count, edge_width), F32), pltpu.VMEM((count, edge_width), BF), pltpu.VMEM((count, edge_width), BF),
            pltpu.VMEM((count, edge_width), BF), pltpu.VMEM((count, edge_width), BF), pltpu.VMEM((count, edge_width), BF), pltpu.VMEM((nodes, edge_width), F32), pltpu.VMEM((dest_rows, edge_width), F32),
        ],
        compiler_params=params(),
        cost_estimate=cost(22),
        name="edge_network",
    )(where, edges, cots, flags, *pin(small, e_lo, e_hi), e_owns[0], *pin(small, *e_owns[1:]), wei_t, w_edge_out, row(gain_three))
    g_in, g_out, g_gain3 = rest[shares:]
    e_slo, e_shi, low_lo, *e_sums = lax.optimization_barrier((e_slo, e_shi, low_lo, *rest[:shares]))
    low_hi = swap(low_lo, "c")
    e_sums = send_shares(e_sums)
    e_parts = scatter_halves(e_slo, e_shi)

    up = lambda rows: rows + (-rows) % (32 * chips)
    pay_early = up(2 * width + 2 * edge_width + MOVED)
    pay_late = width + 2 * edge_width - MOVED
    pay_late += (-pay_late) % (16 * chips)
    early_rows, late_rows = pay_early // (2 * chips), pay_late // (2 * chips)
    kept = (chips, early_rows + rows_own, width)
    operands = (
        *pin(small, e_parts), *stay(e_sums[0]), *pin(small, *e_sums[1:]), node_in, node_cot, node_out, first_in, second_in, ffn_slope, total, slopes,
        wei_t, w_msg_in, w_ffn_in, w_ffn_out, w_msg_out, row(gain_one), row(gain_two), *stay(g_in, g_out),
    )
    specs = [whole(x.shape) for x in operands]
    specs[13:18] = [part((edge_width, 2 * width))] + [ANY] * 4
    specs[-2:] = [ANY] * 2
    outs = [
        sds((rows_own, width), BF), sds((rows_own, width), F32), sds((8, width), F32), vmem(small, kept, BF),
        vmem(small, (chips, early_rows, width), BF),
    ]
    d_hidden, n_grad, g_gains, keep, send = pl.pallas_call(
        functools.partial(node_backward, norm_scale),
        grid=(1,),
        in_specs=[SCALARS] + specs,
        out_specs=[whole(x.shape) for x in outs],
        out_shape=outs,
        scratch_shapes=[
            pltpu.VMEM((pay_early, width), BF), pltpu.VMEM(w_ffn_out.shape, BF), pltpu.VMEM(w_ffn_in.shape, BF),
            pltpu.VMEM(w_msg_out.shape, BF), pltpu.VMEM((width, width), BF),
            pltpu.VMEM(g_in.shape, F32), pltpu.VMEM(g_out.shape, F32), pltpu.SemaphoreType.DMA((6,)),
        ],
        compiler_params=params(48 if small else 56),
        name="node_backward",
    )(where, *operands)
    d_hiddens = send_shares([d_hidden] * shares)
    early, *d_hiddens = lax.optimization_barrier((chip_sum(keep, send), *d_hiddens))
    early_parts = to_owners(early)

    sent = (chips, late_rows + rows_own, width)
    keep, send, e_grad = pl.pallas_call(
        message_backward,
        grid=(steps,),
        in_specs=[SCALARS, edge_spec, per_step(per, (width_k, dest_rows, width)), flag_spec, edge_spec]
        + share_spec + [ANY] * 3 + [whole((8, width))]
        + [whole((8, edge_width)), whole((edge_width, edge_width)), whole((edge_width, edge_width))],
        out_specs=[whole(sent), whole(sent), edge_spec],
        out_shape=[vmem(small, sent, BF), vmem(small, sent, BF), sds(edges.shape, F32)],
        scratch_shapes=[
            pltpu.VMEM((dest_rows, width), F32), pltpu.VMEM((count, width), BF), pltpu.VMEM((nodes, width), F32),
            pltpu.VMEM((edge_width, width), F32), pltpu.VMEM((8, width), F32), pltpu.VMEM((pay_late, width), F32),
            pltpu.VMEM((half, width), BF), pltpu.VMEM((half, width), BF), pltpu.VMEM((edge_width, width), BF),
            pltpu.SemaphoreType.DMA((3,)),
        ],
        compiler_params=params(),
        cost_estimate=cost(13),
        name="message_backward",
    )(where, edges, f_slope, flags, d_sum, d_hiddens[0], *pin(small, *d_hiddens[1:]), w_msg_in, lo, hi, g_gains, g_gain3, g_in, g_out)
    late, early_parts = lax.optimization_barrier((chip_sum(keep, send), early_parts))
    late_parts = to_owners(late)
    dffn_lo = early_parts[:, early_rows:, :].reshape(half, width)
    dffn_hi = swap(dffn_lo, "c")

    tile = 256
    g_ffn_in, g_ffn_out = pl.pallas_call(
        ffn_grads,
        grid=(hidden_width // tile,),
        in_specs=[whole((half, width))] * 4
        + [pl.BlockSpec((width, tile), lambda i: (0, i)), pl.BlockSpec((tile, width), lambda i: (i, 0))],
        out_specs=[pl.BlockSpec((width, tile), lambda i: (0, i)), pl.BlockSpec((tile, width), lambda i: (i, 0))],
        out_shape=[sds(w_ffn_in.shape, F32), sds(w_ffn_out.shape, F32)],
        compiler_params=params(),
        cost_estimate=cost(18),
        name="ffn_grads",
    )(low_lo, low_hi, dffn_lo, dffn_hi, w_ffn_in, w_ffn_out)

    layers = lax.axis_size("z")
    plane = chips // layers
    mine = early_parts[:, :early_rows, :].astype(F32).sum(0).astype(BF)
    mine, late_parts, g_ffn_in, g_ffn_out = lax.optimization_barrier((mine, late_parts, g_ffn_in, g_ffn_out))
    spread = pl.pallas_call(
        functools.partial(finish_payload, late_rows),
        out_shape=sds((layers, early_rows + late_rows, width), BF),
        compiler_params=pltpu.CompilerParams(vmem_limit_bytes=(48 if small else 56) << 20),
        name="finish_payload",
    )(mine, *pin(small, late_parts))
    node_grad = pl.pallas_call(
        functools.partial(finish_nodes, late_rows),
        grid=(1,),
        in_specs=[whole(late_parts.shape), whole(n_grad.shape), part((width, width), 1, 0)],
        out_specs=whole(n_grad.shape),
        out_shape=sds(n_grad.shape, F32),
        compiler_params=params(48 if small else 56),
        name="finish_nodes",
    )(*pin(small, late_parts), n_grad, w_msg_in)
    layer = lax.all_to_all(spread, "z", 0, 0)
    same = lax.all_to_all(jnp.broadcast_to(layer[None], (plane,) + layer.shape), ("x", "y"), 0, 0)
    other = swap(same, "c")
    g_msg_in, g_msg_out, g_edge_t, g_edge_out, *vecs = pl.pallas_call(
        functools.partial(finish_weights, edge_width),
        in_specs=[SCALARS] + [pl.BlockSpec(memory_space=pltpu.VMEM)] * 2,
        out_shape=[
            sds(w_msg_in.shape, F32), sds((width, width), F32), sds(wei_t.shape, F32), sds((edge_width, edge_width), F32),
            sds((1, width), F32), sds((1, width), F32), sds((1, edge_width), F32), sds((1, width), F32),
        ],
        scratch_shapes=[pltpu.VMEM((pay_early, width), BF), pltpu.VMEM((pay_late, width), F32)],
        compiler_params=pltpu.CompilerParams(vmem_limit_bytes=(24 if small else 56) << 20),
        name="finish_weights",
    )(where, *pin(small, same, other))
    g_gain1, g_gain2, g_gain3, g_chain = (v.reshape(-1) for v in vecs)
    return (
        node_out, edge_new.transpose(1, 0, 2), node_grad, e_grad.transpose(1, 0, 2), g_msg_in, g_chain, g_msg_out,
        g_gain1, g_ffn_in, g_ffn_out, g_gain2, g_edge_t.T, g_edge_out, g_gain3,
    )


def solution(mesh):
    groups, shares = mesh.shape["res"], mesh.shape["edge"]
    fine = Mesh(mesh.devices.reshape(groups // 2, 2, shares // 2, 2), ("z", "x", "y", "c"))
    rows = P(("z", "x", "y", "c"), None)
    edges = P(("z", "x"), ("y", "c"), None)
    in_specs = (rows, edges, P(("z", "x"), ("y", "c"))) + (P(),) * 12 + (rows, edges)
    out_specs = (rows, edges, rows, edges) + (P(),) * 10
    return jax.shard_map(per_device, mesh=fine, in_specs=in_specs, out_specs=out_specs, check_vma=False)
```

```python
import functools
import math

import jax
import jax.numpy as jnp
from jax import lax
from jax.experimental import pallas as pl
from jax.experimental.pallas import tpu as pltpu
from jax.sharding import Mesh, PartitionSpec as P

EPS = 1e-05
CHIPS = ("z", "x", "y")
BF = jnp.bfloat16
F32 = jnp.float32
ROWS = 80
PIECE = 800
MOVED = 128
SPAN = 1280
RSQRT2 = math.sqrt(0.5)
INV_SQRT_2PI = 1.0 / math.sqrt(2.0 * math.pi)
PLACE, MASK, CROSS = 0, 1, 2


def mm(a, b):
    return jnp.dot(a, b, preferred_element_type=F32)


def mm_nt(a, b):
    return lax.dot_general(a, b, (((1,), (1,)), ((), ())), preferred_element_type=F32)


def mm_tn(a, b):
    return lax.dot_general(a, b, (((0,), (0,)), ((), ())), preferred_element_type=F32)


def gelu_pair(v):
    cdf = 0.5 * (1.0 + lax.erf(v * RSQRT2))
    pdf = INV_SQRT_2PI * jnp.exp(-0.5 * v * v)
    return v * cdf, cdf + v * pdf


def norm_parts(z):
    centre = z - jnp.mean(z, axis=-1, keepdims=True)
    r = lax.rsqrt(jnp.mean(centre * centre, axis=-1, keepdims=True) + EPS)
    return centre * r, r


def norm_back(n, r, gain, cot):
    b = cot * gain
    dz = r * (b - jnp.mean(b, -1, keepdims=True) - n * jnp.mean(b * n, -1, keepdims=True))
    return dz, jnp.sum(cot * n, axis=0, keepdims=True)


def gather_rows(place, halves):
    total = None
    for h, table in enumerate(halves):
        count = table.shape[0]
        block = min(count, SPAN)
        for start in range(0, count, block):
            lane = lax.broadcasted_iota(jnp.int32, (place.shape[0], block), 1) + (h * count + start)
            hot = jnp.where(lane == place, 1.0, 0.0).astype(BF)
            part = mm(hot, table[start : start + block, :])
            total = part if total is None else total + part
    return total


def scatter_rows(place_row, rows, acc):
    nodes = acc.shape[0]
    block = min(nodes, SPAN // 2)

    @pl.loop(0, nodes // block)
    def _(i):
        start = pl.multiple_of(i * block, block)
        row = lax.broadcasted_iota(jnp.int32, (block, place_row.shape[1]), 0) + start
        hot = jnp.where(row == place_row, 1.0, 0.0).astype(BF)
        acc[pl.ds(start, block), :] += mm(hot, rows)


def group_rows(where_ref, lo_ref, hi_ref, rows_own):
    group, core = where_ref[1], where_ref[2]
    start = pl.multiple_of(group * 2 * rows_own, 2 * rows_own)
    same = lo_ref[pl.ds(start, 2 * rows_own), :].astype(F32)
    other = hi_ref[pl.ds(start, 2 * rows_own), :].astype(F32)
    swapped = core == 1
    first = jnp.where(swapped, other, same)
    second = jnp.where(swapped, same, other)
    rows = [first[:rows_own], second[:rows_own], first[rows_own:], second[rows_own:]]
    return jnp.concatenate(rows, axis=0)


def put_shares(where_ref, refs, out):
    rows = refs[0].shape[0]
    shares = len(refs)
    for q, ref in enumerate(refs):
        at = lax.rem(where_ref[0] + shares - q, shares) * rows
        out[pl.ds(pl.multiple_of(at, 8), rows), :] = ref[...].astype(out.dtype)


def take_shares(where_ref, acc, refs):
    rows = refs[0].shape[0]
    shares = len(refs)
    for q, ref in enumerate(refs):
        at = lax.rem(where_ref[0] + q, shares) * rows
        ref[...] = acc[pl.ds(pl.multiple_of(at, 8), rows), :].astype(ref.dtype)


def add_up(refs):
    total = refs[0][...].astype(F32)
    for ref in refs[1:]:
        total += ref[...].astype(F32)
    return total


def message_forward(
    rows_own,
    where_ref, edge_ref, flags_ref, lo_ref, hi_ref, wmi_ref, chain_ref,
    slope_ref, s0, s1, s2, s3,
    table_lo, table_hi, own, acc, pre_s,
):
    step = pl.program_id(0)
    width = wmi_ref.shape[1]
    per, dest_rows, edge_width = edge_ref.shape
    edges = per * dest_rows

    @pl.when(step == 0)
    def _():
        weights = wmi_ref[width : 2 * width, :]
        half = lo_ref.shape[0]
        block = half // 2 if half <= SPAN else SPAN // 2

        @pl.loop(0, half // block)
        def _(i):
            at = pl.ds(pl.multiple_of(i * block, block), block)
            table_lo[at, :] = mm(lo_ref[at, :], weights).astype(BF)
            table_hi[at, :] = mm(hi_ref[at, :], weights).astype(BF)

        group = group_rows(where_ref, lo_ref, hi_ref, rows_own).astype(BF)
        own[...] = mm(group, wmi_ref[:width, :])
        acc[...] = jnp.zeros_like(acc)

    flags = jnp.transpose(flags_ref[0])[:edges, :]
    place = flags[:, PLACE : PLACE + 1].astype(jnp.int32)
    pre_s[...] = gather_rows(place, (table_lo, table_hi)) + mm(
        edge_ref[...].reshape(edges, edge_width), wmi_ref[2 * width :, :]
    )
    for j in range(per):
        for r in range(0, dest_rows, ROWS):
            at = slice(j * dest_rows + r, j * dest_rows + r + ROWS)
            mask = flags[at, MASK : MASK + 1]
            cross = flags[at, CROSS : CROSS + 1]
            pre = pre_s[at, :] + own[r : r + ROWS, :] + cross * chain_ref[...]
            hidden, slope = gelu_pair(pre)
            slope = slope * mask
            slope_ref[j, r : r + ROWS, :] = slope.astype(BF)
            acc[r : r + ROWS, :width] += hidden.astype(BF).astype(F32) * mask
            acc[r : r + ROWS, width:] += slope

    @pl.when(step == pl.num_programs(0) - 1)
    def _():
        take_shares(where_ref, acc, (s0, s1, s2, s3))


def start_copies(sources, targets, sems):
    copies = [pltpu.make_async_copy(s, t, sems.at[i]) for i, (s, t) in enumerate(zip(sources, targets))]
    for copy in copies:
        copy.start()
    return copies


def node_forward(
    norm_scale,
    s0, s1, s2, s3, node_ref, wmo_ref, gain1_ref, wfi_any, wfo_any, gain2_ref, weit_any,
    total_ref, slopes_ref, first_ref, second_ref, low_ref, fslope_ref, fhidden_ref, out_ref, src_ref, eown_ref,
    wfi_ref, wfo_ref, weit_ref, sems,
):
    copies = start_copies((wfi_any, wfo_any, weit_any), (wfi_ref, wfo_ref, weit_ref), sems)
    width = node_ref.shape[1]
    sums = add_up((s0, s1, s2, s3))
    total = sums[:, :width].astype(BF)
    total_ref[...] = total
    slopes_ref[...] = sums[:, width:]
    first_in = node_ref[...].astype(F32) + mm(total, wmo_ref[...]) * (1.0 / norm_scale)
    first_ref[...] = first_in
    norm_one = norm_parts(first_in)[0] * gain1_ref[...]
    low = norm_one.astype(BF)
    for i in range(low_ref.shape[0]):
        low_ref[i] = low
    copies[0].wait()
    hidden, slope = gelu_pair(mm(low, wfi_ref[...]))
    hidden = hidden.astype(BF)
    fslope_ref[...] = slope
    fhidden_ref[...] = hidden
    copies[1].wait()
    second_in = norm_one + mm(hidden, wfo_ref[...])
    second_ref[...] = second_in
    node_out = (norm_parts(second_in)[0] * gain2_ref[...]).astype(BF)
    out_ref[...] = node_out
    copies[2].wait()
    eown_ref[...] = mm_nt(node_out, weit_ref[:, :width]).astype(BF)
    src = mm_nt(node_out, weit_ref[:, width : 2 * width]).astype(BF)
    for i in range(src_ref.shape[0]):
        src_ref[i] = src


def edge_network(
    where_ref, edge_ref, cot_ref, flags_ref, lo_ref, hi_ref, e0, e1, e2, e3, weit_ref, weo_ref, gain_ref,
    out_ref, dsum_ref, slo_ref, shi_ref, o0, o1, o2, o3, gin_ref, gout_ref, ggain_ref,
    own, dpre_s, hidden_s, delta_s, out_s, dsum_s, acc, own_acc,
):
    step = pl.program_id(0)
    per, dest_rows, edge_width = edge_ref.shape
    edges = per * dest_rows
    width = (weit_ref.shape[1] - edge_width) // 2
    weights_t = weit_ref[:, 2 * width :]

    @pl.when(step == 0)
    def _():
        put_shares(where_ref, (e0, e1, e2, e3), own)
        for j in range(1, per):
            own[j * dest_rows : (j + 1) * dest_rows, :] = own[:dest_rows, :]
        acc[...] = jnp.zeros_like(acc)
        own_acc[...] = jnp.zeros_like(own_acc)
        gin_ref[...] = jnp.zeros_like(gin_ref)
        gout_ref[...] = jnp.zeros_like(gout_ref)
        ggain_ref[...] = jnp.zeros_like(ggain_ref)

    flags = jnp.transpose(flags_ref[0])[:edges, :]
    place = flags[:, PLACE : PLACE + 1].astype(jnp.int32)
    edge_all = edge_ref[...].reshape(edges, edge_width)
    cot_all = cot_ref[...].reshape(edges, edge_width)
    pre_all = gather_rows(place, (lo_ref, hi_ref)) + mm_nt(edge_all, weights_t) + own[...]
    gain = gain_ref[...]
    piece = PIECE if edges % PIECE == 0 else edges
    for start in range(0, edges, piece):
        at = slice(start, start + piece)
        mask = flags[at, MASK : MASK + 1]
        hidden, slope = gelu_pair(pre_all[at, :])
        hidden = (hidden * mask).astype(BF)
        hidden_s[at, :] = hidden
        n, r = norm_parts(edge_all[at, :].astype(F32) + mm(hidden, weo_ref[...]))
        out_s[at, :] = (n * gain).astype(BF)
        cot = cot_all[at, :].astype(F32)
        cn = cot * n
        ggain_ref[...] += jnp.sum(cn.reshape(piece // 8, 8, edge_width), axis=0)
        b = cot * gain
        dz = r * (b - jnp.mean(b, -1, keepdims=True) - n * jnp.mean(cn * gain, -1, keepdims=True))
        d_delta = (dz * mask).astype(BF)
        delta_s[at, :] = d_delta
        d_low = (slope * mm_nt(d_delta, weo_ref[...])).astype(BF)
        dpre_s[at, :] = d_low
        dsum_s[at, :] = (dz + mm(d_low, weights_t)).astype(BF)
    out_ref[...] = out_s[...].reshape(out_ref.shape)
    dsum_ref[...] = dsum_s[...].reshape(dsum_ref.shape)
    for j in range(per):
        own_acc[...] += dpre_s[j * dest_rows : (j + 1) * dest_rows, :].astype(F32)
    gout_ref[...] += mm_tn(hidden_s[...], delta_s[...])
    gin_ref[...] += mm_tn(edge_all, dpre_s[...])
    place_row = flags_ref[0, PLACE : PLACE + 1, :edges].astype(jnp.int32)
    scatter_rows(place_row, dpre_s[...], acc)

    @pl.when(step == pl.num_programs(0) - 1)
    def _():
        half = slo_ref.shape[0]
        slo_ref[...] = acc[:half, :].astype(BF)
        shi_ref[...] = acc[half:, :].astype(BF)
        take_shares(where_ref, own_acc, (o0, o1, o2, o3))


def node_backward(
    norm_scale,
    where_ref, parts_ref, o0, o1, o2, o3, node_ref, node_cot_ref, out_ref, first_ref, second_ref, fslope_ref,
    total_ref, slopes_ref, weit_ref, wmi_any, wfi_any, wfo_any, wmo_any, gain1_ref, gain2_ref,
    gin_any, gout_any,
    d_ref, ngrad_ref, ggain_ref, keep_ref, send_ref,
    pay, wfo_ref, wfi_ref, wmo_ref, wmi_ref, gin_ref, gout_ref, sems,
):
    width = out_ref.shape[1]
    own_rows = wmi_any.at[pl.ds(0, width), :]
    sources = (wfo_any, wfi_any, wmo_any, own_rows, gin_any, gout_any)
    copies = start_copies(sources, (wfo_ref, wfi_ref, wmo_ref, wmi_ref, gin_ref, gout_ref), sems)
    from_sources = add_up(tuple(parts_ref.at[i] for i in range(parts_ref.shape[0]))).astype(BF)
    from_own = add_up((o0, o1, o2, o3)).astype(BF)
    d_updated = (
        node_cot_ref[...].astype(F32)
        + mm(from_own, weit_ref[:, :width])
        + mm(from_sources, weit_ref[:, width : 2 * width])
    )
    node_out = out_ref[...]
    n, r = norm_parts(second_ref[...])
    d_second, ggain2 = norm_back(n, r, gain2_ref[...], d_updated)
    dffn = d_second.astype(BF)
    copies[0].wait()
    d_ffn_pre = (fslope_ref[...] * mm_nt(dffn, wfo_ref[...])).astype(BF)
    copies[1].wait()
    d_norm_one = d_second + mm_nt(d_ffn_pre, wfi_ref[...])
    n, r = norm_parts(first_ref[...])
    d_first, ggain1 = norm_back(n, r, gain1_ref[...], d_norm_one)
    d_summed = (d_first * (1.0 / norm_scale)).astype(BF)
    copies[2].wait()
    d_hidden = mm_nt(d_summed, wmo_ref[...])
    d_ref[...] = d_hidden.astype(BF)
    own_sum = (d_hidden * slopes_ref[...]).astype(BF)
    copies[3].wait()
    ngrad_ref[...] = d_first + mm_nt(own_sum, wmi_ref[...])
    ggain_ref[...] = jnp.concatenate([ggain1, ggain2, jnp.zeros((6, width), F32)], axis=0)
    parts = (
        mm_tn(total_ref[...], d_summed), mm_tn(node_ref[...], own_sum), mm_tn(from_own, node_out), mm_tn(from_sources, node_out)
    )
    at = 0
    for part in parts:
        pay[at : at + part.shape[0], :] = part.astype(BF)
        at += part.shape[0]
    copies[4].wait()
    copies[5].wait()
    edge_width = gin_ref.shape[1]
    spare = jnp.zeros((MOVED, width - 2 * edge_width), F32)
    pay[at : at + MOVED, :] = jnp.concatenate([gin_ref[:MOVED, :], gout_ref[:MOVED, :], spare], axis=1).astype(BF)
    at += MOVED
    if at < pay.shape[0]:
        pay[at:, :] = jnp.zeros((pay.shape[0] - at, width), BF)
    early = pay.shape[0] // 2 // keep_ref.shape[0]
    split_halves(where_ref, pay, early, keep_ref, send_ref)
    for i in range(keep_ref.shape[0]):
        keep_ref[i, early:, :] = dffn


def split_halves(where_ref, pay, rows, keep_ref, send_ref):
    half = pay.shape[0] // 2
    at = pl.multiple_of(where_ref[2] * half, 16)
    shape = (keep_ref.shape[0], rows, pay.shape[1])
    keep_ref[:, :rows, :] = pay[pl.ds(at, half), :].reshape(shape)
    send_ref[:, :rows, :] = pay[pl.ds(half - at, half), :].reshape(shape)


def message_backward(
    where_ref, edge_ref, slope_ref, flags_ref, dsum_ref, d0, d1, d2, d3, wmi_any, lo_any, hi_any, gain_ref, gain3_ref, gin_ref,
    gout_ref,
    keep_ref, send_ref, eg_ref,
    own, dpre_s, acc, gin, chain, pay, lo_ref, hi_ref, wme_ref, sems,
):
    step = pl.program_id(0)
    width = wme_ref.shape[1]
    per, dest_rows, edge_width = edge_ref.shape
    edges = per * dest_rows
    copy_w = pltpu.make_async_copy(wmi_any.at[pl.ds(2 * width, edge_width), :], wme_ref, sems.at[2])
    copy_lo = pltpu.make_async_copy(lo_any, lo_ref, sems.at[0])
    copy_hi = pltpu.make_async_copy(hi_any, hi_ref, sems.at[1])

    @pl.when(step == 0)
    def _():
        copy_w.start()
        copy_lo.start()
        copy_hi.start()
        put_shares(where_ref, (d0, d1, d2, d3), own)
        acc[...] = jnp.zeros_like(acc)
        gin[...] = jnp.zeros_like(gin)
        chain[...] = jnp.zeros_like(chain)

    flags = jnp.transpose(flags_ref[0])[:edges, :]
    for j in range(per):
        for r in range(0, dest_rows, ROWS):
            at = slice(j * dest_rows + r, j * dest_rows + r + ROWS)
            d_low = (slope_ref[j, r : r + ROWS, :].astype(F32) * own[r : r + ROWS, :]).astype(BF)
            dpre_s[at, :] = d_low
            crossed = d_low.astype(F32) * flags[at, CROSS : CROSS + 1]
            chain[...] += jnp.sum(crossed.reshape(ROWS // 8, 8, width), axis=0)
    @pl.when(step == 0)
    def _():
        copy_w.wait()

    d_all = dpre_s[...]
    gin[...] += mm_tn(edge_ref[...].reshape(edges, edge_width), d_all)
    back = mm_nt(d_all, wme_ref[...])
    for j in range(per):
        eg_ref[j] = dsum_ref[j].astype(F32) + back[j * dest_rows : (j + 1) * dest_rows, :]
    place_row = flags_ref[0, PLACE : PLACE + 1, :edges].astype(jnp.int32)
    scatter_rows(place_row, d_all, acc)

    @pl.when(step == pl.num_programs(0) - 1)
    def _():
        half = lo_ref.shape[0]
        chips = keep_ref.shape[0]
        rows = half // chips
        late = keep_ref.shape[1] - rows
        copy_lo.wait()
        copy_hi.wait()
        pay[:width, :] = mm_tn(lo_ref[...], acc[:half, :].astype(BF)) + mm_tn(hi_ref[...], acc[half:, :].astype(BF))
        pay[width : width + edge_width, :] = gin[...]
        at = width + edge_width
        pay[at:, :] = jnp.zeros((pay.shape[0] - at, width), F32)
        left = edge_width - MOVED
        pay[at : at + left, : 2 * edge_width] = jnp.concatenate([gin_ref[MOVED:, :], gout_ref[MOVED:, :]], axis=1)
        crossed = jnp.sum(chain[...], axis=0, keepdims=True)
        gain3 = jnp.sum(gain3_ref[...], axis=0, keepdims=True)
        gain3 = jnp.concatenate([gain3, jnp.zeros((1, width - edge_width), F32)], axis=1)
        lanes = width - 2 * edge_width
        for v, vec in enumerate((gain_ref[:1, :], gain_ref[1:2, :], gain3, crossed)):
            for q in range(width // lanes):
                line = at + v * (width // lanes) + q
                pay[line : line + 1, 2 * edge_width :] = vec[:, q * lanes : (q + 1) * lanes]
        half_pay = pay.shape[0] // 2
        core = where_ref[2]
        for chip in range(chips):
            mine = pay[pl.ds(pl.multiple_of(core * half_pay + chip * late, 8), late), :]
            other = pay[pl.ds(pl.multiple_of((1 - core) * half_pay + chip * late, 8), late), :]
            same_rows = acc[chip * rows : (chip + 1) * rows, :]
            other_rows = acc[half + chip * rows : half + (chip + 1) * rows, :]
            keep_ref[chip] = jnp.concatenate([mine, same_rows], axis=0).astype(BF)
            send_ref[chip] = jnp.concatenate([other, other_rows], axis=0).astype(BF)


def finish_nodes(late, parts_ref, ngrad_ref, wmi_ref, out_ref):
    total = add_up(tuple(parts_ref.at[i] for i in range(parts_ref.shape[0])))[late:, :]
    out_ref[...] = ngrad_ref[...] + mm_nt(total.astype(BF), wmi_ref[...])


def finish_payload(late, mine_ref, parts_ref, spread_ref):
    early = mine_ref.shape[0]
    other = add_up(tuple(parts_ref.at[i, :late, :] for i in range(parts_ref.shape[0]))).astype(BF)
    for i in range(spread_ref.shape[0]):
        spread_ref[i, :early, :] = mine_ref[...]
        spread_ref[i, early:, :] = other


def place_layers(where_ref, *refs):
    out_ref = refs[-1]
    for k, ref in enumerate(refs[:-1]):
        z = lax.rem(where_ref[3] + k, out_ref.shape[1])
        for p in range(out_ref.shape[0]):
            out_ref[p, z] = ref[...]


def finish_weights(
    edge_width,
    where_ref, same_ref, other_ref,
    gmi_ref, gmo_ref, geit_ref, geo_ref, g1_ref, g2_ref, g3_ref, gchain_ref,
    early, late,
):
    width = gmi_ref.shape[1]
    plane, layers = same_ref.shape[:2]
    first = early.shape[0] // 2 // (plane * layers)
    second = late.shape[0] // 2 // (plane * layers)
    core = where_ref[2]
    for part, half in ((same_ref, core), (other_ref, 1 - core)):
        for p in range(plane):
            for z in range(layers):
                chip = half * plane * layers + z * plane + p
                early[pl.ds(pl.multiple_of(chip * first, 16), first), :] = part[p, z, :first, :]
                late[pl.ds(pl.multiple_of(chip * second, 8), second), :] = part[p, z, first:, :].astype(F32)
    gmo_ref[...] = early[:width, :].astype(F32)
    gmi_ref[:width, :] = early[width : 2 * width, :].astype(F32)
    gmi_ref[width:, :] = late[: width + edge_width, :]
    at = 2 * width
    geit_ref[:, :width] = early[at : at + edge_width, :].astype(F32)
    geit_ref[:, width : 2 * width] = early[at + edge_width : at + 2 * edge_width, :].astype(F32)
    at += 2 * edge_width
    line = width + edge_width
    moved = early[at : at + MOVED, : 2 * edge_width].astype(F32)
    small = jnp.concatenate([moved, late[line : line + edge_width - MOVED, : 2 * edge_width]], axis=0)
    geit_ref[:, 2 * width :] = jnp.transpose(small[:, :edge_width])
    geo_ref[...] = small[:, edge_width:]
    count = width // (width - 2 * edge_width)
    for v, ref in enumerate((g1_ref, g2_ref, g3_ref, gchain_ref)):
        vec = [late[line + v * count + q : line + v * count + q + 1, 2 * edge_width :] for q in range(count)]
        ref[...] = jnp.concatenate(vec, axis=1)[:, : ref.shape[1]]


def ffn_grads(llo_ref, lhi_ref, dlo_ref, dhi_ref, wfi_ref, wfo_ref, gfi_ref, gfo_ref):
    block = min(llo_ref.shape[0], SPAN // 2)
    gfi = gfo = None
    for low_ref, dffn_ref in ((llo_ref, dlo_ref), (lhi_ref, dhi_ref)):
        for start in range(0, low_ref.shape[0], block):
            low = low_ref[start : start + block, :]
            dffn = dffn_ref[start : start + block, :]
            hidden, slope = gelu_pair(mm(low, wfi_ref[...]))
            part = mm_tn(hidden.astype(BF), dffn)
            gfo = part if gfo is None else gfo + part
            d_pre = (slope * mm_nt(dffn, wfo_ref[...])).astype(BF)
            part = mm_tn(low, d_pre)
            gfi = part if gfi is None else gfi + part
    gfo_ref[...] = gfo
    gfi_ref[...] = gfi


def whole(shape):
    return pl.BlockSpec(tuple(shape), lambda *_: (0,) * len(shape))


def part(shape, *index):
    return pl.BlockSpec(tuple(shape), lambda *_: index or (0,) * len(shape))


def per_step(count, shape):
    return pl.BlockSpec((count,) + tuple(shape[1:]), lambda i: (i,) + (0,) * (len(shape) - 1))


SCALARS = pl.BlockSpec(memory_space=pltpu.SMEM)
ANY = pl.BlockSpec(memory_space=pl.ANY)


def params(limit=56):
    return pltpu.CompilerParams(vmem_limit_bytes=limit << 20, dimension_semantics=("arbitrary",))


def pin(small, *arrays):
    return [pltpu.with_memory_space_constraint(x, pltpu.VMEM) if small else x for x in arrays]


def stay(*arrays):
    return [pltpu.with_memory_space_constraint(x, pltpu.HBM) for x in arrays]


def vmem(small, shape, dtype):
    return pltpu.VMEM(tuple(shape), dtype) if small else sds(shape, dtype)


def sds(shape, dtype):
    return jax.ShapeDtypeStruct(tuple(shape), dtype)


def swap(x, axis):
    return lax.ppermute(x, axis, [(0, 1), (1, 0)])


def gather_spread(spread):
    same = lax.all_to_all(spread, CHIPS, 0, 0).reshape(-1, spread.shape[2])
    return same, swap(same, "c")


def scatter_halves(lo, hi):
    got = swap(hi, "c")
    both = (lo.astype(F32) + got.astype(F32)).astype(lo.dtype)
    return lax.all_to_all(both.reshape(lax.axis_size(CHIPS), -1, lo.shape[1]), CHIPS, 0, 0)


def send_shares(pieces):
    shares = len(pieces)
    got = [pieces[0]]
    for q in range(1, shares):
        got.append(lax.ppermute(pieces[q], ("y", "c"), [(s, (s + q) % shares) for s in range(shares)]))
    return got


def chip_sum(keep, send):
    got = jnp.pad(swap(send, "c"), ((0, 0), (0, keep.shape[1] - send.shape[1]), (0, 0)))
    return (keep.astype(F32) + got.astype(F32)).astype(keep.dtype)


def to_owners(both):
    return lax.all_to_all(both, CHIPS, 0, 0)


def cost(micros):
    return pl.CostEstimate(flops=int(micros * 1e9), bytes_accessed=int(micros * 1e6), transcendentals=0)


def per_device(
    node_in, edge_in, neighbors, chain_ids, residue_mask, w_msg_in, chain_vec, w_msg_out, gain_one,
    w_ffn_in, w_ffn_out, gain_two, w_edge_in, w_edge_out, gain_three, node_cot, edge_cot,
):
    dest_rows, width_k, edge_width = edge_in.shape
    rows_own, width = node_in.shape
    hidden_width = w_ffn_in.shape[1]
    nodes = chain_ids.shape[0]
    half = nodes // 2
    small = nodes <= 2 * SPAN
    chips = lax.axis_size(CHIPS)
    per = 5 if width_k % 5 == 0 else 1
    steps = width_k // per
    count = per * dest_rows
    lanes = count + (-count) % 128
    shares = dest_rows // rows_own
    norm_scale = math.sqrt(width_k * shares)
    me_core = lax.axis_index("c")
    share = lax.axis_index("y") * 2 + me_core
    group = lax.axis_index("z") * 2 + lax.axis_index("x")
    z, x, y = (lax.axis_index(axis) for axis in CHIPS)
    where = jnp.stack([share, group, me_core, z, x, y]).astype(jnp.int32)

    edges = edge_in.transpose(1, 0, 2)
    cots = edge_cot.transpose(1, 0, 2)
    lo, hi = gather_spread(jnp.broadcast_to(node_in[None], (chips,) + node_in.shape))

    first_row = group * dest_rows
    source = neighbors.T
    dest_chain = lax.dynamic_slice_in_dim(chain_ids, first_row, dest_rows)
    dest_mask = lax.dynamic_slice_in_dim(residue_mask, first_row, dest_rows)
    lower = jnp.sum((chain_ids[None, :] < dest_chain[:, None]).astype(jnp.int32), axis=1)
    upper = jnp.sum((chain_ids[None, :] <= dest_chain[:, None]).astype(jnp.int32), axis=1)
    bits = jnp.sum(residue_mask.reshape(nodes // 16, 16) << jnp.arange(16, dtype=jnp.int32)[None, :], axis=1)
    pick = (source >> 4)[:, :, None] == jnp.arange(nodes // 16, dtype=jnp.int32)[None, None, :]
    word = jnp.sum(jnp.where(pick, bits[None, None, :], 0), axis=2)
    present = (word >> (source & 15)) & 1
    pair_mask = (dest_mask[None, :] * present).astype(F32)
    cross = ((source < lower[None, :]) | (source >= upper[None, :])).astype(F32)
    block = source // rows_own
    place = ((block % 2) ^ me_core) * half + (block // 2) * rows_own + source % rows_own
    table = jnp.stack([place.astype(F32), pair_mask, cross]).reshape(3, steps, count).transpose(1, 0, 2)
    flags = jnp.pad(table, ((0, 0), (0, 5), (0, lanes - count)))

    row = lambda v: v.reshape(1, -1)
    wei_t = w_edge_in.T
    edge_spec = per_step(per, edges.shape)
    flag_spec = per_step(1, flags.shape)
    wide_spec = [whole((rows_own, 2 * width))] * shares
    wide_out = [sds((rows_own, 2 * width), BF)] * shares
    share_spec = [whole((rows_own, width))] * shares

    f_slope, *sums = pl.pallas_call(
        functools.partial(message_forward, rows_own),
        grid=(steps,),
        in_specs=[
            SCALARS, edge_spec, flag_spec, whole((half, width)), whole((half, width)), whole(w_msg_in.shape), whole((1, width)),
        ],
        out_specs=[per_step(per, (width_k, dest_rows, width))] + wide_spec,
        out_shape=[sds((width_k, dest_rows, width), BF)] + wide_out,
        scratch_shapes=[
            pltpu.VMEM((half, width), BF), pltpu.VMEM((half, width), BF), pltpu.VMEM((dest_rows, width), F32),
            pltpu.VMEM((dest_rows, 2 * width), F32), pltpu.VMEM((count, width), F32),
        ],
        compiler_params=params(),
        name="message_forward",
    )(where, edges, flags, *pin(small, lo, hi), w_msg_in, row(chain_vec))
    sums = send_shares(sums)

    total, slopes, first_in, second_in, low, ffn_slope, ffn_hidden, node_out, e_spread, e_own = pl.pallas_call(
        functools.partial(node_forward, norm_scale),
        out_shape=[
            sds((rows_own, width), BF), sds((rows_own, width), F32), sds((rows_own, width), F32), sds((rows_own, width), F32),
            sds((chips, rows_own, width), BF), sds((rows_own, hidden_width), F32), sds((rows_own, hidden_width), BF), sds((rows_own, width), BF),
            sds((chips, rows_own, edge_width), BF), sds((rows_own, edge_width), BF),
        ],
        in_specs=[pl.BlockSpec(memory_space=pltpu.VMEM)] * 7 + [ANY] * 2 + [pl.BlockSpec(memory_space=pltpu.VMEM), ANY],
        scratch_shapes=[
            pltpu.VMEM(w_ffn_in.shape, BF), pltpu.VMEM(w_ffn_out.shape, BF), pltpu.VMEM(wei_t.shape, BF),
            pltpu.SemaphoreType.DMA((3,)),
        ],
        compiler_params=pltpu.CompilerParams(vmem_limit_bytes=56 << 20),
        name="node_forward",
    )(sums[0], *pin(small, *sums[1:]), node_in, w_msg_out, row(gain_one), w_ffn_in, w_ffn_out, row(gain_two), wei_t)

    e_owns = send_shares([e_own] * shares)
    e_lo = lax.all_to_all(e_spread, CHIPS, 0, 0).reshape(-1, edge_width)
    e_lo, *e_owns = lax.optimization_barrier((e_lo, *e_owns))
    e_hi = swap(e_lo, "c")
    e_lo, low = lax.optimization_barrier((e_lo, low))
    low_lo = lax.all_to_all(low, CHIPS, 0, 0).reshape(half, width)

    edge_new, d_sum, e_slo, e_shi, *rest = pl.pallas_call(
        edge_network,
        grid=(steps,),
        in_specs=[SCALARS, edge_spec, edge_spec, flag_spec, whole((half, edge_width)), whole((half, edge_width))]
        + [whole((rows_own, edge_width))] * shares
        + [whole(wei_t.shape), whole(w_edge_out.shape), whole((1, edge_width))],
        out_specs=[edge_spec, edge_spec, whole((half, edge_width)), whole((half, edge_width))]
        + [whole((rows_own, edge_width))] * shares
        + [whole((edge_width, edge_width)), whole((edge_width, edge_width)), whole((8, edge_width))],
        out_shape=[sds(edges.shape, BF), sds(edges.shape, BF), vmem(small, (half, edge_width), BF), sds((half, edge_width), BF)]
        + [sds((rows_own, edge_width), BF)] * shares
        + [sds((edge_width, edge_width), F32), sds((edge_width, edge_width), F32), sds((8, edge_width), F32)],
        scratch_shapes=[
            pltpu.VMEM((count, edge_width), F32), pltpu.VMEM((count, edge_width), BF), pltpu.VMEM((count, edge_width), BF),
            pltpu.VMEM((count, edge_width), BF), pltpu.VMEM((count, edge_width), BF), pltpu.VMEM((count, edge_width), BF), pltpu.VMEM((nodes, edge_width), F32), pltpu.VMEM((dest_rows, edge_width), F32),
        ],
        compiler_params=params(),
        cost_estimate=cost(22),
        name="edge_network",
    )(where, edges, cots, flags, *pin(small, e_lo, e_hi), e_owns[0], *pin(small, *e_owns[1:]), wei_t, w_edge_out, row(gain_three))
    g_in, g_out, g_gain3 = rest[shares:]
    e_slo, e_shi, low_lo, *e_sums = lax.optimization_barrier((e_slo, e_shi, low_lo, *rest[:shares]))
    low_hi = swap(low_lo, "c")
    e_sums = send_shares(e_sums)
    e_parts = scatter_halves(e_slo, e_shi)

    up = lambda rows: rows + (-rows) % (32 * chips)
    pay_early = up(2 * width + 2 * edge_width + MOVED)
    pay_late = width + 2 * edge_width - MOVED
    pay_late += (-pay_late) % (16 * chips)
    early_rows, late_rows = pay_early // (2 * chips), pay_late // (2 * chips)
    kept = (chips, early_rows + rows_own, width)
    operands = (
        *pin(small, e_parts), *stay(e_sums[0]), *pin(small, *e_sums[1:]), node_in, node_cot, node_out, first_in, second_in, ffn_slope, total, slopes,
        wei_t, w_msg_in, w_ffn_in, w_ffn_out, w_msg_out, row(gain_one), row(gain_two), *stay(g_in, g_out),
    )
    specs = [whole(x.shape) for x in operands]
    specs[13:18] = [part((edge_width, 2 * width))] + [ANY] * 4
    specs[-2:] = [ANY] * 2
    outs = [
        sds((rows_own, width), BF), sds((rows_own, width), F32), sds((8, width), F32), vmem(small, kept, BF),
        vmem(small, (chips, early_rows, width), BF),
    ]
    d_hidden, n_grad, g_gains, keep, send = pl.pallas_call(
        functools.partial(node_backward, norm_scale),
        grid=(1,),
        in_specs=[SCALARS] + specs,
        out_specs=[whole(x.shape) for x in outs],
        out_shape=outs,
        scratch_shapes=[
            pltpu.VMEM((pay_early, width), BF), pltpu.VMEM(w_ffn_out.shape, BF), pltpu.VMEM(w_ffn_in.shape, BF),
            pltpu.VMEM(w_msg_out.shape, BF), pltpu.VMEM((width, width), BF),
            pltpu.VMEM(g_in.shape, F32), pltpu.VMEM(g_out.shape, F32), pltpu.SemaphoreType.DMA((6,)),
        ],
        compiler_params=params(48 if small else 56),
        name="node_backward",
    )(where, *operands)
    d_hiddens = send_shares([d_hidden] * shares)
    early, *d_hiddens = lax.optimization_barrier((chip_sum(keep, send), *d_hiddens))
    early_parts = to_owners(early)

    sent = (chips, late_rows + rows_own, width)
    keep, send, e_grad = pl.pallas_call(
        message_backward,
        grid=(steps,),
        in_specs=[SCALARS, edge_spec, per_step(per, (width_k, dest_rows, width)), flag_spec, edge_spec]
        + share_spec + [ANY] * 3 + [whole((8, width))]
        + [whole((8, edge_width)), whole((edge_width, edge_width)), whole((edge_width, edge_width))],
        out_specs=[whole(sent), whole(sent), edge_spec],
        out_shape=[vmem(small, sent, BF), vmem(small, sent, BF), sds(edges.shape, F32)],
        scratch_shapes=[
            pltpu.VMEM((dest_rows, width), F32), pltpu.VMEM((count, width), BF), pltpu.VMEM((nodes, width), F32),
            pltpu.VMEM((edge_width, width), F32), pltpu.VMEM((8, width), F32), pltpu.VMEM((pay_late, width), F32),
            pltpu.VMEM((half, width), BF), pltpu.VMEM((half, width), BF), pltpu.VMEM((edge_width, width), BF),
            pltpu.SemaphoreType.DMA((3,)),
        ],
        compiler_params=params(),
        cost_estimate=cost(13),
        name="message_backward",
    )(where, edges, f_slope, flags, d_sum, d_hiddens[0], *pin(small, *d_hiddens[1:]), w_msg_in, lo, hi, g_gains, g_gain3, g_in, g_out)
    late, early_parts = lax.optimization_barrier((chip_sum(keep, send), early_parts))
    late_parts = to_owners(late)
    dffn_lo = early_parts[:, early_rows:, :].reshape(half, width)
    dffn_hi = swap(dffn_lo, "c")

    tile = 256
    g_ffn_in, g_ffn_out = pl.pallas_call(
        ffn_grads,
        grid=(hidden_width // tile,),
        in_specs=[whole((half, width))] * 4
        + [pl.BlockSpec((width, tile), lambda i: (0, i)), pl.BlockSpec((tile, width), lambda i: (i, 0))],
        out_specs=[pl.BlockSpec((width, tile), lambda i: (0, i)), pl.BlockSpec((tile, width), lambda i: (i, 0))],
        out_shape=[sds(w_ffn_in.shape, F32), sds(w_ffn_out.shape, F32)],
        compiler_params=params(),
        cost_estimate=cost(18),
        name="ffn_grads",
    )(low_lo, low_hi, dffn_lo, dffn_hi, w_ffn_in, w_ffn_out)

    layers = lax.axis_size("z")
    plane = chips // layers
    mine = early_parts[:, :early_rows, :].astype(F32).sum(0).astype(BF)
    mine, late_parts, g_ffn_in, g_ffn_out = lax.optimization_barrier((mine, late_parts, g_ffn_in, g_ffn_out))
    spread = pl.pallas_call(
        functools.partial(finish_payload, late_rows),
        out_shape=vmem(small, (1 if layers <= 4 else layers, early_rows + late_rows, width), BF),
        compiler_params=pltpu.CompilerParams(vmem_limit_bytes=(48 if small else 56) << 20),
        name="finish_payload",
    )(mine, *pin(small, late_parts))
    node_grad = pl.pallas_call(
        functools.partial(finish_nodes, late_rows),
        grid=(1,),
        in_specs=[whole(late_parts.shape), whole(n_grad.shape), part((width, width), 1, 0)],
        out_specs=whole(n_grad.shape),
        out_shape=sds(n_grad.shape, F32),
        compiler_params=params(48 if small else 56),
        name="finish_nodes",
    )(*pin(small, late_parts), n_grad, w_msg_in)
    if layers <= 4:
        piece = spread[0]
        got = [lax.ppermute(piece, "z", [((z + k) % layers, z) for z in range(layers)]) for k in range(1, layers)]
        layer = pl.pallas_call(
            place_layers,
            in_specs=[SCALARS] + [pl.BlockSpec(memory_space=pltpu.VMEM)] * layers,
            out_shape=vmem(small, (plane, layers) + piece.shape, BF),
            compiler_params=pltpu.CompilerParams(vmem_limit_bytes=(48 if small else 56) << 20),
            name="place_layers",
        )(where, *pin(small, piece, *got))
    else:
        layer = lax.all_to_all(spread, "z", 0, 0)
        layer = jnp.broadcast_to(layer[None], (plane,) + layer.shape)
    same = lax.all_to_all(layer, ("x", "y"), 0, 0)
    other = swap(same, "c")
    g_msg_in, g_msg_out, g_edge_t, g_edge_out, *vecs = pl.pallas_call(
        functools.partial(finish_weights, edge_width),
        in_specs=[SCALARS] + [pl.BlockSpec(memory_space=pltpu.VMEM)] * 2,
        out_shape=[
            sds(w_msg_in.shape, F32), sds((width, width), F32), sds(wei_t.shape, F32), sds((edge_width, edge_width), F32),
            sds((1, width), F32), sds((1, width), F32), sds((1, edge_width), F32), sds((1, width), F32),
        ],
        scratch_shapes=[pltpu.VMEM((pay_early, width), BF), pltpu.VMEM((pay_late, width), F32)],
        compiler_params=pltpu.CompilerParams(vmem_limit_bytes=(24 if small else 56) << 20),
        name="finish_weights",
    )(where, *pin(small, same, other))
    g_gain1, g_gain2, g_gain3, g_chain = (v.reshape(-1) for v in vecs)
    return (
        node_out, edge_new.transpose(1, 0, 2), node_grad, e_grad.transpose(1, 0, 2), g_msg_in, g_chain, g_msg_out,
        g_gain1, g_ffn_in, g_ffn_out, g_gain2, g_edge_t.T, g_edge_out, g_gain3,
    )


def solution(mesh):
    groups, shares = mesh.shape["res"], mesh.shape["edge"]
    fine = Mesh(mesh.devices.reshape(groups // 2, 2, shares // 2, 2), ("z", "x", "y", "c"))
    rows = P(("z", "x", "y", "c"), None)
    edges = P(("z", "x"), ("y", "c"), None)
    in_specs = (rows, edges, P(("z", "x"), ("y", "c"))) + (P(),) * 12 + (rows, edges)
    out_specs = (rows, edges, rows, edges) + (P(),) * 10
    return jax.shard_map(per_device, mesh=fine, in_specs=in_specs, out_specs=out_specs, check_vma=False)
```

```python
import functools
import math

import jax
import jax.numpy as jnp
from jax import lax
from jax.experimental import pallas as pl
from jax.experimental.pallas import tpu as pltpu
from jax.sharding import Mesh, PartitionSpec as P

EPS = 1e-05
CHIPS = ("z", "x", "y")
BF = jnp.bfloat16
F32 = jnp.float32
ROWS = 80
PIECE = 800
MOVED = 128
SPAN = 1280
RSQRT2 = math.sqrt(0.5)
INV_SQRT_2PI = 1.0 / math.sqrt(2.0 * math.pi)
PLACE, MASK, CROSS = 0, 1, 2


def mm(a, b):
    return jnp.dot(a, b, preferred_element_type=F32)


def mm_nt(a, b):
    return lax.dot_general(a, b, (((1,), (1,)), ((), ())), preferred_element_type=F32)


def mm_tn(a, b):
    return lax.dot_general(a, b, (((0,), (0,)), ((), ())), preferred_element_type=F32)


def gelu_pair(v):
    cdf = 0.5 * (1.0 + lax.erf(v * RSQRT2))
    pdf = INV_SQRT_2PI * jnp.exp(-0.5 * v * v)
    return v * cdf, cdf + v * pdf


def norm_parts(z):
    centre = z - jnp.mean(z, axis=-1, keepdims=True)
    r = lax.rsqrt(jnp.mean(centre * centre, axis=-1, keepdims=True) + EPS)
    return centre * r, r


def norm_back(n, r, gain, cot):
    b = cot * gain
    dz = r * (b - jnp.mean(b, -1, keepdims=True) - n * jnp.mean(b * n, -1, keepdims=True))
    return dz, jnp.sum(cot * n, axis=0, keepdims=True)


def gather_rows(place, halves):
    total = None
    for h, table in enumerate(halves):
        count = table.shape[0]
        block = min(count, SPAN)
        for start in range(0, count, block):
            lane = lax.broadcasted_iota(jnp.int32, (place.shape[0], block), 1) + (h * count + start)
            hot = jnp.where(lane == place, 1.0, 0.0).astype(BF)
            part = mm(hot, table[start : start + block, :])
            total = part if total is None else total + part
    return total


def scatter_rows(place_row, rows, acc):
    nodes = acc.shape[0]
    block = min(nodes, SPAN // 2)

    @pl.loop(0, nodes // block)
    def _(i):
        start = pl.multiple_of(i * block, block)
        row = lax.broadcasted_iota(jnp.int32, (block, place_row.shape[1]), 0) + start
        hot = jnp.where(row == place_row, 1.0, 0.0).astype(BF)
        acc[pl.ds(start, block), :] += mm(hot, rows)


def group_rows(where_ref, lo_ref, hi_ref, rows_own):
    group, core = where_ref[1], where_ref[2]
    start = pl.multiple_of(group * 2 * rows_own, 2 * rows_own)
    same = lo_ref[pl.ds(start, 2 * rows_own), :].astype(F32)
    other = hi_ref[pl.ds(start, 2 * rows_own), :].astype(F32)
    swapped = core == 1
    first = jnp.where(swapped, other, same)
    second = jnp.where(swapped, same, other)
    rows = [first[:rows_own], second[:rows_own], first[rows_own:], second[rows_own:]]
    return jnp.concatenate(rows, axis=0)


def put_shares(where_ref, refs, out):
    rows = refs[0].shape[0]
    shares = len(refs)
    for q, ref in enumerate(refs):
        at = lax.rem(where_ref[0] + shares - q, shares) * rows
        out[pl.ds(pl.multiple_of(at, 8), rows), :] = ref[...].astype(out.dtype)


def take_shares(where_ref, acc, refs):
    rows = refs[0].shape[0]
    shares = len(refs)
    for q, ref in enumerate(refs):
        at = lax.rem(where_ref[0] + q, shares) * rows
        ref[...] = acc[pl.ds(pl.multiple_of(at, 8), rows), :].astype(ref.dtype)


def add_up(refs):
    total = refs[0][...].astype(F32)
    for ref in refs[1:]:
        total += ref[...].astype(F32)
    return total


def message_forward(
    rows_own,
    where_ref, edge_ref, flags_ref, lo_ref, hi_ref, wmi_ref, chain_ref,
    slope_ref, s0, s1, s2, s3,
    table_lo, table_hi, own, acc, pre_s,
):
    step = pl.program_id(0)
    width = wmi_ref.shape[1]
    per, dest_rows, edge_width = edge_ref.shape
    edges = per * dest_rows

    @pl.when(step == 0)
    def _():
        weights = wmi_ref[width : 2 * width, :]
        half = lo_ref.shape[0]
        block = half // 2 if half <= SPAN else SPAN // 2

        @pl.loop(0, half // block)
        def _(i):
            at = pl.ds(pl.multiple_of(i * block, block), block)
            table_lo[at, :] = mm(lo_ref[at, :], weights).astype(BF)
            table_hi[at, :] = mm(hi_ref[at, :], weights).astype(BF)

        group = group_rows(where_ref, lo_ref, hi_ref, rows_own).astype(BF)
        own[...] = mm(group, wmi_ref[:width, :])
        acc[...] = jnp.zeros_like(acc)

    flags = jnp.transpose(flags_ref[0])[:edges, :]
    place = flags[:, PLACE : PLACE + 1].astype(jnp.int32)
    pre_s[...] = gather_rows(place, (table_lo, table_hi)) + mm(
        edge_ref[...].reshape(edges, edge_width), wmi_ref[2 * width :, :]
    )
    for j in range(per):
        for r in range(0, dest_rows, ROWS):
            at = slice(j * dest_rows + r, j * dest_rows + r + ROWS)
            mask = flags[at, MASK : MASK + 1]
            cross = flags[at, CROSS : CROSS + 1]
            pre = pre_s[at, :] + own[r : r + ROWS, :] + cross * chain_ref[...]
            hidden, slope = gelu_pair(pre)
            slope = slope * mask
            slope_ref[j, r : r + ROWS, :] = slope.astype(BF)
            acc[r : r + ROWS, :width] += hidden.astype(BF).astype(F32) * mask
            acc[r : r + ROWS, width:] += slope

    @pl.when(step == pl.num_programs(0) - 1)
    def _():
        take_shares(where_ref, acc, (s0, s1, s2, s3))


def start_copies(sources, targets, sems):
    copies = [pltpu.make_async_copy(s, t, sems.at[i]) for i, (s, t) in enumerate(zip(sources, targets))]
    for copy in copies:
        copy.start()
    return copies


def node_forward(
    norm_scale,
    s0, s1, s2, s3, node_ref, wmo_ref, gain1_ref, wfi_any, wfo_any, gain2_ref, weit_any,
    total_ref, slopes_ref, first_ref, second_ref, low_ref, fslope_ref, fhidden_ref, out_ref, src_ref, eown_ref,
    wfi_ref, wfo_ref, weit_ref, sems,
):
    copies = start_copies((wfi_any, wfo_any, weit_any), (wfi_ref, wfo_ref, weit_ref), sems)
    width = node_ref.shape[1]
    sums = add_up((s0, s1, s2, s3))
    total = sums[:, :width].astype(BF)
    total_ref[...] = total
    slopes_ref[...] = sums[:, width:]
    first_in = node_ref[...].astype(F32) + mm(total, wmo_ref[...]) * (1.0 / norm_scale)
    first_ref[...] = first_in
    norm_one = norm_parts(first_in)[0] * gain1_ref[...]
    low = norm_one.astype(BF)
    for i in range(low_ref.shape[0]):
        low_ref[i] = low
    copies[0].wait()
    hidden, slope = gelu_pair(mm(low, wfi_ref[...]))
    hidden = hidden.astype(BF)
    fslope_ref[...] = slope
    fhidden_ref[...] = hidden
    copies[1].wait()
    second_in = norm_one + mm(hidden, wfo_ref[...])
    second_ref[...] = second_in
    node_out = (norm_parts(second_in)[0] * gain2_ref[...]).astype(BF)
    out_ref[...] = node_out
    copies[2].wait()
    eown_ref[...] = mm_nt(node_out, weit_ref[:, :width]).astype(BF)
    src = mm_nt(node_out, weit_ref[:, width : 2 * width]).astype(BF)
    for i in range(src_ref.shape[0]):
        src_ref[i] = src


def edge_network(
    where_ref, edge_ref, cot_ref, flags_ref, lo_ref, hi_ref, e0, e1, e2, e3, weit_ref, weo_ref, gain_ref,
    out_ref, dsum_ref, slo_ref, shi_ref, o0, o1, o2, o3, gin_ref, gout_ref, ggain_ref,
    own, dpre_s, hidden_s, delta_s, out_s, dsum_s, acc, own_acc,
):
    step = pl.program_id(0)
    per, dest_rows, edge_width = edge_ref.shape
    edges = per * dest_rows
    width = (weit_ref.shape[1] - edge_width) // 2
    weights_t = weit_ref[:, 2 * width :]

    @pl.when(step == 0)
    def _():
        put_shares(where_ref, (e0, e1, e2, e3), own)
        for j in range(1, per):
            own[j * dest_rows : (j + 1) * dest_rows, :] = own[:dest_rows, :]
        acc[...] = jnp.zeros_like(acc)
        own_acc[...] = jnp.zeros_like(own_acc)
        gin_ref[...] = jnp.zeros_like(gin_ref)
        gout_ref[...] = jnp.zeros_like(gout_ref)
        ggain_ref[...] = jnp.zeros_like(ggain_ref)

    flags = jnp.transpose(flags_ref[0])[:edges, :]
    place = flags[:, PLACE : PLACE + 1].astype(jnp.int32)
    edge_all = edge_ref[...].reshape(edges, edge_width)
    cot_all = cot_ref[...].reshape(edges, edge_width)
    pre_all = gather_rows(place, (lo_ref, hi_ref)) + mm_nt(edge_all, weights_t) + own[...]
    gain = gain_ref[...]
    piece = PIECE if edges % PIECE == 0 else edges
    for start in range(0, edges, piece):
        at = slice(start, start + piece)
        mask = flags[at, MASK : MASK + 1]
        hidden, slope = gelu_pair(pre_all[at, :])
        hidden = (hidden * mask).astype(BF)
        hidden_s[at, :] = hidden
        n, r = norm_parts(edge_all[at, :].astype(F32) + mm(hidden, weo_ref[...]))
        out_s[at, :] = (n * gain).astype(BF)
        cot = cot_all[at, :].astype(F32)
        cn = cot * n
        ggain_ref[...] += jnp.sum(cn.reshape(piece // 8, 8, edge_width), axis=0)
        b = cot * gain
        dz = r * (b - jnp.mean(b, -1, keepdims=True) - n * jnp.mean(cn * gain, -1, keepdims=True))
        d_delta = (dz * mask).astype(BF)
        delta_s[at, :] = d_delta
        d_low = (slope * mm_nt(d_delta, weo_ref[...])).astype(BF)
        dpre_s[at, :] = d_low
        dsum_s[at, :] = (dz + mm(d_low, weights_t)).astype(BF)
    out_ref[...] = out_s[...].reshape(out_ref.shape)
    dsum_ref[...] = dsum_s[...].reshape(dsum_ref.shape)
    for j in range(per):
        own_acc[...] += dpre_s[j * dest_rows : (j + 1) * dest_rows, :].astype(F32)
    gout_ref[...] += mm_tn(hidden_s[...], delta_s[...])
    gin_ref[...] += mm_tn(edge_all, dpre_s[...])
    place_row = flags_ref[0, PLACE : PLACE + 1, :edges].astype(jnp.int32)
    scatter_rows(place_row, dpre_s[...], acc)

    @pl.when(step == pl.num_programs(0) - 1)
    def _():
        half = slo_ref.shape[0]
        slo_ref[...] = acc[:half, :].astype(BF)
        shi_ref[...] = acc[half:, :].astype(BF)
        take_shares(where_ref, own_acc, (o0, o1, o2, o3))


def node_backward(
    norm_scale,
    where_ref, parts_ref, o0, o1, o2, o3, node_ref, node_cot_ref, out_ref, first_ref, second_ref, fslope_ref,
    total_ref, slopes_ref, weit_ref, wmi_any, wfi_any, wfo_any, wmo_any, gain1_ref, gain2_ref,
    gin_any, gout_any,
    d_ref, ngrad_ref, ggain_ref, keep_ref, send_ref,
    pay, wfo_ref, wfi_ref, wmo_ref, wmi_ref, gin_ref, gout_ref, sems,
):
    width = out_ref.shape[1]
    own_rows = wmi_any.at[pl.ds(0, width), :]
    sources = (wfo_any, wfi_any, wmo_any, own_rows, gin_any, gout_any)
    copies = start_copies(sources, (wfo_ref, wfi_ref, wmo_ref, wmi_ref, gin_ref, gout_ref), sems)
    from_sources = add_up(tuple(parts_ref.at[i] for i in range(parts_ref.shape[0]))).astype(BF)
    from_own = add_up((o0, o1, o2, o3)).astype(BF)
    d_updated = (
        node_cot_ref[...].astype(F32)
        + mm(from_own, weit_ref[:, :width])
        + mm(from_sources, weit_ref[:, width : 2 * width])
    )
    node_out = out_ref[...]
    n, r = norm_parts(second_ref[...])
    d_second, ggain2 = norm_back(n, r, gain2_ref[...], d_updated)
    dffn = d_second.astype(BF)
    copies[0].wait()
    d_ffn_pre = (fslope_ref[...] * mm_nt(dffn, wfo_ref[...])).astype(BF)
    copies[1].wait()
    d_norm_one = d_second + mm_nt(d_ffn_pre, wfi_ref[...])
    n, r = norm_parts(first_ref[...])
    d_first, ggain1 = norm_back(n, r, gain1_ref[...], d_norm_one)
    d_summed = (d_first * (1.0 / norm_scale)).astype(BF)
    copies[2].wait()
    d_hidden = mm_nt(d_summed, wmo_ref[...])
    d_ref[...] = d_hidden.astype(BF)
    own_sum = (d_hidden * slopes_ref[...]).astype(BF)
    copies[3].wait()
    ngrad_ref[...] = d_first + mm_nt(own_sum, wmi_ref[...])
    ggain_ref[...] = jnp.concatenate([ggain1, ggain2, jnp.zeros((6, width), F32)], axis=0)
    parts = (
        mm_tn(total_ref[...], d_summed), mm_tn(node_ref[...], own_sum), mm_tn(from_own, node_out), mm_tn(from_sources, node_out)
    )
    at = 0
    for part in parts:
        pay[at : at + part.shape[0], :] = part.astype(BF)
        at += part.shape[0]
    copies[4].wait()
    copies[5].wait()
    edge_width = gin_ref.shape[1]
    spare = jnp.zeros((MOVED, width - 2 * edge_width), F32)
    pay[at : at + MOVED, :] = jnp.concatenate([gin_ref[:MOVED, :], gout_ref[:MOVED, :], spare], axis=1).astype(BF)
    at += MOVED
    if at < pay.shape[0]:
        pay[at:, :] = jnp.zeros((pay.shape[0] - at, width), BF)
    early = pay.shape[0] // 2 // keep_ref.shape[0]
    split_halves(where_ref, pay, early, keep_ref, send_ref)
    for i in range(keep_ref.shape[0]):
        keep_ref[i, early:, :] = dffn


def split_halves(where_ref, pay, rows, keep_ref, send_ref):
    half = pay.shape[0] // 2
    at = pl.multiple_of(where_ref[2] * half, 16)
    shape = (keep_ref.shape[0], rows, pay.shape[1])
    keep_ref[:, :rows, :] = pay[pl.ds(at, half), :].reshape(shape)
    send_ref[:, :rows, :] = pay[pl.ds(half - at, half), :].reshape(shape)


def message_backward(
    where_ref, edge_ref, slope_ref, flags_ref, dsum_ref, d0, d1, d2, d3, wmi_any, lo_any, hi_any, gain_ref, gain3_ref, gin_ref,
    gout_ref,
    keep_ref, send_ref, eg_ref,
    own, dpre_s, acc, gin, chain, pay, lo_ref, hi_ref, wme_ref, sems,
):
    step = pl.program_id(0)
    width = wme_ref.shape[1]
    per, dest_rows, edge_width = edge_ref.shape
    edges = per * dest_rows
    copy_w = pltpu.make_async_copy(wmi_any.at[pl.ds(2 * width, edge_width), :], wme_ref, sems.at[2])
    copy_lo = pltpu.make_async_copy(lo_any, lo_ref, sems.at[0])
    copy_hi = pltpu.make_async_copy(hi_any, hi_ref, sems.at[1])

    @pl.when(step == 0)
    def _():
        copy_w.start()
        copy_lo.start()
        copy_hi.start()
        put_shares(where_ref, (d0, d1, d2, d3), own)
        acc[...] = jnp.zeros_like(acc)
        gin[...] = jnp.zeros_like(gin)
        chain[...] = jnp.zeros_like(chain)

    flags = jnp.transpose(flags_ref[0])[:edges, :]
    for j in range(per):
        for r in range(0, dest_rows, ROWS):
            at = slice(j * dest_rows + r, j * dest_rows + r + ROWS)
            d_low = (slope_ref[j, r : r + ROWS, :].astype(F32) * own[r : r + ROWS, :]).astype(BF)
            dpre_s[at, :] = d_low
            crossed = d_low.astype(F32) * flags[at, CROSS : CROSS + 1]
            chain[...] += jnp.sum(crossed.reshape(ROWS // 8, 8, width), axis=0)
    @pl.when(step == 0)
    def _():
        copy_w.wait()

    d_all = dpre_s[...]
    gin[...] += mm_tn(edge_ref[...].reshape(edges, edge_width), d_all)
    back = mm_nt(d_all, wme_ref[...])
    for j in range(per):
        eg_ref[j] = dsum_ref[j].astype(F32) + back[j * dest_rows : (j + 1) * dest_rows, :]
    place_row = flags_ref[0, PLACE : PLACE + 1, :edges].astype(jnp.int32)
    scatter_rows(place_row, d_all, acc)

    @pl.when(step == pl.num_programs(0) - 1)
    def _():
        half = lo_ref.shape[0]
        chips = keep_ref.shape[0]
        rows = half // chips
        late = keep_ref.shape[1] - rows
        copy_lo.wait()
        copy_hi.wait()
        pay[:width, :] = mm_tn(lo_ref[...], acc[:half, :].astype(BF)) + mm_tn(hi_ref[...], acc[half:, :].astype(BF))
        pay[width : width + edge_width, :] = gin[...]
        at = width + edge_width
        pay[at:, :] = jnp.zeros((pay.shape[0] - at, width), F32)
        left = edge_width - MOVED
        pay[at : at + left, : 2 * edge_width] = jnp.concatenate([gin_ref[MOVED:, :], gout_ref[MOVED:, :]], axis=1)
        crossed = jnp.sum(chain[...], axis=0, keepdims=True)
        gain3 = jnp.sum(gain3_ref[...], axis=0, keepdims=True)
        gain3 = jnp.concatenate([gain3, jnp.zeros((1, width - edge_width), F32)], axis=1)
        lanes = width - 2 * edge_width
        for v, vec in enumerate((gain_ref[:1, :], gain_ref[1:2, :], gain3, crossed)):
            for q in range(width // lanes):
                line = at + v * (width // lanes) + q
                pay[line : line + 1, 2 * edge_width :] = vec[:, q * lanes : (q + 1) * lanes]
        half_pay = pay.shape[0] // 2
        core = where_ref[2]
        for chip in range(chips):
            mine = pay[pl.ds(pl.multiple_of(core * half_pay + chip * late, 8), late), :]
            other = pay[pl.ds(pl.multiple_of((1 - core) * half_pay + chip * late, 8), late), :]
            same_rows = acc[chip * rows : (chip + 1) * rows, :]
            other_rows = acc[half + chip * rows : half + (chip + 1) * rows, :]
            keep_ref[chip] = jnp.concatenate([mine, same_rows], axis=0).astype(BF)
            send_ref[chip] = jnp.concatenate([other, other_rows], axis=0).astype(BF)


def finish_nodes(late, parts_ref, ngrad_ref, wmi_ref, out_ref):
    total = add_up(tuple(parts_ref.at[i] for i in range(parts_ref.shape[0])))[late:, :]
    out_ref[...] = ngrad_ref[...] + mm_nt(total.astype(BF), wmi_ref[...])


def finish_payload(late, mine_ref, parts_ref, spread_ref):
    early = mine_ref.shape[0]
    other = add_up(tuple(parts_ref.at[i, :late, :] for i in range(parts_ref.shape[0]))).astype(BF)
    for i in range(spread_ref.shape[0]):
        spread_ref[i, :early, :] = mine_ref[...]
        spread_ref[i, early:, :] = other


def place_layers(where_ref, *refs):
    out_ref = refs[-1]
    for k, ref in enumerate(refs[:-1]):
        out_ref[lax.rem(where_ref[3] + k, out_ref.shape[0])] = ref[...]


def finish_weights(
    edge_width,
    where_ref, p0, p1, p2, p3, p4, p5, p6, p7,
    gmi_ref, gmo_ref, geit_ref, geo_ref, g1_ref, g2_ref, g3_ref, gchain_ref,
    early, late,
):
    width = gmi_ref.shape[1]
    layers = p0.shape[0]
    first = early.shape[0] // 2 // (4 * layers)
    second = late.shape[0] // 2 // (4 * layers)
    for i, piece in enumerate((p0, p1, p2, p3, p4, p5, p6, p7)):
        half = where_ref[2] ^ (i // 4)
        place = (where_ref[4] ^ (i % 2)) * 2 + (where_ref[5] ^ (i // 2 % 2))
        for z in range(layers):
            chip = (half * layers + z) * 4 + place
            early[pl.ds(pl.multiple_of(chip * first, 16), first), :] = piece[z, :first, :]
            late[pl.ds(pl.multiple_of(chip * second, 8), second), :] = piece[z, first:, :].astype(F32)
    gmo_ref[...] = early[:width, :].astype(F32)
    gmi_ref[:width, :] = early[width : 2 * width, :].astype(F32)
    gmi_ref[width:, :] = late[: width + edge_width, :]
    at = 2 * width
    geit_ref[:, :width] = early[at : at + edge_width, :].astype(F32)
    geit_ref[:, width : 2 * width] = early[at + edge_width : at + 2 * edge_width, :].astype(F32)
    at += 2 * edge_width
    line = width + edge_width
    moved = early[at : at + MOVED, : 2 * edge_width].astype(F32)
    small = jnp.concatenate([moved, late[line : line + edge_width - MOVED, : 2 * edge_width]], axis=0)
    geit_ref[:, 2 * width :] = jnp.transpose(small[:, :edge_width])
    geo_ref[...] = small[:, edge_width:]
    count = width // (width - 2 * edge_width)
    for v, ref in enumerate((g1_ref, g2_ref, g3_ref, gchain_ref)):
        vec = [late[line + v * count + q : line + v * count + q + 1, 2 * edge_width :] for q in range(count)]
        ref[...] = jnp.concatenate(vec, axis=1)[:, : ref.shape[1]]


def ffn_grads(llo_ref, lhi_ref, dlo_ref, dhi_ref, wfi_ref, wfo_ref, gfi_ref, gfo_ref):
    block = min(llo_ref.shape[0], SPAN // 2)
    gfi = gfo = None
    for low_ref, dffn_ref in ((llo_ref, dlo_ref), (lhi_ref, dhi_ref)):
        for start in range(0, low_ref.shape[0], block):
            low = low_ref[start : start + block, :]
            dffn = dffn_ref[start : start + block, :]
            hidden, slope = gelu_pair(mm(low, wfi_ref[...]))
            part = mm_tn(hidden.astype(BF), dffn)
            gfo = part if gfo is None else gfo + part
            d_pre = (slope * mm_nt(dffn, wfo_ref[...])).astype(BF)
            part = mm_tn(low, d_pre)
            gfi = part if gfi is None else gfi + part
    gfo_ref[...] = gfo
    gfi_ref[...] = gfi


def whole(shape):
    return pl.BlockSpec(tuple(shape), lambda *_: (0,) * len(shape))


def part(shape, *index):
    return pl.BlockSpec(tuple(shape), lambda *_: index or (0,) * len(shape))


def per_step(count, shape):
    return pl.BlockSpec((count,) + tuple(shape[1:]), lambda i: (i,) + (0,) * (len(shape) - 1))


SCALARS = pl.BlockSpec(memory_space=pltpu.SMEM)
ANY = pl.BlockSpec(memory_space=pl.ANY)


def params(limit=56):
    return pltpu.CompilerParams(vmem_limit_bytes=limit << 20, dimension_semantics=("arbitrary",))


def pin(small, *arrays):
    return [pltpu.with_memory_space_constraint(x, pltpu.VMEM) if small else x for x in arrays]


def stay(*arrays):
    return [pltpu.with_memory_space_constraint(x, pltpu.HBM) for x in arrays]


def vmem(small, shape, dtype):
    return pltpu.VMEM(tuple(shape), dtype) if small else sds(shape, dtype)


def sds(shape, dtype):
    return jax.ShapeDtypeStruct(tuple(shape), dtype)


def swap(x, axis):
    return lax.ppermute(x, axis, [(0, 1), (1, 0)])


def gather_spread(spread):
    same = lax.all_to_all(spread, CHIPS, 0, 0).reshape(-1, spread.shape[2])
    return same, swap(same, "c")


def scatter_halves(lo, hi):
    got = swap(hi, "c")
    both = (lo.astype(F32) + got.astype(F32)).astype(lo.dtype)
    return lax.all_to_all(both.reshape(lax.axis_size(CHIPS), -1, lo.shape[1]), CHIPS, 0, 0)


def send_shares(pieces):
    shares = len(pieces)
    got = [pieces[0]]
    for q in range(1, shares):
        got.append(lax.ppermute(pieces[q], ("y", "c"), [(s, (s + q) % shares) for s in range(shares)]))
    return got


def chip_sum(keep, send):
    got = jnp.pad(swap(send, "c"), ((0, 0), (0, keep.shape[1] - send.shape[1]), (0, 0)))
    return (keep.astype(F32) + got.astype(F32)).astype(keep.dtype)


def to_owners(both):
    return lax.all_to_all(both, CHIPS, 0, 0)


def cost(micros):
    return pl.CostEstimate(flops=int(micros * 1e9), bytes_accessed=int(micros * 1e6), transcendentals=0)


def per_device(
    node_in, edge_in, neighbors, chain_ids, residue_mask, w_msg_in, chain_vec, w_msg_out, gain_one,
    w_ffn_in, w_ffn_out, gain_two, w_edge_in, w_edge_out, gain_three, node_cot, edge_cot,
):
    dest_rows, width_k, edge_width = edge_in.shape
    rows_own, width = node_in.shape
    hidden_width = w_ffn_in.shape[1]
    nodes = chain_ids.shape[0]
    half = nodes // 2
    small = nodes <= 2 * SPAN
    chips = lax.axis_size(CHIPS)
    per = 5 if width_k % 5 == 0 else 1
    steps = width_k // per
    count = per * dest_rows
    lanes = count + (-count) % 128
    shares = dest_rows // rows_own
    norm_scale = math.sqrt(width_k * shares)
    me_core = lax.axis_index("c")
    share = lax.axis_index("y") * 2 + me_core
    group = lax.axis_index("z") * 2 + lax.axis_index("x")
    z, x, y = (lax.axis_index(axis) for axis in CHIPS)
    where = jnp.stack([share, group, me_core, z, x, y]).astype(jnp.int32)

    edges = edge_in.transpose(1, 0, 2)
    cots = edge_cot.transpose(1, 0, 2)
    lo, hi = gather_spread(jnp.broadcast_to(node_in[None], (chips,) + node_in.shape))

    first_row = group * dest_rows
    source = neighbors.T
    dest_chain = lax.dynamic_slice_in_dim(chain_ids, first_row, dest_rows)
    dest_mask = lax.dynamic_slice_in_dim(residue_mask, first_row, dest_rows)
    lower = jnp.sum((chain_ids[None, :] < dest_chain[:, None]).astype(jnp.int32), axis=1)
    upper = jnp.sum((chain_ids[None, :] <= dest_chain[:, None]).astype(jnp.int32), axis=1)
    bits = jnp.sum(residue_mask.reshape(nodes // 16, 16) << jnp.arange(16, dtype=jnp.int32)[None, :], axis=1)
    pick = (source >> 4)[:, :, None] == jnp.arange(nodes // 16, dtype=jnp.int32)[None, None, :]
    word = jnp.sum(jnp.where(pick, bits[None, None, :], 0), axis=2)
    present = (word >> (source & 15)) & 1
    pair_mask = (dest_mask[None, :] * present).astype(F32)
    cross = ((source < lower[None, :]) | (source >= upper[None, :])).astype(F32)
    block = source // rows_own
    place = ((block % 2) ^ me_core) * half + (block // 2) * rows_own + source % rows_own
    table = jnp.stack([place.astype(F32), pair_mask, cross]).reshape(3, steps, count).transpose(1, 0, 2)
    flags = jnp.pad(table, ((0, 0), (0, 5), (0, lanes - count)))

    row = lambda v: v.reshape(1, -1)
    wei_t = w_edge_in.T
    edge_spec = per_step(per, edges.shape)
    flag_spec = per_step(1, flags.shape)
    wide_spec = [whole((rows_own, 2 * width))] * shares
    wide_out = [sds((rows_own, 2 * width), BF)] * shares
    share_spec = [whole((rows_own, width))] * shares

    f_slope, *sums = pl.pallas_call(
        functools.partial(message_forward, rows_own),
        grid=(steps,),
        in_specs=[
            SCALARS, edge_spec, flag_spec, whole((half, width)), whole((half, width)), whole(w_msg_in.shape), whole((1, width)),
        ],
        out_specs=[per_step(per, (width_k, dest_rows, width))] + wide_spec,
        out_shape=[sds((width_k, dest_rows, width), BF)] + wide_out,
        scratch_shapes=[
            pltpu.VMEM((half, width), BF), pltpu.VMEM((half, width), BF), pltpu.VMEM((dest_rows, width), F32),
            pltpu.VMEM((dest_rows, 2 * width), F32), pltpu.VMEM((count, width), F32),
        ],
        compiler_params=params(),
        name="message_forward",
    )(where, edges, flags, *pin(small, lo, hi), w_msg_in, row(chain_vec))
    sums = send_shares(sums)

    total, slopes, first_in, second_in, low, ffn_slope, ffn_hidden, node_out, e_spread, e_own = pl.pallas_call(
        functools.partial(node_forward, norm_scale),
        out_shape=[
            sds((rows_own, width), BF), sds((rows_own, width), F32), sds((rows_own, width), F32), sds((rows_own, width), F32),
            sds((chips, rows_own, width), BF), sds((rows_own, hidden_width), F32), sds((rows_own, hidden_width), BF), sds((rows_own, width), BF),
            sds((chips, rows_own, edge_width), BF), sds((rows_own, edge_width), BF),
        ],
        in_specs=[pl.BlockSpec(memory_space=pltpu.VMEM)] * 7 + [ANY] * 2 + [pl.BlockSpec(memory_space=pltpu.VMEM), ANY],
        scratch_shapes=[
            pltpu.VMEM(w_ffn_in.shape, BF), pltpu.VMEM(w_ffn_out.shape, BF), pltpu.VMEM(wei_t.shape, BF),
            pltpu.SemaphoreType.DMA((3,)),
        ],
        compiler_params=pltpu.CompilerParams(vmem_limit_bytes=56 << 20),
        name="node_forward",
    )(sums[0], *pin(small, *sums[1:]), node_in, w_msg_out, row(gain_one), w_ffn_in, w_ffn_out, row(gain_two), wei_t)

    e_owns = send_shares([e_own] * shares)
    e_lo = lax.all_to_all(e_spread, CHIPS, 0, 0).reshape(-1, edge_width)
    e_lo, *e_owns = lax.optimization_barrier((e_lo, *e_owns))
    e_hi = swap(e_lo, "c")
    e_lo, low = lax.optimization_barrier((e_lo, low))
    low_lo = lax.all_to_all(low, CHIPS, 0, 0).reshape(half, width)

    edge_new, d_sum, e_slo, e_shi, *rest = pl.pallas_call(
        edge_network,
        grid=(steps,),
        in_specs=[SCALARS, edge_spec, edge_spec, flag_spec, whole((half, edge_width)), whole((half, edge_width))]
        + [whole((rows_own, edge_width))] * shares
        + [whole(wei_t.shape), whole(w_edge_out.shape), whole((1, edge_width))],
        out_specs=[edge_spec, edge_spec, whole((half, edge_width)), whole((half, edge_width))]
        + [whole((rows_own, edge_width))] * shares
        + [whole((edge_width, edge_width)), whole((edge_width, edge_width)), whole((8, edge_width))],
        out_shape=[sds(edges.shape, BF), sds(edges.shape, BF), vmem(small, (half, edge_width), BF), sds((half, edge_width), BF)]
        + [sds((rows_own, edge_width), BF)] * shares
        + [sds((edge_width, edge_width), F32), sds((edge_width, edge_width), F32), sds((8, edge_width), F32)],
        scratch_shapes=[
            pltpu.VMEM((count, edge_width), F32), pltpu.VMEM((count, edge_width), BF), pltpu.VMEM((count, edge_width), BF),
            pltpu.VMEM((count, edge_width), BF), pltpu.VMEM((count, edge_width), BF), pltpu.VMEM((count, edge_width), BF), pltpu.VMEM((nodes, edge_width), F32), pltpu.VMEM((dest_rows, edge_width), F32),
        ],
        compiler_params=params(),
        cost_estimate=cost(22),
        name="edge_network",
    )(where, edges, cots, flags, *pin(small, e_lo, e_hi), e_owns[0], *pin(small, *e_owns[1:]), wei_t, w_edge_out, row(gain_three))
    g_in, g_out, g_gain3 = rest[shares:]
    e_slo, e_shi, low_lo, *e_sums = lax.optimization_barrier((e_slo, e_shi, low_lo, *rest[:shares]))
    low_hi = swap(low_lo, "c")
    e_sums = send_shares(e_sums)
    e_parts = scatter_halves(e_slo, e_shi)

    up = lambda rows: rows + (-rows) % (32 * chips)
    pay_early = up(2 * width + 2 * edge_width + MOVED)
    pay_late = width + 2 * edge_width - MOVED
    pay_late += (-pay_late) % (16 * chips)
    early_rows, late_rows = pay_early // (2 * chips), pay_late // (2 * chips)
    kept = (chips, early_rows + rows_own, width)
    operands = (
        *pin(small, e_parts), *stay(e_sums[0]), *pin(small, *e_sums[1:]), node_in, node_cot, node_out, first_in, second_in, ffn_slope, total, slopes,
        wei_t, w_msg_in, w_ffn_in, w_ffn_out, w_msg_out, row(gain_one), row(gain_two), *stay(g_in, g_out),
    )
    specs = [whole(x.shape) for x in operands]
    specs[13:18] = [part((edge_width, 2 * width))] + [ANY] * 4
    specs[-2:] = [ANY] * 2
    outs = [
        sds((rows_own, width), BF), sds((rows_own, width), F32), sds((8, width), F32), vmem(small, kept, BF),
        vmem(small, (chips, early_rows, width), BF),
    ]
    d_hidden, n_grad, g_gains, keep, send = pl.pallas_call(
        functools.partial(node_backward, norm_scale),
        grid=(1,),
        in_specs=[SCALARS] + specs,
        out_specs=[whole(x.shape) for x in outs],
        out_shape=outs,
        scratch_shapes=[
            pltpu.VMEM((pay_early, width), BF), pltpu.VMEM(w_ffn_out.shape, BF), pltpu.VMEM(w_ffn_in.shape, BF),
            pltpu.VMEM(w_msg_out.shape, BF), pltpu.VMEM((width, width), BF),
            pltpu.VMEM(g_in.shape, F32), pltpu.VMEM(g_out.shape, F32), pltpu.SemaphoreType.DMA((6,)),
        ],
        compiler_params=params(48 if small else 56),
        name="node_backward",
    )(where, *operands)
    d_hiddens = send_shares([d_hidden] * shares)
    early, *d_hiddens = lax.optimization_barrier((chip_sum(keep, send), *d_hiddens))
    early_parts = to_owners(early)

    sent = (chips, late_rows + rows_own, width)
    keep, send, e_grad = pl.pallas_call(
        message_backward,
        grid=(steps,),
        in_specs=[SCALARS, edge_spec, per_step(per, (width_k, dest_rows, width)), flag_spec, edge_spec]
        + share_spec + [ANY] * 3 + [whole((8, width))]
        + [whole((8, edge_width)), whole((edge_width, edge_width)), whole((edge_width, edge_width))],
        out_specs=[whole(sent), whole(sent), edge_spec],
        out_shape=[vmem(small, sent, BF), vmem(small, sent, BF), sds(edges.shape, F32)],
        scratch_shapes=[
            pltpu.VMEM((dest_rows, width), F32), pltpu.VMEM((count, width), BF), pltpu.VMEM((nodes, width), F32),
            pltpu.VMEM((edge_width, width), F32), pltpu.VMEM((8, width), F32), pltpu.VMEM((pay_late, width), F32),
            pltpu.VMEM((half, width), BF), pltpu.VMEM((half, width), BF), pltpu.VMEM((edge_width, width), BF),
            pltpu.SemaphoreType.DMA((3,)),
        ],
        compiler_params=params(),
        cost_estimate=cost(13),
        name="message_backward",
    )(where, edges, f_slope, flags, d_sum, d_hiddens[0], *pin(small, *d_hiddens[1:]), w_msg_in, lo, hi, g_gains, g_gain3, g_in, g_out)
    late, early_parts = lax.optimization_barrier((chip_sum(keep, send), early_parts))
    late_parts = to_owners(late)
    dffn_lo = early_parts[:, early_rows:, :].reshape(half, width)
    dffn_hi = swap(dffn_lo, "c")

    tile = 256
    g_ffn_in, g_ffn_out = pl.pallas_call(
        ffn_grads,
        grid=(hidden_width // tile,),
        in_specs=[whole((half, width))] * 4
        + [pl.BlockSpec((width, tile), lambda i: (0, i)), pl.BlockSpec((tile, width), lambda i: (i, 0))],
        out_specs=[pl.BlockSpec((width, tile), lambda i: (0, i)), pl.BlockSpec((tile, width), lambda i: (i, 0))],
        out_shape=[sds(w_ffn_in.shape, F32), sds(w_ffn_out.shape, F32)],
        compiler_params=params(),
        cost_estimate=cost(18),
        name="ffn_grads",
    )(low_lo, low_hi, dffn_lo, dffn_hi, w_ffn_in, w_ffn_out)

    layers = lax.axis_size("z")
    mine = early_parts[:, :early_rows, :].astype(F32).sum(0).astype(BF)
    mine, late_parts, g_ffn_in, g_ffn_out = lax.optimization_barrier((mine, late_parts, g_ffn_in, g_ffn_out))
    spread = pl.pallas_call(
        functools.partial(finish_payload, late_rows),
        out_shape=vmem(small, (1 if layers <= 4 else layers, early_rows + late_rows, width), BF),
        compiler_params=pltpu.CompilerParams(vmem_limit_bytes=(48 if small else 56) << 20),
        name="finish_payload",
    )(mine, *pin(small, late_parts))
    node_grad = pl.pallas_call(
        functools.partial(finish_nodes, late_rows),
        grid=(1,),
        in_specs=[whole(late_parts.shape), whole(n_grad.shape), part((width, width), 1, 0)],
        out_specs=whole(n_grad.shape),
        out_shape=sds(n_grad.shape, F32),
        compiler_params=params(48 if small else 56),
        name="finish_nodes",
    )(*pin(small, late_parts), n_grad, w_msg_in)
    if layers <= 4:
        piece = spread[0]
        got = [lax.ppermute(piece, "z", [((z + k) % layers, z) for z in range(layers)]) for k in range(1, layers)]
        layer = pl.pallas_call(
            place_layers,
            in_specs=[SCALARS] + [pl.BlockSpec(memory_space=pltpu.VMEM)] * layers,
            out_shape=vmem(small, (layers,) + piece.shape, BF),
            compiler_params=pltpu.CompilerParams(vmem_limit_bytes=(48 if small else 56) << 20),
            name="place_layers",
        )(where, *pin(small, piece, *got))
    else:
        layer = lax.all_to_all(spread, "z", 0, 0)
    same = [layer, swap(layer, "x"), swap(layer, "y"), lax.ppermute(layer, ("x", "y"), [(p, 3 - p) for p in range(4)])]
    other = [swap(p, "c") for p in same]
    g_msg_in, g_msg_out, g_edge_t, g_edge_out, *vecs = pl.pallas_call(
        functools.partial(finish_weights, edge_width),
        in_specs=[SCALARS] + [pl.BlockSpec(memory_space=pltpu.VMEM)] * 8,
        out_shape=[
            sds(w_msg_in.shape, F32), sds((width, width), F32), sds(wei_t.shape, F32), sds((edge_width, edge_width), F32),
            sds((1, width), F32), sds((1, width), F32), sds((1, edge_width), F32), sds((1, width), F32),
        ],
        scratch_shapes=[pltpu.VMEM((pay_early, width), BF), pltpu.VMEM((pay_late, width), F32)],
        compiler_params=pltpu.CompilerParams(vmem_limit_bytes=(24 if small else 56) << 20),
        name="finish_weights",
    )(where, *pin(small, *same, *other))
    g_gain1, g_gain2, g_gain3, g_chain = (v.reshape(-1) for v in vecs)
    return (
        node_out, edge_new.transpose(1, 0, 2), node_grad, e_grad.transpose(1, 0, 2), g_msg_in, g_chain, g_msg_out,
        g_gain1, g_ffn_in, g_ffn_out, g_gain2, g_edge_t.T, g_edge_out, g_gain3,
    )


def solution(mesh):
    groups, shares = mesh.shape["res"], mesh.shape["edge"]
    fine = Mesh(mesh.devices.reshape(groups // 2, 2, shares // 2, 2), ("z", "x", "y", "c"))
    rows = P(("z", "x", "y", "c"), None)
    edges = P(("z", "x"), ("y", "c"), None)
    in_specs = (rows, edges, P(("z", "x"), ("y", "c"))) + (P(),) * 12 + (rows, edges)
    out_specs = (rows, edges, rows, edges) + (P(),) * 10
    return jax.shard_map(per_device, mesh=fine, in_specs=in_specs, out_specs=out_specs, check_vma=False)
```

```python
import functools
import math

import jax
import jax.numpy as jnp
from jax import lax
from jax.experimental import pallas as pl
from jax.experimental.pallas import tpu as pltpu
from jax.sharding import Mesh, PartitionSpec as P

EPS = 1e-05
CHIPS = ("z", "x", "y")
BF = jnp.bfloat16
F32 = jnp.float32
ROWS = 80
PIECE = 800
MOVED = 128
SPAN = 1280
RSQRT2 = math.sqrt(0.5)
INV_SQRT_2PI = 1.0 / math.sqrt(2.0 * math.pi)
PLACE, MASK, CROSS = 0, 1, 2


def mm(a, b):
    return jnp.dot(a, b, preferred_element_type=F32)


def mm_nt(a, b):
    return lax.dot_general(a, b, (((1,), (1,)), ((), ())), preferred_element_type=F32)


def mm_tn(a, b):
    return lax.dot_general(a, b, (((0,), (0,)), ((), ())), preferred_element_type=F32)


def gelu_pair(v):
    cdf = 0.5 * (1.0 + lax.erf(v * RSQRT2))
    pdf = INV_SQRT_2PI * jnp.exp(-0.5 * v * v)
    return v * cdf, cdf + v * pdf


def norm_parts(z):
    centre = z - jnp.mean(z, axis=-1, keepdims=True)
    r = lax.rsqrt(jnp.mean(centre * centre, axis=-1, keepdims=True) + EPS)
    return centre * r, r


def norm_back(n, r, gain, cot):
    b = cot * gain
    dz = r * (b - jnp.mean(b, -1, keepdims=True) - n * jnp.mean(b * n, -1, keepdims=True))
    return dz, jnp.sum(cot * n, axis=0, keepdims=True)


def gather_rows(place, halves):
    total = None
    for h, table in enumerate(halves):
        count = table.shape[0]
        block = min(count, SPAN)
        for start in range(0, count, block):
            lane = lax.broadcasted_iota(jnp.int32, (place.shape[0], block), 1) + (h * count + start)
            hot = jnp.where(lane == place, 1.0, 0.0).astype(BF)
            part = mm(hot, table[start : start + block, :])
            total = part if total is None else total + part
    return total


def scatter_rows(place_row, rows, acc):
    nodes = acc.shape[0]
    block = min(nodes, SPAN // 2)

    @pl.loop(0, nodes // block)
    def _(i):
        start = pl.multiple_of(i * block, block)
        row = lax.broadcasted_iota(jnp.int32, (block, place_row.shape[1]), 0) + start
        hot = jnp.where(row == place_row, 1.0, 0.0).astype(BF)
        acc[pl.ds(start, block), :] += mm(hot, rows)


def group_rows(where_ref, lo_ref, hi_ref, rows_own):
    group, core = where_ref[1], where_ref[2]
    start = pl.multiple_of(group * 2 * rows_own, 2 * rows_own)
    same = lo_ref[pl.ds(start, 2 * rows_own), :].astype(F32)
    other = hi_ref[pl.ds(start, 2 * rows_own), :].astype(F32)
    swapped = core == 1
    first = jnp.where(swapped, other, same)
    second = jnp.where(swapped, same, other)
    rows = [first[:rows_own], second[:rows_own], first[rows_own:], second[rows_own:]]
    return jnp.concatenate(rows, axis=0)


def put_shares(where_ref, refs, out):
    rows = refs[0].shape[0]
    shares = len(refs)
    for q, ref in enumerate(refs):
        at = lax.rem(where_ref[0] + shares - q, shares) * rows
        out[pl.ds(pl.multiple_of(at, 8), rows), :] = ref[...].astype(out.dtype)


def take_shares(where_ref, acc, refs):
    rows = refs[0].shape[0]
    shares = len(refs)
    for q, ref in enumerate(refs):
        at = lax.rem(where_ref[0] + q, shares) * rows
        ref[...] = acc[pl.ds(pl.multiple_of(at, 8), rows), :].astype(ref.dtype)


def add_up(refs):
    total = refs[0][...].astype(F32)
    for ref in refs[1:]:
        total += ref[...].astype(F32)
    return total


def message_forward(
    rows_own,
    where_ref, edge_ref, flags_ref, lo_ref, hi_ref, wmi_ref, chain_ref,
    slope_ref, s0, s1, s2, s3,
    table_lo, table_hi, own, acc, pre_s,
):
    step = pl.program_id(0)
    width = wmi_ref.shape[1]
    per, dest_rows, edge_width = edge_ref.shape
    edges = per * dest_rows

    @pl.when(step == 0)
    def _():
        weights = wmi_ref[width : 2 * width, :]
        half = lo_ref.shape[0]
        block = half // 2 if half <= SPAN else SPAN // 2

        @pl.loop(0, half // block)
        def _(i):
            at = pl.ds(pl.multiple_of(i * block, block), block)
            table_lo[at, :] = mm(lo_ref[at, :], weights).astype(BF)
            table_hi[at, :] = mm(hi_ref[at, :], weights).astype(BF)

        group = group_rows(where_ref, lo_ref, hi_ref, rows_own).astype(BF)
        own[...] = mm(group, wmi_ref[:width, :])
        acc[...] = jnp.zeros_like(acc)

    flags = jnp.transpose(flags_ref[0])[:edges, :]
    place = flags[:, PLACE : PLACE + 1].astype(jnp.int32)
    pre_s[...] = gather_rows(place, (table_lo, table_hi)) + mm(
        edge_ref[...].reshape(edges, edge_width), wmi_ref[2 * width :, :]
    )
    for j in range(per):
        for r in range(0, dest_rows, ROWS):
            at = slice(j * dest_rows + r, j * dest_rows + r + ROWS)
            mask = flags[at, MASK : MASK + 1]
            cross = flags[at, CROSS : CROSS + 1]
            pre = pre_s[at, :] + own[r : r + ROWS, :] + cross * chain_ref[...]
            hidden, slope = gelu_pair(pre)
            slope = slope * mask
            slope_ref[j, r : r + ROWS, :] = slope.astype(BF)
            acc[r : r + ROWS, :width] += hidden.astype(BF).astype(F32) * mask
            acc[r : r + ROWS, width:] += slope

    @pl.when(step == pl.num_programs(0) - 1)
    def _():
        take_shares(where_ref, acc, (s0, s1, s2, s3))


def start_copies(sources, targets, sems):
    copies = [pltpu.make_async_copy(s, t, sems.at[i]) for i, (s, t) in enumerate(zip(sources, targets))]
    for copy in copies:
        copy.start()
    return copies


def node_forward(
    norm_scale,
    s0, s1, s2, s3, node_ref, wmo_ref, gain1_ref, wfi_any, wfo_any, gain2_ref, weit_any,
    total_ref, slopes_ref, first_ref, second_ref, low_ref, fslope_ref, fhidden_ref, out_ref, src_ref, eown_ref,
    wfi_ref, wfo_ref, weit_ref, sems,
):
    copies = start_copies((wfi_any, wfo_any, weit_any), (wfi_ref, wfo_ref, weit_ref), sems)
    width = node_ref.shape[1]
    sums = add_up((s0, s1, s2, s3))
    total = sums[:, :width].astype(BF)
    total_ref[...] = total
    slopes_ref[...] = sums[:, width:]
    first_in = node_ref[...].astype(F32) + mm(total, wmo_ref[...]) * (1.0 / norm_scale)
    first_ref[...] = first_in
    norm_one = norm_parts(first_in)[0] * gain1_ref[...]
    low = norm_one.astype(BF)
    for i in range(low_ref.shape[0]):
        low_ref[i] = low
    copies[0].wait()
    hidden, slope = gelu_pair(mm(low, wfi_ref[...]))
    hidden = hidden.astype(BF)
    fslope_ref[...] = slope
    fhidden_ref[...] = hidden
    copies[1].wait()
    second_in = norm_one + mm(hidden, wfo_ref[...])
    second_ref[...] = second_in
    node_out = (norm_parts(second_in)[0] * gain2_ref[...]).astype(BF)
    out_ref[...] = node_out
    copies[2].wait()
    eown_ref[...] = mm_nt(node_out, weit_ref[:, :width]).astype(BF)
    src = mm_nt(node_out, weit_ref[:, width : 2 * width]).astype(BF)
    for i in range(src_ref.shape[0]):
        src_ref[i] = src


def edge_network(
    where_ref, edge_ref, cot_ref, flags_ref, lo_ref, hi_ref, e0, e1, e2, e3, weit_ref, weo_ref, gain_ref,
    out_ref, dsum_ref, slo_ref, shi_ref, o0, o1, o2, o3, gin_ref, gout_ref, ggain_ref,
    own, dpre_s, hidden_s, delta_s, out_s, dsum_s, acc, own_acc,
):
    step = pl.program_id(0)
    per, dest_rows, edge_width = edge_ref.shape
    edges = per * dest_rows
    width = (weit_ref.shape[1] - edge_width) // 2
    weights_t = weit_ref[:, 2 * width :]

    @pl.when(step == 0)
    def _():
        put_shares(where_ref, (e0, e1, e2, e3), own)
        for j in range(1, per):
            own[j * dest_rows : (j + 1) * dest_rows, :] = own[:dest_rows, :]
        acc[...] = jnp.zeros_like(acc)
        own_acc[...] = jnp.zeros_like(own_acc)
        gin_ref[...] = jnp.zeros_like(gin_ref)
        gout_ref[...] = jnp.zeros_like(gout_ref)
        ggain_ref[...] = jnp.zeros_like(ggain_ref)

    flags = jnp.transpose(flags_ref[0])[:edges, :]
    place = flags[:, PLACE : PLACE + 1].astype(jnp.int32)
    edge_all = edge_ref[...].reshape(edges, edge_width)
    cot_all = cot_ref[...].reshape(edges, edge_width)
    pre_all = gather_rows(place, (lo_ref, hi_ref)) + mm_nt(edge_all, weights_t) + own[...]
    gain = gain_ref[...]
    piece = PIECE if edges % PIECE == 0 else edges
    for start in range(0, edges, piece):
        at = slice(start, start + piece)
        mask = flags[at, MASK : MASK + 1]
        hidden, slope = gelu_pair(pre_all[at, :])
        hidden = (hidden * mask).astype(BF)
        hidden_s[at, :] = hidden
        n, r = norm_parts(edge_all[at, :].astype(F32) + mm(hidden, weo_ref[...]))
        out_s[at, :] = (n * gain).astype(BF)
        cot = cot_all[at, :].astype(F32)
        cn = cot * n
        ggain_ref[...] += jnp.sum(cn.reshape(piece // 8, 8, edge_width), axis=0)
        b = cot * gain
        dz = r * (b - jnp.mean(b, -1, keepdims=True) - n * jnp.mean(cn * gain, -1, keepdims=True))
        d_delta = (dz * mask).astype(BF)
        delta_s[at, :] = d_delta
        d_low = (slope * mm_nt(d_delta, weo_ref[...])).astype(BF)
        dpre_s[at, :] = d_low
        dsum_s[at, :] = (dz + mm(d_low, weights_t)).astype(BF)
    out_ref[...] = out_s[...].reshape(out_ref.shape)
    dsum_ref[...] = dsum_s[...].reshape(dsum_ref.shape)
    for j in range(per):
        own_acc[...] += dpre_s[j * dest_rows : (j + 1) * dest_rows, :].astype(F32)
    gout_ref[...] += mm_tn(hidden_s[...], delta_s[...])
    gin_ref[...] += mm_tn(edge_all, dpre_s[...])
    place_row = flags_ref[0, PLACE : PLACE + 1, :edges].astype(jnp.int32)
    scatter_rows(place_row, dpre_s[...], acc)

    @pl.when(step == pl.num_programs(0) - 1)
    def _():
        half = slo_ref.shape[0]
        slo_ref[...] = acc[:half, :].astype(BF)
        shi_ref[...] = acc[half:, :].astype(BF)
        take_shares(where_ref, own_acc, (o0, o1, o2, o3))


def node_backward(
    norm_scale,
    where_ref, parts_ref, o0, o1, o2, o3, node_ref, node_cot_ref, out_ref, first_ref, second_ref, fslope_ref,
    total_ref, slopes_ref, weit_ref, wmi_any, wfi_any, wfo_any, wmo_any, gain1_ref, gain2_ref,
    gin_any, gout_any,
    d_ref, ngrad_ref, ggain_ref, keep_ref, send_ref,
    pay, wfo_ref, wfi_ref, wmo_ref, wmi_ref, gin_ref, gout_ref, sems,
):
    width = out_ref.shape[1]
    own_rows = wmi_any.at[pl.ds(0, width), :]
    sources = (wfo_any, wfi_any, wmo_any, own_rows, gin_any, gout_any)
    copies = start_copies(sources, (wfo_ref, wfi_ref, wmo_ref, wmi_ref, gin_ref, gout_ref), sems)
    from_sources = add_up(tuple(parts_ref.at[i] for i in range(parts_ref.shape[0]))).astype(BF)
    from_own = add_up((o0, o1, o2, o3)).astype(BF)
    d_updated = (
        node_cot_ref[...].astype(F32)
        + mm(from_own, weit_ref[:, :width])
        + mm(from_sources, weit_ref[:, width : 2 * width])
    )
    node_out = out_ref[...]
    n, r = norm_parts(second_ref[...])
    d_second, ggain2 = norm_back(n, r, gain2_ref[...], d_updated)
    dffn = d_second.astype(BF)
    copies[0].wait()
    d_ffn_pre = (fslope_ref[...] * mm_nt(dffn, wfo_ref[...])).astype(BF)
    copies[1].wait()
    d_norm_one = d_second + mm_nt(d_ffn_pre, wfi_ref[...])
    n, r = norm_parts(first_ref[...])
    d_first, ggain1 = norm_back(n, r, gain1_ref[...], d_norm_one)
    d_summed = (d_first * (1.0 / norm_scale)).astype(BF)
    copies[2].wait()
    d_hidden = mm_nt(d_summed, wmo_ref[...])
    d_ref[...] = d_hidden.astype(BF)
    own_sum = (d_hidden * slopes_ref[...]).astype(BF)
    copies[3].wait()
    ngrad_ref[...] = d_first + mm_nt(own_sum, wmi_ref[...])
    ggain_ref[...] = jnp.concatenate([ggain1, ggain2, jnp.zeros((6, width), F32)], axis=0)
    parts = (
        mm_tn(total_ref[...], d_summed), mm_tn(node_ref[...], own_sum), mm_tn(from_own, node_out), mm_tn(from_sources, node_out)
    )
    at = 0
    for part in parts:
        pay[at : at + part.shape[0], :] = part.astype(BF)
        at += part.shape[0]
    copies[4].wait()
    copies[5].wait()
    edge_width = gin_ref.shape[1]
    spare = jnp.zeros((MOVED, width - 2 * edge_width), F32)
    pay[at : at + MOVED, :] = jnp.concatenate([gin_ref[:MOVED, :], gout_ref[:MOVED, :], spare], axis=1).astype(BF)
    at += MOVED
    if at < pay.shape[0]:
        pay[at:, :] = jnp.zeros((pay.shape[0] - at, width), BF)
    early = pay.shape[0] // 2 // keep_ref.shape[0]
    split_halves(where_ref, pay, early, keep_ref, send_ref)
    for i in range(keep_ref.shape[0]):
        keep_ref[i, early:, :] = dffn


def split_halves(where_ref, pay, rows, keep_ref, send_ref):
    half = pay.shape[0] // 2
    at = pl.multiple_of(where_ref[2] * half, 16)
    shape = (keep_ref.shape[0], rows, pay.shape[1])
    keep_ref[:, :rows, :] = pay[pl.ds(at, half), :].reshape(shape)
    send_ref[:, :rows, :] = pay[pl.ds(half - at, half), :].reshape(shape)


def message_backward(
    where_ref, edge_ref, slope_ref, flags_ref, dsum_ref, d0, d1, d2, d3, wmi_any, lo_any, hi_any, gain_ref, gain3_ref, gin_ref,
    gout_ref,
    keep_ref, send_ref, eg_ref,
    own, dpre_s, acc, gin, chain, pay, lo_ref, hi_ref, wme_ref, sems,
):
    step = pl.program_id(0)
    width = wme_ref.shape[1]
    per, dest_rows, edge_width = edge_ref.shape
    edges = per * dest_rows
    copy_w = pltpu.make_async_copy(wmi_any.at[pl.ds(2 * width, edge_width), :], wme_ref, sems.at[2])
    copy_lo = pltpu.make_async_copy(lo_any, lo_ref, sems.at[0])
    copy_hi = pltpu.make_async_copy(hi_any, hi_ref, sems.at[1])

    @pl.when(step == 0)
    def _():
        copy_w.start()
        copy_lo.start()
        copy_hi.start()
        put_shares(where_ref, (d0, d1, d2, d3), own)
        acc[...] = jnp.zeros_like(acc)
        gin[...] = jnp.zeros_like(gin)
        chain[...] = jnp.zeros_like(chain)

    flags = jnp.transpose(flags_ref[0])[:edges, :]
    for j in range(per):
        for r in range(0, dest_rows, ROWS):
            at = slice(j * dest_rows + r, j * dest_rows + r + ROWS)
            d_low = (slope_ref[j, r : r + ROWS, :].astype(F32) * own[r : r + ROWS, :]).astype(BF)
            dpre_s[at, :] = d_low
            crossed = d_low.astype(F32) * flags[at, CROSS : CROSS + 1]
            chain[...] += jnp.sum(crossed.reshape(ROWS // 8, 8, width), axis=0)
    @pl.when(step == 0)
    def _():
        copy_w.wait()

    d_all = dpre_s[...]
    gin[...] += mm_tn(edge_ref[...].reshape(edges, edge_width), d_all)
    back = mm_nt(d_all, wme_ref[...])
    for j in range(per):
        eg_ref[j] = dsum_ref[j].astype(F32) + back[j * dest_rows : (j + 1) * dest_rows, :]
    place_row = flags_ref[0, PLACE : PLACE + 1, :edges].astype(jnp.int32)
    scatter_rows(place_row, d_all, acc)

    @pl.when(step == pl.num_programs(0) - 1)
    def _():
        half = lo_ref.shape[0]
        chips = keep_ref.shape[0]
        rows = half // chips
        late = keep_ref.shape[1] - rows
        copy_lo.wait()
        copy_hi.wait()
        pay[:width, :] = mm_tn(lo_ref[...], acc[:half, :].astype(BF)) + mm_tn(hi_ref[...], acc[half:, :].astype(BF))
        pay[width : width + edge_width, :] = gin[...]
        at = width + edge_width
        pay[at:, :] = jnp.zeros((pay.shape[0] - at, width), F32)
        left = edge_width - MOVED
        pay[at : at + left, : 2 * edge_width] = jnp.concatenate([gin_ref[MOVED:, :], gout_ref[MOVED:, :]], axis=1)
        crossed = jnp.sum(chain[...], axis=0, keepdims=True)
        gain3 = jnp.sum(gain3_ref[...], axis=0, keepdims=True)
        gain3 = jnp.concatenate([gain3, jnp.zeros((1, width - edge_width), F32)], axis=1)
        lanes = width - 2 * edge_width
        for v, vec in enumerate((gain_ref[:1, :], gain_ref[1:2, :], gain3, crossed)):
            for q in range(width // lanes):
                line = at + v * (width // lanes) + q
                pay[line : line + 1, 2 * edge_width :] = vec[:, q * lanes : (q + 1) * lanes]
        half_pay = pay.shape[0] // 2
        core = where_ref[2]
        for chip in range(chips):
            mine = pay[pl.ds(pl.multiple_of(core * half_pay + chip * late, 8), late), :]
            other = pay[pl.ds(pl.multiple_of((1 - core) * half_pay + chip * late, 8), late), :]
            same_rows = acc[chip * rows : (chip + 1) * rows, :]
            other_rows = acc[half + chip * rows : half + (chip + 1) * rows, :]
            keep_ref[chip] = jnp.concatenate([mine, same_rows], axis=0).astype(BF)
            send_ref[chip] = jnp.concatenate([other, other_rows], axis=0).astype(BF)


def finish_nodes(late, parts_ref, ngrad_ref, wmi_ref, out_ref):
    total = add_up(tuple(parts_ref.at[i] for i in range(parts_ref.shape[0])))[late:, :]
    out_ref[...] = ngrad_ref[...] + mm_nt(total.astype(BF), wmi_ref[...])


def finish_payload(late, mine_ref, parts_ref, spread_ref):
    early = mine_ref.shape[0]
    other = add_up(tuple(parts_ref.at[i, :late, :] for i in range(parts_ref.shape[0]))).astype(BF)
    for i in range(spread_ref.shape[0]):
        spread_ref[i, :early, :] = mine_ref[...]
        spread_ref[i, early:, :] = other


def place_layers(where_ref, *refs):
    out_ref = refs[-1]
    for k, ref in enumerate(refs[:-1]):
        out_ref[lax.rem(where_ref[3] + k, out_ref.shape[0])] = ref[...]


def place_chips(where_ref, p0, p1, p2, p3, out_ref):
    for i, piece in enumerate((p0, p1, p2, p3)):
        place = (where_ref[4] ^ (i % 2)) * 2 + (where_ref[5] ^ (i // 2))
        for z in range(piece.shape[0]):
            out_ref[z * 4 + place] = piece[z]


def finish_weights(
    edge_width,
    where_ref, p0, p1, p2, p3, p4, p5, p6, p7,
    gmi_ref, gmo_ref, geit_ref, geo_ref, g1_ref, g2_ref, g3_ref, gchain_ref,
    early, late,
):
    width = gmi_ref.shape[1]
    layers = p0.shape[0]
    first = early.shape[0] // 2 // (4 * layers)
    second = late.shape[0] // 2 // (4 * layers)
    for i, piece in enumerate((p0, p1, p2, p3, p4, p5, p6, p7)):
        half = where_ref[2] ^ (i // 4)
        place = (where_ref[4] ^ (i % 2)) * 2 + (where_ref[5] ^ (i // 2 % 2))
        for z in range(layers):
            chip = (half * layers + z) * 4 + place
            early[pl.ds(pl.multiple_of(chip * first, 16), first), :] = piece[z, :first, :]
            late[pl.ds(pl.multiple_of(chip * second, 8), second), :] = piece[z, first:, :].astype(F32)
    gmo_ref[...] = early[:width, :].astype(F32)
    gmi_ref[:width, :] = early[width : 2 * width, :].astype(F32)
    gmi_ref[width:, :] = late[: width + edge_width, :]
    at = 2 * width
    geit_ref[:, :width] = early[at : at + edge_width, :].astype(F32)
    geit_ref[:, width : 2 * width] = early[at + edge_width : at + 2 * edge_width, :].astype(F32)
    at += 2 * edge_width
    line = width + edge_width
    moved = early[at : at + MOVED, : 2 * edge_width].astype(F32)
    small = jnp.concatenate([moved, late[line : line + edge_width - MOVED, : 2 * edge_width]], axis=0)
    geit_ref[:, 2 * width :] = jnp.transpose(small[:, :edge_width])
    geo_ref[...] = small[:, edge_width:]
    count = width // (width - 2 * edge_width)
    for v, ref in enumerate((g1_ref, g2_ref, g3_ref, gchain_ref)):
        vec = [late[line + v * count + q : line + v * count + q + 1, 2 * edge_width :] for q in range(count)]
        ref[...] = jnp.concatenate(vec, axis=1)[:, : ref.shape[1]]


def ffn_grads(llo_ref, lhi_ref, dlo_ref, dhi_ref, wfi_ref, wfo_ref, gfi_ref, gfo_ref):
    block = min(llo_ref.shape[0], SPAN // 2)
    gfi = gfo = None
    for low_ref, dffn_ref in ((llo_ref, dlo_ref), (lhi_ref, dhi_ref)):
        for start in range(0, low_ref.shape[0], block):
            low = low_ref[start : start + block, :]
            dffn = dffn_ref[start : start + block, :]
            hidden, slope = gelu_pair(mm(low, wfi_ref[...]))
            part = mm_tn(hidden.astype(BF), dffn)
            gfo = part if gfo is None else gfo + part
            d_pre = (slope * mm_nt(dffn, wfo_ref[...])).astype(BF)
            part = mm_tn(low, d_pre)
            gfi = part if gfi is None else gfi + part
    gfo_ref[...] = gfo
    gfi_ref[...] = gfi


def whole(shape):
    return pl.BlockSpec(tuple(shape), lambda *_: (0,) * len(shape))


def part(shape, *index):
    return pl.BlockSpec(tuple(shape), lambda *_: index or (0,) * len(shape))


def per_step(count, shape):
    return pl.BlockSpec((count,) + tuple(shape[1:]), lambda i: (i,) + (0,) * (len(shape) - 1))


SCALARS = pl.BlockSpec(memory_space=pltpu.SMEM)
ANY = pl.BlockSpec(memory_space=pl.ANY)


def params(limit=56):
    return pltpu.CompilerParams(vmem_limit_bytes=limit << 20, dimension_semantics=("arbitrary",))


def pin(small, *arrays):
    return [pltpu.with_memory_space_constraint(x, pltpu.VMEM) if small else x for x in arrays]


def stay(*arrays):
    return [pltpu.with_memory_space_constraint(x, pltpu.HBM) for x in arrays]


def vmem(small, shape, dtype):
    return pltpu.VMEM(tuple(shape), dtype) if small else sds(shape, dtype)


def sds(shape, dtype):
    return jax.ShapeDtypeStruct(tuple(shape), dtype)


def swap(x, axis):
    return lax.ppermute(x, axis, [(0, 1), (1, 0)])


def gather_spread(spread):
    same = lax.all_to_all(spread, CHIPS, 0, 0).reshape(-1, spread.shape[2])
    return same, swap(same, "c")


def scatter_halves(lo, hi):
    got = swap(hi, "c")
    both = (lo.astype(F32) + got.astype(F32)).astype(lo.dtype)
    return lax.all_to_all(both.reshape(lax.axis_size(CHIPS), -1, lo.shape[1]), CHIPS, 0, 0)


def send_shares(pieces):
    shares = len(pieces)
    got = [pieces[0]]
    for q in range(1, shares):
        got.append(lax.ppermute(pieces[q], ("y", "c"), [(s, (s + q) % shares) for s in range(shares)]))
    return got


def chip_sum(keep, send):
    got = jnp.pad(swap(send, "c"), ((0, 0), (0, keep.shape[1] - send.shape[1]), (0, 0)))
    return (keep.astype(F32) + got.astype(F32)).astype(keep.dtype)


def to_owners(both):
    return lax.all_to_all(both, CHIPS, 0, 0)


def cost(micros):
    return pl.CostEstimate(flops=int(micros * 1e9), bytes_accessed=int(micros * 1e6), transcendentals=0)


def per_device(
    node_in, edge_in, neighbors, chain_ids, residue_mask, w_msg_in, chain_vec, w_msg_out, gain_one,
    w_ffn_in, w_ffn_out, gain_two, w_edge_in, w_edge_out, gain_three, node_cot, edge_cot,
):
    dest_rows, width_k, edge_width = edge_in.shape
    rows_own, width = node_in.shape
    hidden_width = w_ffn_in.shape[1]
    nodes = chain_ids.shape[0]
    half = nodes // 2
    small = nodes <= 2 * SPAN
    chips = lax.axis_size(CHIPS)
    per = 5 if width_k % 5 == 0 else 1
    steps = width_k // per
    count = per * dest_rows
    lanes = count + (-count) % 128
    shares = dest_rows // rows_own
    norm_scale = math.sqrt(width_k * shares)
    me_core = lax.axis_index("c")
    share = lax.axis_index("y") * 2 + me_core
    group = lax.axis_index("z") * 2 + lax.axis_index("x")
    z, x, y = (lax.axis_index(axis) for axis in CHIPS)
    where = jnp.stack([share, group, me_core, z, x, y]).astype(jnp.int32)

    edges = edge_in.transpose(1, 0, 2)
    cots = edge_cot.transpose(1, 0, 2)
    layers = lax.axis_size("z")
    if layers <= 4:
        got = [lax.ppermute(node_in, "z", [((z + k) % layers, z) for z in range(layers)]) for k in range(1, layers)]
        first = pl.pallas_call(
            place_layers,
            in_specs=[SCALARS] + [pl.BlockSpec(memory_space=pltpu.VMEM)] * layers,
            out_shape=vmem(small, (layers,) + node_in.shape, BF),
            compiler_params=pltpu.CompilerParams(vmem_limit_bytes=(48 if small else 56) << 20),
            name="place_node_layers",
        )(where, node_in, *pin(small, *got))
        pieces = [swap(first, "x"), swap(first, "y"), lax.ppermute(first, ("x", "y"), [(p, 3 - p) for p in range(4)])]
        lo = pl.pallas_call(
            place_chips,
            in_specs=[SCALARS] + [pl.BlockSpec(memory_space=pltpu.VMEM)] * 4,
            out_shape=vmem(small, (chips,) + node_in.shape, BF),
            compiler_params=pltpu.CompilerParams(vmem_limit_bytes=(48 if small else 56) << 20),
            name="place_node_chips",
        )(where, *pin(small, first, *pieces)).reshape(half, width)
        hi = swap(lo, "c")
    else:
        lo, hi = gather_spread(jnp.broadcast_to(node_in[None], (chips,) + node_in.shape))

    first_row = group * dest_rows
    source = neighbors.T
    dest_chain = lax.dynamic_slice_in_dim(chain_ids, first_row, dest_rows)
    dest_mask = lax.dynamic_slice_in_dim(residue_mask, first_row, dest_rows)
    lower = jnp.sum((chain_ids[None, :] < dest_chain[:, None]).astype(jnp.int32), axis=1)
    upper = jnp.sum((chain_ids[None, :] <= dest_chain[:, None]).astype(jnp.int32), axis=1)
    bits = jnp.sum(residue_mask.reshape(nodes // 16, 16) << jnp.arange(16, dtype=jnp.int32)[None, :], axis=1)
    pick = (source >> 4)[:, :, None] == jnp.arange(nodes // 16, dtype=jnp.int32)[None, None, :]
    word = jnp.sum(jnp.where(pick, bits[None, None, :], 0), axis=2)
    present = (word >> (source & 15)) & 1
    pair_mask = (dest_mask[None, :] * present).astype(F32)
    cross = ((source < lower[None, :]) | (source >= upper[None, :])).astype(F32)
    block = source // rows_own
    place = ((block % 2) ^ me_core) * half + (block // 2) * rows_own + source % rows_own
    table = jnp.stack([place.astype(F32), pair_mask, cross]).reshape(3, steps, count).transpose(1, 0, 2)
    flags = jnp.pad(table, ((0, 0), (0, 5), (0, lanes - count)))

    row = lambda v: v.reshape(1, -1)
    wei_t = w_edge_in.T
    edge_spec = per_step(per, edges.shape)
    flag_spec = per_step(1, flags.shape)
    wide_spec = [whole((rows_own, 2 * width))] * shares
    wide_out = [sds((rows_own, 2 * width), BF)] * shares
    share_spec = [whole((rows_own, width))] * shares

    f_slope, *sums = pl.pallas_call(
        functools.partial(message_forward, rows_own),
        grid=(steps,),
        in_specs=[
            SCALARS, edge_spec, flag_spec, whole((half, width)), whole((half, width)), whole(w_msg_in.shape), whole((1, width)),
        ],
        out_specs=[per_step(per, (width_k, dest_rows, width))] + wide_spec,
        out_shape=[sds((width_k, dest_rows, width), BF)] + wide_out,
        scratch_shapes=[
            pltpu.VMEM((half, width), BF), pltpu.VMEM((half, width), BF), pltpu.VMEM((dest_rows, width), F32),
            pltpu.VMEM((dest_rows, 2 * width), F32), pltpu.VMEM((count, width), F32),
        ],
        compiler_params=params(),
        name="message_forward",
    )(where, edges, flags, *pin(small, lo, hi), w_msg_in, row(chain_vec))
    sums = send_shares(sums)

    total, slopes, first_in, second_in, low, ffn_slope, ffn_hidden, node_out, e_spread, e_own = pl.pallas_call(
        functools.partial(node_forward, norm_scale),
        out_shape=[
            sds((rows_own, width), BF), sds((rows_own, width), F32), sds((rows_own, width), F32), sds((rows_own, width), F32),
            sds((chips, rows_own, width), BF), sds((rows_own, hidden_width), F32), sds((rows_own, hidden_width), BF), sds((rows_own, width), BF),
            sds((chips, rows_own, edge_width), BF), sds((rows_own, edge_width), BF),
        ],
        in_specs=[pl.BlockSpec(memory_space=pltpu.VMEM)] * 7 + [ANY] * 2 + [pl.BlockSpec(memory_space=pltpu.VMEM), ANY],
        scratch_shapes=[
            pltpu.VMEM(w_ffn_in.shape, BF), pltpu.VMEM(w_ffn_out.shape, BF), pltpu.VMEM(wei_t.shape, BF),
            pltpu.SemaphoreType.DMA((3,)),
        ],
        compiler_params=pltpu.CompilerParams(vmem_limit_bytes=56 << 20),
        name="node_forward",
    )(sums[0], *pin(small, *sums[1:]), node_in, w_msg_out, row(gain_one), w_ffn_in, w_ffn_out, row(gain_two), wei_t)

    e_owns = send_shares([e_own] * shares)
    e_lo = lax.all_to_all(e_spread, CHIPS, 0, 0).reshape(-1, edge_width)
    e_lo, *e_owns = lax.optimization_barrier((e_lo, *e_owns))
    e_hi = swap(e_lo, "c")
    e_lo, low = lax.optimization_barrier((e_lo, low))
    low_lo = lax.all_to_all(low, CHIPS, 0, 0).reshape(half, width)

    edge_new, d_sum, e_slo, e_shi, *rest = pl.pallas_call(
        edge_network,
        grid=(steps,),
        in_specs=[SCALARS, edge_spec, edge_spec, flag_spec, whole((half, edge_width)), whole((half, edge_width))]
        + [whole((rows_own, edge_width))] * shares
        + [whole(wei_t.shape), whole(w_edge_out.shape), whole((1, edge_width))],
        out_specs=[edge_spec, edge_spec, whole((half, edge_width)), whole((half, edge_width))]
        + [whole((rows_own, edge_width))] * shares
        + [whole((edge_width, edge_width)), whole((edge_width, edge_width)), whole((8, edge_width))],
        out_shape=[sds(edges.shape, BF), sds(edges.shape, BF), vmem(small, (half, edge_width), BF), sds((half, edge_width), BF)]
        + [sds((rows_own, edge_width), BF)] * shares
        + [sds((edge_width, edge_width), F32), sds((edge_width, edge_width), F32), sds((8, edge_width), F32)],
        scratch_shapes=[
            pltpu.VMEM((count, edge_width), F32), pltpu.VMEM((count, edge_width), BF), pltpu.VMEM((count, edge_width), BF),
            pltpu.VMEM((count, edge_width), BF), pltpu.VMEM((count, edge_width), BF), pltpu.VMEM((count, edge_width), BF), pltpu.VMEM((nodes, edge_width), F32), pltpu.VMEM((dest_rows, edge_width), F32),
        ],
        compiler_params=params(),
        cost_estimate=cost(22),
        name="edge_network",
    )(where, edges, cots, flags, *pin(small, e_lo, e_hi), e_owns[0], *pin(small, *e_owns[1:]), wei_t, w_edge_out, row(gain_three))
    g_in, g_out, g_gain3 = rest[shares:]
    e_slo, e_shi, low_lo, *e_sums = lax.optimization_barrier((e_slo, e_shi, low_lo, *rest[:shares]))
    low_hi = swap(low_lo, "c")
    e_sums = send_shares(e_sums)
    e_parts = scatter_halves(e_slo, e_shi)

    up = lambda rows: rows + (-rows) % (32 * chips)
    pay_early = up(2 * width + 2 * edge_width + MOVED)
    pay_late = width + 2 * edge_width - MOVED
    pay_late += (-pay_late) % (16 * chips)
    early_rows, late_rows = pay_early // (2 * chips), pay_late // (2 * chips)
    kept = (chips, early_rows + rows_own, width)
    operands = (
        *pin(small, e_parts), *stay(e_sums[0]), *pin(small, *e_sums[1:]), node_in, node_cot, node_out, first_in, second_in, ffn_slope, total, slopes,
        wei_t, w_msg_in, w_ffn_in, w_ffn_out, w_msg_out, row(gain_one), row(gain_two), *stay(g_in, g_out),
    )
    specs = [whole(x.shape) for x in operands]
    specs[13:18] = [part((edge_width, 2 * width))] + [ANY] * 4
    specs[-2:] = [ANY] * 2
    outs = [
        sds((rows_own, width), BF), sds((rows_own, width), F32), sds((8, width), F32), vmem(small, kept, BF),
        vmem(small, (chips, early_rows, width), BF),
    ]
    d_hidden, n_grad, g_gains, keep, send = pl.pallas_call(
        functools.partial(node_backward, norm_scale),
        grid=(1,),
        in_specs=[SCALARS] + specs,
        out_specs=[whole(x.shape) for x in outs],
        out_shape=outs,
        scratch_shapes=[
            pltpu.VMEM((pay_early, width), BF), pltpu.VMEM(w_ffn_out.shape, BF), pltpu.VMEM(w_ffn_in.shape, BF),
            pltpu.VMEM(w_msg_out.shape, BF), pltpu.VMEM((width, width), BF),
            pltpu.VMEM(g_in.shape, F32), pltpu.VMEM(g_out.shape, F32), pltpu.SemaphoreType.DMA((6,)),
        ],
        compiler_params=params(48 if small else 56),
        name="node_backward",
    )(where, *operands)
    d_hiddens = send_shares([d_hidden] * shares)
    early, *d_hiddens = lax.optimization_barrier((chip_sum(keep, send), *d_hiddens))
    early_parts = to_owners(early)

    sent = (chips, late_rows + rows_own, width)
    keep, send, e_grad = pl.pallas_call(
        message_backward,
        grid=(steps,),
        in_specs=[SCALARS, edge_spec, per_step(per, (width_k, dest_rows, width)), flag_spec, edge_spec]
        + share_spec + [ANY] * 3 + [whole((8, width))]
        + [whole((8, edge_width)), whole((edge_width, edge_width)), whole((edge_width, edge_width))],
        out_specs=[whole(sent), whole(sent), edge_spec],
        out_shape=[vmem(small, sent, BF), vmem(small, sent, BF), sds(edges.shape, F32)],
        scratch_shapes=[
            pltpu.VMEM((dest_rows, width), F32), pltpu.VMEM((count, width), BF), pltpu.VMEM((nodes, width), F32),
            pltpu.VMEM((edge_width, width), F32), pltpu.VMEM((8, width), F32), pltpu.VMEM((pay_late, width), F32),
            pltpu.VMEM((half, width), BF), pltpu.VMEM((half, width), BF), pltpu.VMEM((edge_width, width), BF),
            pltpu.SemaphoreType.DMA((3,)),
        ],
        compiler_params=params(),
        cost_estimate=cost(13),
        name="message_backward",
    )(where, edges, f_slope, flags, d_sum, d_hiddens[0], *pin(small, *d_hiddens[1:]), w_msg_in, lo, hi, g_gains, g_gain3, g_in, g_out)
    late, early_parts = lax.optimization_barrier((chip_sum(keep, send), early_parts))
    late_parts = to_owners(late)
    dffn_lo = early_parts[:, early_rows:, :].reshape(half, width)
    dffn_hi = swap(dffn_lo, "c")

    tile = 256
    g_ffn_in, g_ffn_out = pl.pallas_call(
        ffn_grads,
        grid=(hidden_width // tile,),
        in_specs=[whole((half, width))] * 4
        + [pl.BlockSpec((width, tile), lambda i: (0, i)), pl.BlockSpec((tile, width), lambda i: (i, 0))],
        out_specs=[pl.BlockSpec((width, tile), lambda i: (0, i)), pl.BlockSpec((tile, width), lambda i: (i, 0))],
        out_shape=[sds(w_ffn_in.shape, F32), sds(w_ffn_out.shape, F32)],
        compiler_params=params(),
        cost_estimate=cost(18),
        name="ffn_grads",
    )(low_lo, low_hi, dffn_lo, dffn_hi, w_ffn_in, w_ffn_out)

    layers = lax.axis_size("z")
    mine = early_parts[:, :early_rows, :].astype(F32).sum(0).astype(BF)
    mine, late_parts, g_ffn_in, g_ffn_out = lax.optimization_barrier((mine, late_parts, g_ffn_in, g_ffn_out))
    spread = pl.pallas_call(
        functools.partial(finish_payload, late_rows),
        out_shape=vmem(small, (1 if layers <= 4 else layers, early_rows + late_rows, width), BF),
        compiler_params=pltpu.CompilerParams(vmem_limit_bytes=(48 if small else 56) << 20),
        name="finish_payload",
    )(mine, *pin(small, late_parts))
    node_grad = pl.pallas_call(
        functools.partial(finish_nodes, late_rows),
        grid=(1,),
        in_specs=[whole(late_parts.shape), whole(n_grad.shape), part((width, width), 1, 0)],
        out_specs=whole(n_grad.shape),
        out_shape=sds(n_grad.shape, F32),
        compiler_params=params(48 if small else 56),
        name="finish_nodes",
    )(*pin(small, late_parts), n_grad, w_msg_in)
    if layers <= 4:
        piece = spread[0]
        got = [lax.ppermute(piece, "z", [((z + k) % layers, z) for z in range(layers)]) for k in range(1, layers)]
        layer = pl.pallas_call(
            place_layers,
            in_specs=[SCALARS] + [pl.BlockSpec(memory_space=pltpu.VMEM)] * layers,
            out_shape=vmem(small, (layers,) + piece.shape, BF),
            compiler_params=pltpu.CompilerParams(vmem_limit_bytes=(48 if small else 56) << 20),
            name="place_layers",
        )(where, *pin(small, piece, *got))
    else:
        layer = lax.all_to_all(spread, "z", 0, 0)
    same = [layer, swap(layer, "x"), swap(layer, "y"), lax.ppermute(layer, ("x", "y"), [(p, 3 - p) for p in range(4)])]
    other = [swap(p, "c") for p in same]
    g_msg_in, g_msg_out, g_edge_t, g_edge_out, *vecs = pl.pallas_call(
        functools.partial(finish_weights, edge_width),
        in_specs=[SCALARS] + [pl.BlockSpec(memory_space=pltpu.VMEM)] * 8,
        out_shape=[
            sds(w_msg_in.shape, F32), sds((width, width), F32), sds(wei_t.shape, F32), sds((edge_width, edge_width), F32),
            sds((1, width), F32), sds((1, width), F32), sds((1, edge_width), F32), sds((1, width), F32),
        ],
        scratch_shapes=[pltpu.VMEM((pay_early, width), BF), pltpu.VMEM((pay_late, width), F32)],
        compiler_params=pltpu.CompilerParams(vmem_limit_bytes=(24 if small else 56) << 20),
        name="finish_weights",
    )(where, *pin(small, *same, *other))
    g_gain1, g_gain2, g_gain3, g_chain = (v.reshape(-1) for v in vecs)
    return (
        node_out, edge_new.transpose(1, 0, 2), node_grad, e_grad.transpose(1, 0, 2), g_msg_in, g_chain, g_msg_out,
        g_gain1, g_ffn_in, g_ffn_out, g_gain2, g_edge_t.T, g_edge_out, g_gain3,
    )


def solution(mesh):
    groups, shares = mesh.shape["res"], mesh.shape["edge"]
    fine = Mesh(mesh.devices.reshape(groups // 2, 2, shares // 2, 2), ("z", "x", "y", "c"))
    rows = P(("z", "x", "y", "c"), None)
    edges = P(("z", "x"), ("y", "c"), None)
    in_specs = (rows, edges, P(("z", "x"), ("y", "c"))) + (P(),) * 12 + (rows, edges)
    out_specs = (rows, edges, rows, edges) + (P(),) * 10
    return jax.shard_map(per_device, mesh=fine, in_specs=in_specs, out_specs=out_specs, check_vma=False)
```
